256 devices in a mesh: seq: 32 (over z_hi, y, core), head: 8 (over x, z_lo).
Axes of the slice: x: 4, y: 4, z: 8 (z_hi: 4, z_lo: 2; z = z_hi * 2 + z_lo), core: 2. Of those that a mesh axis runs over, the one named last changes fastest.
Arguments:
- queries: bfloat16 [32768, 2048], P('seq', 'head'), may hold values from -8 to 8
- key_states: bfloat16 [32768, 2048], P('seq', 'head'), may hold values from -8 to 8
- value_states: bfloat16 [32768, 2048], P('seq', 'head'), may hold values from -6 to 6
- out_weight: bfloat16 [2048, 2048], P('head'), may hold values from -0.125 to 0.125
- cotangent: bfloat16 [32768, 2048], P('seq', 'head'), may hold values from -6 to 6
Outputs:
- attended: bfloat16 [32768, 2048], P('seq', 'head')
- grad_queries: bfloat16 [32768, 2048], P('seq', 'head')
- grad_keys: bfloat16 [32768, 2048], P('seq', 'head')
- grad_values: bfloat16 [32768, 2048], P('seq', 'head')
- grad_weight: bfloat16 [2048, 2048], P('head')
The draws below stay inside these ranges and needn't reach their ends.
All inputs are finite; a program needn't handle non-finite values.
Results may differ from the reference program's by a relative error of at most 0.02.
Values may be sent and summed in bfloat16 or wider, within the bound.
A program may use at most 128 MiB of HBM per device.

```python
import jax
import jax.numpy as jnp
from jax import lax

HEADS = 16
HEAD_DIM = 128
BLOCK = 256
POOLED = 128
D = 2048
HEADS_DEV = 2
SEQ = 32768
N_HEAD = 8


def base_draw(key):
    return jnp.clip(jax.random.normal(key, (SEQ, D), jnp.float32), -6.0, 6.0)


def draw_queries(key, part):
    values = base_draw(jax.random.fold_in(key, 1))
    return values.astype(jnp.bfloat16)


def draw_key_states(key, part):
    values = base_draw(jax.random.fold_in(key, 2))
    return values.astype(jnp.bfloat16)


def level_of(stream_key, dims, split, smallest, largest):
    level, own = 1.0, jax.random.fold_in(stream_key, 6)
    for dim, blocks in split:
        heights = jnp.exp(jax.random.uniform(jax.random.fold_in(own, dim), (blocks,), jnp.float32, smallest / len(split), largest / len(split)))
        level = level * jnp.repeat(heights, dims[dim] // blocks).reshape([-1 if axis == dim else 1 for axis in range(len(dims))])
    return level


def bell_draw(rng, dims, deviation, most, shards=(), kind=jnp.bfloat16):
    result = jax.random.normal(rng, dims, jnp.float32) * deviation
    if len(shards) > 0:
        result = level_of(rng, dims, shards, -0.22, 0.18) * result
    return jnp.clip(result, min=-most, max=most).astype(kind)


def setup_inputs(seed: int = 0) -> dict:
    streams_of = jax.random.split(jax.random.key(seed), 6)
    queries = draw_queries(jax.random.fold_in(streams_of[5], 71), 0)
    key_states = draw_key_states(jax.random.fold_in(streams_of[5], 71), 0)
    value_states = bell_draw(streams_of[2], (SEQ, D), 1.0, 6.0, ((0, 32), (1, 8)))
    out_weight = bell_draw(streams_of[3], (D, D), D ** -0.5, 0.125, ((0, 8),))
    cotangent = bell_draw(streams_of[4], (SEQ, D), 1.0, 6.0, ((0, 32), (1, 8)))
    return {"queries": queries, "key_states": key_states, "value_states": value_states, "out_weight": out_weight, "cotangent": cotangent}


def pair_mean(rows):
    wide = rows.astype(jnp.float32).reshape(rows.shape[0] // 2, 2, rows.shape[1])
    return (0.5 * (wide[:, 0] + wide[:, 1])).astype(jnp.bfloat16)


def widen(rows):
    return jnp.repeat(rows, 2, axis=0) * 0.5


def rounded(values):
    return lax.optimization_barrier(values.astype(jnp.bfloat16)).astype(jnp.float32)


def sibling_rows(coarse, level):
    width = coarse.shape[1]
    halves = coarse.reshape(-1, 2, POOLED, width)[:, ::-1].reshape(-1, POOLED, width)
    return jnp.repeat(halves, 2 ** (level - 1), axis=0)


def sibling_grads(part, level):
    width = part.shape[2]
    span = 2 ** (level - 1)
    summed = jnp.sum(part.reshape(-1, span, POOLED, width), axis=1)
    return summed.reshape(-1, 2, POOLED, width)[:, ::-1].reshape(-1, width)


def head_pass(operands):
    query, key_rows, value_rows, grad_mixed = operands
    blocks = SEQ // BLOCK
    levels = blocks.bit_length() - 1
    logit_scale = HEAD_DIM ** -0.5
    key_parts = [key_rows.reshape(blocks, BLOCK, HEAD_DIM)]
    value_parts = [value_rows.reshape(blocks, BLOCK, HEAD_DIM)]
    coarse_keys = key_rows
    coarse_values = value_rows
    for level in range(1, levels + 1):
        coarse_keys = pair_mean(coarse_keys)
        coarse_values = pair_mean(coarse_values)
        key_parts.append(sibling_rows(coarse_keys, level))
        value_parts.append(sibling_rows(coarse_values, level))
    gathered_key_rows = jnp.concatenate(key_parts, axis=1).astype(jnp.float32)
    gathered_value_rows = jnp.concatenate(value_parts, axis=1).astype(jnp.float32)
    blocked_queries = query.reshape(blocks, BLOCK, HEAD_DIM).astype(jnp.float32)
    attention_logits = logit_scale * jnp.einsum("ohw,oiw->ohi", blocked_queries, gathered_key_rows)
    top = jnp.max(attention_logits, axis=-1, keepdims=True)
    expo = jnp.exp(attention_logits - top)
    probs = expo / jnp.sum(expo, axis=-1, keepdims=True)
    attention_probabilities = rounded(probs)
    blended_output = jnp.einsum("xlv,xvd->xld", attention_probabilities, gathered_value_rows).astype(jnp.bfloat16)
    block_gradient_rows = grad_mixed.reshape(blocks, BLOCK, HEAD_DIM).astype(jnp.float32)
    probability_gradient = jnp.einsum("ohw,oiw->ohi", block_gradient_rows, gathered_value_rows)
    inner = jnp.sum(probs * probability_gradient, axis=-1, keepdims=True)
    logit_gradient = rounded(probs * (probability_gradient - inner))
    query_gradient = (logit_scale * jnp.einsum("xlv,xvd->xld", logit_gradient, gathered_key_rows)).astype(jnp.bfloat16)
    gathered_key_gradient = logit_scale * jnp.einsum("ozj,ozc->ojc", logit_gradient, blocked_queries)
    gathered_value_gradient = jnp.einsum("ozj,ozc->ojc", attention_probabilities, block_gradient_rows)
    accum_keys = None
    accum_values = None
    for level in range(levels, 0, -1):
        offset = BLOCK + (level - 1) * POOLED
        back_keys = sibling_grads(gathered_key_gradient[:, offset:offset + POOLED], level)
        back_values = sibling_grads(gathered_value_gradient[:, offset:offset + POOLED], level)
        if accum_keys is None:
            accum_keys = back_keys
            accum_values = back_values
        else:
            accum_keys = back_keys + widen(accum_keys)
            accum_values = back_values + widen(accum_values)
    grad_key = gathered_key_gradient[:, :BLOCK].reshape(SEQ, HEAD_DIM) + widen(accum_keys)
    grad_value = gathered_value_gradient[:, :BLOCK].reshape(SEQ, HEAD_DIM) + widen(accum_values)
    return (blended_output.reshape(SEQ, HEAD_DIM), query_gradient.reshape(SEQ, HEAD_DIM),
            grad_key.astype(jnp.bfloat16), grad_value.astype(jnp.bfloat16))


def by_head(values):
    return values.reshape(SEQ, HEADS, HEAD_DIM).transpose(1, 0, 2)


def to_rows(values):
    return values.transpose(1, 0, 2).reshape(SEQ, HEADS * HEAD_DIM)


def reference(queries, key_states, value_states, out_weight, cotangent):
    grad_mixed = jnp.dot(cotangent, out_weight.T, preferred_element_type=jnp.float32).astype(jnp.bfloat16)
    blended_output, query_gradient, grad_key, grad_value = lax.map(
        head_pass, (by_head(queries), by_head(key_states), by_head(value_states), by_head(grad_mixed)))
    blended_output = to_rows(blended_output)
    width = HEADS_DEV * HEAD_DIM
    total = jnp.zeros((SEQ, D), jnp.float32)
    for index in range(N_HEAD):
        partial_out = jnp.dot(blended_output[:, index * width:(index + 1) * width],
                              out_weight[index * width:(index + 1) * width],
                              preferred_element_type=jnp.float32)
        total = total + rounded(partial_out)
    attended = total.astype(jnp.bfloat16)
    grad_weight = jnp.dot(blended_output.T, cotangent, preferred_element_type=jnp.float32).astype(jnp.bfloat16)
    return attended, to_rows(query_gradient), to_rows(grad_key), to_rows(grad_value), grad_weight
```

```python
import math

import jax
import jax.numpy as jnp
from jax import lax
from jax.experimental import pallas as pl
from jax.experimental.pallas import tpu as pltpu
from jax.sharding import PartitionSpec as P

BF = jnp.bfloat16
F32 = jnp.float32
HD = 128
BLOCK = 256
NB = 4
ROWS = NB * BLOCK
W2 = 256
LOCAL = 512
FAR = 640
SCALE = HD**-0.5
SCALE2 = SCALE * math.log2(math.e)

AG = 0
RELAY = 8
WZ = 12
WC = 16
KV = 20
MX = 27
GM = 31
RS1 = 35
RS2 = 39
GW = 47
GK = 62
N_SEM = 69


def dot_nt(a, b):
    return lax.dot_general(a, b, (((1,), (1,)), ((), ())), preferred_element_type=F32)


def dot_nn(a, b):
    return lax.dot_general(a, b, (((1,), (0,)), ((), ())), preferred_element_type=F32)


def dot_tn(a, b):
    return lax.dot_general(a, b, (((0,), (0,)), ((), ())), preferred_element_type=F32)


def pool_matrix(rows):
    r = lax.broadcasted_iota(jnp.int32, (rows // 2, rows), 0)
    c = lax.broadcasted_iota(jnp.int32, (rows // 2, rows), 1)
    return jnp.where((c == 2 * r) | (c == 2 * r + 1), 0.5, 0.0).astype(BF)


def pool(x):
    return dot_nn(pool_matrix(x.shape[0]), x).astype(BF)


def spread(x, factor):
    rows = x.shape[0]
    r = lax.broadcasted_iota(jnp.int32, (rows * factor, rows), 0)
    c = lax.broadcasted_iota(jnp.int32, (rows * factor, rows), 1)
    d = r - c * factor
    e = jnp.where((d >= 0) & (d < factor), 1.0 / factor, 0.0).astype(BF)
    high = x.astype(BF)
    low = (x - high.astype(F32)).astype(BF)
    return dot_nn(e, high) + dot_nn(e, low)


def kernel(q_hbm, k_hbm, v_hbm, w_hbm, c_hbm,
           att_hbm, gq_hbm, gk_hbm, gv_hbm, gw_hbm,
           q, kl, kf, c3, c4, c5, c6, c7, cg, wt, mx, probs,
           gmo, gms, gmr, rs_a, rs_ar, rs_b, rs_br, part0, part_r, part_l,
           gws, gwr, gwo, s1b, yr, s2b, zr, s3b, s4, gwf,
           dkl, dkf, tok, gz_s, gz_r, gy_s, gy_r, gc_s, gc_r,
           oatt, ogq, ogk,
           ssem, rsem, lsem):
    seq = lax.axis_index("seq")
    head = lax.axis_index("head")
    core = lax.rem(seq, 2)
    y = lax.rem(seq // 2, 4)
    zh = seq // 8
    x = head // 2
    z = lax.rem(head, 2)
    oc = 1 - core
    oz = 1 - z

    def xor4(a, k):
        if k == 1:
            return a + 1 - 2 * lax.rem(a, 2)
        if k == 2:
            return lax.rem(a + 2, 4)
        return 3 - a

    xr = lax.rem(x + 1, 4)
    xl = lax.rem(x + 3, 4)
    xf = lax.rem(x + 2, 4)
    right = (seq, xr * 2 + z)
    left = (seq, xl * 2 + z)
    pair = (seq, x * 2 + oz)
    sib = (zh * 8 + y * 2 + oc, head)
    yp = [(zh * 8 + xor4(y, k) * 2 + core, head) for k in (1, 2, 3)]
    zp = [(xor4(zh, k) * 8 + y * 2 + core, head) for k in (1, 2, 3)]
    yk = [xor4(y, k) for k in (1, 2, 3)]
    zk = [xor4(zh, k) for k in (1, 2, 3)]

    def rows_of(b):
        return pl.ds(pl.multiple_of(b * BLOCK, BLOCK), BLOCK)

    def rcopy(src, dst, slot, peer):
        return pltpu.make_async_remote_copy(
            src_ref=src, dst_ref=dst, send_sem=ssem.at[slot], recv_sem=rsem.at[slot],
            device_id=peer, device_id_type=pl.DeviceIdType.MESH)

    loads = []
    for b in range(NB):
        loads.append(pltpu.make_async_copy(k_hbm.at[pl.ds(b * BLOCK, BLOCK)], kl.at[0, b, pl.ds(0, BLOCK)], lsem.at[2 * b]))
        loads.append(pltpu.make_async_copy(v_hbm.at[pl.ds(b * BLOCK, BLOCK)], kl.at[1, b, pl.ds(0, BLOCK)], lsem.at[2 * b + 1]))
    for copy in loads:
        copy.start()
    load_q = pltpu.make_async_copy(q_hbm, q, lsem.at[8])
    load_q.start()
    load_c = pltpu.make_async_copy(c_hbm, cg.at[x], lsem.at[9])
    load_c.start()
    zrow = pl.multiple_of(z * W2, W2)
    ozrow = pl.multiple_of(oz * W2, W2)
    load_w = [
        pltpu.make_async_copy(
            w_hbm.at[:, pl.ds(pl.multiple_of(512 * s + W2 * z, W2), W2)], wt.at[s, pl.ds(zrow, W2)], lsem.at[10 + s])
        for s in range(4)]
    for copy in load_w:
        copy.start()

    barrier = pltpu.get_barrier_semaphore()
    peers = [right, left, pair, sib] + yp + zp
    for peer in peers:
        pl.semaphore_signal(barrier, inc=1, device_id=peer, device_id_type=pl.DeviceIdType.MESH)
    pl.semaphore_wait(barrier, len(peers))

    ag_r = []
    ag_l = []
    for b in (0, 1, 2, 3):
        rb = pl.ds(b * BLOCK, BLOCK)
        ag_r.append(rcopy(c_hbm.at[rb], cg.at[x, rb], AG + b, right))
        ag_l.append(rcopy(c_hbm.at[rb], cg.at[x, rb], AG + 4 + b, left))
    for b in range(4):
        ag_r[b].start()
        ag_l[3 - b].start()
    crow = pl.multiple_of(core * 128, 128)
    wz = [
        rcopy(w_hbm.at[pl.ds(crow, 128), pl.ds(pl.multiple_of(512 * s + W2 * oz, W2), W2)],
              wt.at[s, pl.ds(pl.multiple_of(zrow + crow, 128), 128)], WZ + s, pair)
        for s in range(4)]
    for copy in wz:
        copy.start()

    for copy in loads:
        copy.wait()
    for t in range(2):
        c2 = []
        for b in range(NB):
            p1 = pool(kl[t, b, 0:BLOCK, :])
            kl[t, b ^ 1, 256:384, :] = p1
            c2.append(pool(p1))
        for p in range(2):
            both = jnp.concatenate([c2[2 * p], c2[2 * p + 1]], axis=0)
            kl[t, 2 - 2 * p, 384:512, :] = both
            kl[t, 3 - 2 * p, 384:512, :] = both
            c3[t, 64 * p:64 * p + 64, :] = pool(both)
    kv_core = rcopy(c3, kf.at[:, pl.ds(0, 128)], KV, sib)
    kv_core.start()
    kv_core.wait_recv()
    for t in range(2):
        mine = pool(c3[t])
        other = pool(kf[t, 0:128, :])
        both = jnp.concatenate([mine, other], axis=0)
        c4[t] = both
        c5[t] = pool(both)
    kv_y = [rcopy(c4, kf.at[:, pl.ds(128, 128)], KV + 1, yp[0]),
            rcopy(c5, kf.at[:, pl.ds(256, 64)], KV + 2, yp[1]),
            rcopy(c5, kf.at[:, pl.ds(320, 64)], KV + 3, yp[2])]
    for copy in kv_y:
        copy.start()
    for copy in kv_y:
        copy.wait_recv()
    for t in range(2):
        c6[t, 0:32, :] = pool(c5[t])
        c6[t, 32:64, :] = pool(pool(kf[t, 128:256, :]))
        c6[t, 64:96, :] = pool(kf[t, 256:320, :])
        c6[t, 96:128, :] = pool(kf[t, 320:384, :])
        c7[t] = pool(c6[t])
    kv_z = [rcopy(c6, kf.at[:, pl.ds(384, 128)], KV + 4, zp[0]),
            rcopy(c7, kf.at[:, pl.ds(512, 64)], KV + 5, zp[1]),
            rcopy(c7, kf.at[:, pl.ds(576, 64)], KV + 6, zp[2])]
    for copy in kv_z:
        copy.start()

    relay_r = []
    relay_l = []
    for i in range(2):
        rb = pl.ds(i * BLOCK, BLOCK)
        rc = pl.ds((i + 2) * BLOCK, BLOCK)
        relay_r.append(rcopy(cg.at[xl, rb], cg.at[xl, rb], RELAY + i, right))
        relay_l.append(rcopy(cg.at[xr, rc], cg.at[xr, rc], RELAY + 2 + i, left))
    for i in range(2):
        ag_r[i].wait_recv()
        relay_r[i].start()
        ag_l[3 - i].wait_recv()
        relay_l[1 - i].start()
    wc = []
    for s in range(4):
        piece = wt.at[s, pl.ds(pl.multiple_of(ozrow + crow, 128), 128)]
        wc.append(rcopy(piece, piece, WC + s, sib))
    for s in range(4):
        wz[s].wait_recv()
        wc[s].start()

    load_q.wait()
    for copy in kv_z:
        copy.wait_recv()

    def mx_copy(b):
        rb = rows_of(b)
        return rcopy(mx.at[z, rb], mx.at[z, rb], MX + b, pair)

    @pl.loop(0, NB)
    def _(b):
        rb = rows_of(b)
        for h in range(2):
            hs = slice(h * HD, h * HD + HD)
            qh = q[rb, hs]
            s_l = dot_nt(qh, kl[0, b, :, hs])
            s_f = dot_nt(qh, kf[0, :, hs])
            top = jnp.maximum(jnp.max(s_l, axis=1, keepdims=True), jnp.max(s_f, axis=1, keepdims=True))
            e_l = jnp.exp2((s_l - top) * SCALE2)
            e_f = jnp.exp2((s_f - top) * SCALE2)
            total = jnp.sum(e_l, axis=1, keepdims=True) + jnp.sum(e_f, axis=1, keepdims=True)
            inv = 1.0 / total
            p_l = e_l * inv
            p_f = e_f * inv
            probs[b, h, :, 0:LOCAL] = p_l
            probs[b, h, :, LOCAL:] = p_f
            out = dot_nn(p_l.astype(BF), kl[1, b, :, hs]) + dot_nn(p_f.astype(BF), kf[1, :, hs])
            mx[z, rb, hs] = out.astype(BF)
        mx_copy(b).start()

    load_c.wait()
    for copy in load_w:
        copy.wait()
    for copy in wc:
        copy.wait_recv()
    for i in range(2):
        relay_r[i].wait_recv()
        relay_l[i].wait_recv()
        ag_r[2 + i].wait_recv()
        ag_l[i].wait_recv()

    def gm_copy(b):
        return rcopy(gms.at[b], gmr.at[b], GM + b, pair)

    @pl.loop(0, NB)
    def _(b):
        rb = rows_of(b)
        give = jnp.zeros((BLOCK, W2), F32)
        for s in range(4):
            give += dot_nt(cg[s, rb, :], wt[s, pl.ds(ozrow, W2), :])
        gms[b] = give.astype(BF)
        gm_copy(b).start()
        keep = jnp.zeros((BLOCK, W2), F32)
        for s in range(4):
            keep += dot_nt(cg[s, rb, :], wt[s, pl.ds(zrow, W2), :])
        gmo[b] = keep

    for b in range(NB):
        mx_copy(b).wait_recv()

    def partial(s, b):
        rb = rows_of(b)
        return dot_nn(mx[0, rb, :], wt[s, 0:W2, :]) + dot_nn(mx[1, rb, :], wt[s, W2:2 * W2, :])

    rs1_r = [rcopy(rs_a.at[i], rs_ar.at[i], RS1 + i, right) for i in range(2)]
    rs1_l = [rcopy(rs_a.at[2 + i], rs_ar.at[2 + i], RS1 + 2 + i, left) for i in range(2)]

    @pl.loop(0, NB)
    def _(b):
        rs_a[b] = partial(xf, b).astype(BF)

    for i in range(2):
        rs1_r[i].start()
        rs1_l[i].start()
    rs2_r = [rcopy(rs_b.at[0, b], rs_br.at[0, b], RS2 + b, right) for b in range(NB)]
    rs2_l = [rcopy(rs_b.at[1, b], rs_br.at[1, b], RS2 + 4 + b, left) for b in range(NB)]

    @pl.loop(0, 2)
    def _(i):
        rs_b[0, 2 + i] = partial(xr, 2 + i).astype(BF)
        rs_b[1, i] = partial(xl, i).astype(BF)
        part_r[i] = partial(xr, i)
        part_l[i] = partial(xl, 2 + i)

    for i in range(2):
        rs2_r[2 + i].start()
        rs2_l[i].start()

    @pl.loop(0, NB)
    def _(b):
        part0[b] = partial(x, b)

    @pl.loop(0, 2)
    def _(j):
        for r in range(2):
            gws[j, r] = dot_tn(mx[r], cg[2 * oc + j]).astype(BF)

    gw_core = rcopy(gws, gwr, GW, sib)
    gw_core.start()

    @pl.loop(0, 2)
    def _(j):
        for r in range(2):
            gwo[j, r] = dot_tn(mx[r], cg[2 * core + j])

    for b in range(NB):
        gm_copy(b).wait_recv()
    dkf[...] = jnp.zeros_like(dkf)
    gw_y = [rcopy(s1b.at[:, :, pl.ds(pl.multiple_of(64 * yk[k], 64), 64)], yr.at[k], GW + 1 + k, yp[k]) for k in range(3)]
    gw_z = [rcopy(s2b.at[:, :, pl.ds(pl.multiple_of(16 * zk[k], 16), 16)], zr.at[k], GW + 4 + k, zp[k]) for k in range(3)]
    gw_p = rcopy(s3b.at[:, oz], s4, GW + 7, pair)
    row_y = pl.multiple_of(64 * y, 64)
    row_z = pl.multiple_of(64 * y + 16 * zh, 16)
    cols = pl.ds(pl.multiple_of(1024 * core, 1024), 1024)
    piece_z = gwf.at[pl.ds(row_z, 16), cols]
    piece_y = gwf.at[pl.ds(row_y, 64), cols]
    piece_c = gwf.at[:, cols]
    gw_zg = [rcopy(piece_z, piece_z, GW + 8 + k, zp[k]) for k in range(3)]
    gw_yg = [rcopy(piece_y, piece_y, GW + 11 + k, yp[k]) for k in range(3)]
    gw_cg = rcopy(piece_c, piece_c, GW + 14, sib)

    @pl.loop(0, NB)
    def _(b):
        rb = rows_of(b)
        for h in range(2):
            hs = slice(h * HD, h * HD + HD)
            do = (gmo[b, :, hs] + gmr[b, :, hs].astype(F32)).astype(BF)
            qh = q[rb, hs]
            p_l = probs[b, h, :, 0:LOCAL]
            p_f = probs[b, h, :, LOCAL:]
            dp_l = dot_nt(do, kl[1, b, :, hs])
            dp_f = dot_nt(do, kf[1, :, hs])
            inner = jnp.sum(p_l * dp_l, axis=1, keepdims=True) + jnp.sum(p_f * dp_f, axis=1, keepdims=True)
            ds_l = (p_l * (dp_l - inner)).astype(BF)
            ds_f = (p_f * (dp_f - inner)).astype(BF)
            dq = dot_nn(ds_l, kl[0, b, :, hs]) + dot_nn(ds_f, kf[0, :, hs])
            ogq[rb, hs] = (dq * SCALE).astype(BF)
            dkf[0, :, hs] += dot_tn(ds_f, qh) * SCALE
            dkf[1, :, hs] += dot_tn(p_f.astype(BF), do)
            dkl[0, b, :, hs] = dot_tn(ds_l, qh) * SCALE
            dkl[1, b, :, hs] = dot_tn(p_l.astype(BF), do)

        @pl.when(b == 0)
        def _():
            gw_core.wait_recv()
            gwo[...] += gwr[...].astype(F32)
            s1b[...] = gwo[...].astype(BF)
            for copy in gw_y:
                copy.start()

        @pl.when(b == 1)
        def _():
            for i in range(2):
                rs1_r[i].wait_recv()
                rs1_l[i].wait_recv()
                rs_b[0, i] = (part_r[i] + rs_ar[i].astype(F32)).astype(BF)
                rs_b[1, 2 + i] = (part_l[i] + rs_ar[2 + i].astype(F32)).astype(BF)
                rs2_r[i].start()
                rs2_l[2 + i].start()

        @pl.when(b == 2)
        def _():
            for copy in gw_y:
                copy.wait_recv()
            own = gwo[:, :, pl.ds(row_y, 64), :]
            for k in range(3):
                own += yr[k].astype(F32)
            gwo[:, :, pl.ds(row_y, 64), :] = own
            s2b[...] = own.astype(BF)
            for copy in gw_z:
                copy.start()

    gz_s[:, 0:256, :] = dkf[:, 384:640, :].astype(BF)
    gk_z = [rcopy(gz_s.at[:, pl.ds(0, 128)], gz_r.at[:, pl.ds(0, 128)], GK, zp[0]),
            rcopy(gz_s.at[:, pl.ds(128, 64)], gz_r.at[:, pl.ds(128, 64)], GK + 1, zp[1]),
            rcopy(gz_s.at[:, pl.ds(192, 64)], gz_r.at[:, pl.ds(192, 64)], GK + 2, zp[2])]
    for copy in gk_z:
        copy.start()
    out_q = pltpu.make_async_copy(ogq, gq_hbm, lsem.at[14])
    out_q.start()

    for copy in gw_z:
        copy.wait_recv()
    fin = gwo[:, :, pl.ds(row_z, 16), :]
    for k in range(3):
        fin += zr[k].astype(F32)
    s3b[...] = fin.astype(BF)
    gw_p.start()

    for t in range(2):
        for p in range(2):
            g2 = dkl[t, 2 - 2 * p, 384:512, :] + dkl[t, 3 - 2 * p, 384:512, :]
            for i in range(2):
                b = 2 * p + i
                g1 = dkl[t, b ^ 1, 256:384, :] + spread(g2[64 * i:64 * i + 64, :], 2)
                tok[t, b] = dkl[t, b, 0:BLOCK, :] + spread(g1, 2)

    for copy in gk_z:
        copy.wait_recv()
    kept = []
    for t in range(2):
        c6g = gz_r[t, 0:128, :].astype(F32) + spread(
            gz_r[t, 128:192, :].astype(F32) + gz_r[t, 192:256, :].astype(F32), 2)
        gy_s[t, 0:128, :] = (dkf[t, 128:256, :] + spread(c6g[32:64, :], 4)).astype(BF)
        gy_s[t, 128:192, :] = (dkf[t, 256:320, :] + spread(c6g[64:96, :], 2)).astype(BF)
        gy_s[t, 192:256, :] = (dkf[t, 320:384, :] + spread(c6g[96:128, :], 2)).astype(BF)
        kept.append(spread(c6g[0:32, :], 4))
    gk_y = [rcopy(gy_s.at[:, pl.ds(0, 128)], gy_r.at[:, pl.ds(0, 128)], GK + 3, yp[0]),
            rcopy(gy_s.at[:, pl.ds(128, 64)], gy_r.at[:, pl.ds(128, 64)], GK + 4, yp[1]),
            rcopy(gy_s.at[:, pl.ds(192, 64)], gy_r.at[:, pl.ds(192, 64)], GK + 5, yp[2])]
    for copy in gk_y:
        copy.start()

    gw_p.wait_recv()
    for j in range(2):
        base = 1024 * core + 512 * j
        gwf[pl.ds(row_z, 16), pl.ds(pl.multiple_of(base + W2 * z, W2), W2)] = s3b[j, z]
        gwf[pl.ds(row_z, 16), pl.ds(pl.multiple_of(base + W2 * oz, W2), W2)] = s4[j]
    for copy in gw_zg:
        copy.start()

    for b in range(NB):
        rs2_r[b].wait_recv()
        rs2_l[b].wait_recv()
        oatt[pl.ds(b * BLOCK, BLOCK), :] = (
            part0[b] + rs_br[0, b].astype(F32) + rs_br[1, b].astype(F32)).astype(BF)
    out_att = pltpu.make_async_copy(oatt, att_hbm, lsem.at[15])
    out_att.start()

    for copy in gk_y:
        copy.wait_recv()
    kept3 = []
    for t in range(2):
        c4g = kept[t] + gy_r[t, 0:128, :].astype(F32) + spread(
            gy_r[t, 128:192, :].astype(F32) + gy_r[t, 192:256, :].astype(F32), 2)
        gc_s[t] = (dkf[t, 0:128, :] + spread(c4g[64:128, :], 2)).astype(BF)
        kept3.append(spread(c4g[0:64, :], 2))
    gk_c = rcopy(gc_s, gc_r, GK + 6, sib)
    gk_c.start()

    for copy in gw_zg:
        copy.wait_recv()
    for copy in gw_yg:
        copy.start()

    gk_c.wait_recv()
    for t in range(2):
        c3g = kept3[t] + gc_r[t].astype(F32)
        for b in range(NB):
            ogk[t, pl.ds(b * BLOCK, BLOCK), :] = (tok[t, b] + spread(c3g[32 * b:32 * b + 32, :], 8)).astype(BF)
    out_k = pltpu.make_async_copy(ogk.at[0], gk_hbm, lsem.at[16])
    out_v = pltpu.make_async_copy(ogk.at[1], gv_hbm, lsem.at[17])
    out_k.start()
    out_v.start()

    for copy in gw_yg:
        copy.wait_recv()
    gw_cg.start()
    gw_cg.wait_recv()
    out_w = pltpu.make_async_copy(gwf, gw_hbm, lsem.at[18])
    out_w.start()

    for copy in (ag_r + ag_l + relay_r + relay_l + wz + wc + [kv_core] + kv_y + kv_z
                 + [mx_copy(b) for b in range(NB)] + [gm_copy(b) for b in range(NB)]
                 + rs1_r + rs1_l + rs2_r + rs2_l
                 + [gw_core] + gw_y + gw_z + [gw_p] + gw_zg + gw_yg + [gw_cg]
                 + gk_z + gk_y + [gk_c]):
        copy.wait_send()
    for copy in (out_q, out_att, out_k, out_v, out_w):
        copy.wait()


SCRATCH = [
    ((ROWS, W2), BF),
    ((2, NB, LOCAL, W2), BF),
    ((2, FAR, W2), BF),
    ((2, 128, W2), BF),
    ((2, 128, W2), BF),
    ((2, 64, W2), BF),
    ((2, 128, W2), BF),
    ((2, 64, W2), BF),
    ((4, ROWS, W2), BF),
    ((4, 2 * W2, W2), BF),
    ((2, ROWS, W2), BF),
    ((NB, 2, BLOCK, LOCAL + FAR), F32),
    ((NB, BLOCK, W2), F32),
    ((NB, BLOCK, W2), BF),
    ((NB, BLOCK, W2), BF),
    ((NB, BLOCK, W2), BF),
    ((NB, BLOCK, W2), BF),
    ((2, NB, BLOCK, W2), BF),
    ((2, NB, BLOCK, W2), BF),
    ((NB, BLOCK, W2), F32),
    ((2, BLOCK, W2), F32),
    ((2, BLOCK, W2), F32),
    ((2, 2, W2, W2), BF),
    ((2, 2, W2, W2), BF),
    ((2, 2, W2, W2), F32),
    ((2, 2, W2, W2), BF),
    ((3, 2, 2, 64, W2), BF),
    ((2, 2, 64, W2), BF),
    ((3, 2, 2, 16, W2), BF),
    ((2, 2, 16, W2), BF),
    ((2, 16, W2), BF),
    ((W2, 2048), BF),
    ((2, NB, LOCAL, W2), F32),
    ((2, FAR, W2), F32),
    ((2, NB, BLOCK, W2), F32),
    ((2, 256, W2), BF),
    ((2, 256, W2), BF),
    ((2, 256, W2), BF),
    ((2, 256, W2), BF),
    ((2, 128, W2), BF),
    ((2, 128, W2), BF),
    ((ROWS, W2), BF),
    ((ROWS, W2), BF),
    ((2, ROWS, W2), BF),
]


def body(queries, key_states, value_states, out_weight, cotangent):
    hbm = pl.BlockSpec(memory_space=pl.ANY)
    rows = jax.ShapeDtypeStruct((ROWS, W2), BF)
    return pl.pallas_call(
        kernel,
        out_shape=(rows, rows, rows, rows, jax.ShapeDtypeStruct((W2, 2048), BF)),
        in_specs=[hbm] * 5,
        out_specs=(hbm,) * 5,
        scratch_shapes=[pltpu.VMEM(shape, kind) for shape, kind in SCRATCH]
        + [pltpu.SemaphoreType.DMA((N_SEM,)), pltpu.SemaphoreType.DMA((N_SEM,)), pltpu.SemaphoreType.DMA((19,))],
        compiler_params=pltpu.CompilerParams(
            collective_id=0, has_side_effects=True, vmem_limit_bytes=56 * 1024 * 1024),
        name="attention",
    )(queries, key_states, value_states, out_weight, cotangent)


def solution(mesh):
    return jax.shard_map(
        body,
        mesh=mesh,
        in_specs=(P("seq", "head"), P("seq", "head"), P("seq", "head"), P("head", None), P("seq", "head")),
        out_specs=(P("seq", "head"), P("seq", "head"), P("seq", "head"), P("seq", "head"), P("head", None)),
        check_vma=False,
    )
```

```python
import math

import jax
import jax.numpy as jnp
from jax import lax
from jax.experimental import pallas as pl
from jax.experimental.pallas import tpu as pltpu
from jax.sharding import PartitionSpec as P

BF = jnp.bfloat16
F32 = jnp.float32
HD = 128
BLOCK = 256
NB = 4
ROWS = NB * BLOCK
W2 = 256
LOCAL = 512
FAR = 640
SCALE = HD**-0.5
SCALE2 = SCALE * math.log2(math.e)

AG = 0
RELAY = 8
WZ = 12
WC = 16
KS = 20
KD = 23
MX = 38
GM = 42
RS1 = 46
RS2 = 50
GW = 58
GP = 86
GS = 87
GD = 88
N_SEM = 103


def dot_nt(a, b):
    return lax.dot_general(a, b, (((1,), (1,)), ((), ())), preferred_element_type=F32)


def dot_nn(a, b):
    return lax.dot_general(a, b, (((1,), (0,)), ((), ())), preferred_element_type=F32)


def dot_tn(a, b):
    return lax.dot_general(a, b, (((0,), (0,)), ((), ())), preferred_element_type=F32)


def pool_matrix(rows):
    r = lax.broadcasted_iota(jnp.int32, (rows // 2, rows), 0)
    c = lax.broadcasted_iota(jnp.int32, (rows // 2, rows), 1)
    return jnp.where((c == 2 * r) | (c == 2 * r + 1), 0.5, 0.0).astype(BF)


def pool(x):
    return dot_nn(pool_matrix(x.shape[0]), x).astype(BF)


def spread(x, factor):
    rows = x.shape[0]
    r = lax.broadcasted_iota(jnp.int32, (rows * factor, rows), 0)
    c = lax.broadcasted_iota(jnp.int32, (rows * factor, rows), 1)
    d = r - c * factor
    e = jnp.where((d >= 0) & (d < factor), 1.0 / factor, 0.0).astype(BF)
    high = x.astype(BF)
    low = (x - high.astype(F32)).astype(BF)
    return dot_nn(e, high) + dot_nn(e, low)


def kernel(q_hbm, k_hbm, v_hbm, w_hbm, c_hbm,
           att_hbm, gq_hbm, gk_hbm, gv_hbm, gw_hbm,
           q, kl, kf, c3, c4, c5, c6, c7, r7, cg, wt, mx, probs,
           gmo, gms, gmr, rs_a, rs_ar, rs_b, rs_br, part0, part_r, part_l,
           gws, gwr, gwo, s1b, yr, s2b, zr, s3b, s4, gwf,
           dkl, dkf, tok, gs_s, gs_r, ga_s, ga_r, gs7, gr7,
           oatt, ogq, ogk,
           ssem, rsem, lsem):
    seq = lax.axis_index("seq")
    head = lax.axis_index("head")
    core = lax.rem(seq, 2)
    y = lax.rem(seq // 2, 4)
    zh = seq // 8
    x = head // 2
    z = lax.rem(head, 2)
    oc = 1 - core
    oz = 1 - z

    def xor4(a, k):
        if k == 0:
            return a
        if k == 1:
            return a + 1 - 2 * lax.rem(a, 2)
        if k == 2:
            return lax.rem(a + 2, 4)
        return 3 - a

    xr = lax.rem(x + 1, 4)
    xl = lax.rem(x + 3, 4)
    xf = lax.rem(x + 2, 4)
    right = (seq, xr * 2 + z)
    left = (seq, xl * 2 + z)
    pair = (seq, x * 2 + oz)
    sib = (zh * 8 + y * 2 + oc, head)

    def chip(a, k):
        return (xor4(zh, a) * 8 + xor4(y, k) * 2 + core, head)

    yp = [chip(0, k) for k in (1, 2, 3)]
    zp = [chip(a, 0) for a in (1, 2, 3)]
    yk = [xor4(y, k) for k in (1, 2, 3)]
    zk = [xor4(zh, k) for k in (1, 2, 3)]
    far_chips = [chip(a, k) for a in (1, 2, 3) for k in range(4)]

    def rows_of(b):
        return pl.ds(pl.multiple_of(b * BLOCK, BLOCK), BLOCK)

    def rcopy(src, dst, slot, peer):
        return pltpu.make_async_remote_copy(
            src_ref=src, dst_ref=dst, send_sem=ssem.at[slot], recv_sem=rsem.at[slot],
            device_id=peer, device_id_type=pl.DeviceIdType.MESH)

    loads = []
    for b in range(NB):
        loads.append(pltpu.make_async_copy(k_hbm.at[pl.ds(b * BLOCK, BLOCK)], kl.at[0, b, pl.ds(0, BLOCK)], lsem.at[2 * b]))
        loads.append(pltpu.make_async_copy(v_hbm.at[pl.ds(b * BLOCK, BLOCK)], kl.at[1, b, pl.ds(0, BLOCK)], lsem.at[2 * b + 1]))
    for copy in loads:
        copy.start()
    load_q = pltpu.make_async_copy(q_hbm, q, lsem.at[8])
    load_q.start()
    load_c = pltpu.make_async_copy(c_hbm, cg.at[x], lsem.at[9])
    load_c.start()
    zrow = pl.multiple_of(z * W2, W2)
    ozrow = pl.multiple_of(oz * W2, W2)
    load_w = [
        pltpu.make_async_copy(
            w_hbm.at[:, pl.ds(pl.multiple_of(512 * s + W2 * z, W2), W2)], wt.at[s, pl.ds(zrow, W2)], lsem.at[10 + s])
        for s in range(4)]
    for copy in load_w:
        copy.start()

    barrier = pltpu.get_barrier_semaphore()
    peers = [right, left, pair, sib] + yp + far_chips
    for peer in peers:
        pl.semaphore_signal(barrier, inc=1, device_id=peer, device_id_type=pl.DeviceIdType.MESH)
    pl.semaphore_wait(barrier, len(peers))

    ag_r = []
    ag_l = []
    for b in range(NB):
        rb = pl.ds(b * BLOCK, BLOCK)
        ag_r.append(rcopy(c_hbm.at[rb], cg.at[x, rb], AG + b, right))
        ag_l.append(rcopy(c_hbm.at[rb], cg.at[x, rb], AG + 4 + b, left))
    for b in range(NB):
        ag_r[b].start()
        ag_l[3 - b].start()
    crow = pl.multiple_of(core * 128, 128)
    wz = [
        rcopy(w_hbm.at[pl.ds(crow, 128), pl.ds(pl.multiple_of(512 * s + W2 * oz, W2), W2)],
              wt.at[s, pl.ds(pl.multiple_of(zrow + crow, 128), 128)], WZ + s, pair)
        for s in range(4)]
    for copy in wz:
        copy.start()

    for copy in loads:
        copy.wait()
    last = []
    for t in range(2):
        c2 = []
        for b in range(NB):
            p1 = pool(kl[t, b, 0:BLOCK, :])
            kl[t, b ^ 1, 256:384, :] = p1
            c2.append(pool(p1))
        p3 = []
        for p in range(2):
            both = jnp.concatenate([c2[2 * p], c2[2 * p + 1]], axis=0)
            kl[t, 2 - 2 * p, 384:512, :] = both
            kl[t, 3 - 2 * p, 384:512, :] = both
            p3.append(pool(both))
        p3 = jnp.concatenate(p3, axis=0)
        p4 = pool(p3)
        p5 = pool(p4)
        p6 = pool(p5)
        c3[t] = p3
        c4[t] = p4
        c5[t] = p5
        c6[t] = p6
        last.append(dot_nn(pool_matrix(16), p6))
    c7[...] = jnp.concatenate(last, axis=0).astype(BF)

    ks_own = rcopy(c3, kf.at[:, pl.ds(0, 128)], KS, sib)
    ks_own.start()
    kd_y = [rcopy(c4, kf.at[:, pl.ds(128, 64)], KD, yp[0]),
            rcopy(c5, kf.at[:, pl.ds(192, 32)], KD + 1, yp[1]),
            rcopy(c5, kf.at[:, pl.ds(224, 32)], KD + 2, yp[2])]
    kd_6 = [rcopy(c6, kf.at[:, pl.ds(256 + 16 * i, 16)], KD + 3 + i, far_chips[i]) for i in range(4)]
    kd_7 = [rcopy(c7, r7.at[i], KD + 7 + i, far_chips[4 + i]) for i in range(8)]
    for copy in kd_6 + kd_7 + kd_y:
        copy.start()

    load_q.wait()

    @pl.loop(0, NB)
    def _(b):
        for h in range(2):
            hs = slice(h * HD, h * HD + HD)
            probs[b, h, :, 0:LOCAL] = dot_nt(q[rows_of(b), hs], kl[0, b, :, hs])

    for copy in kd_y:
        copy.wait_recv()
    ks_y = rcopy(kf.at[:, pl.ds(128, 128)], kf.at[:, pl.ds(384, 128)], KS + 1, sib)
    ks_y.start()
    relay_r = []
    relay_l = []
    for i in range(2):
        rb = pl.ds(i * BLOCK, BLOCK)
        rc = pl.ds((i + 2) * BLOCK, BLOCK)
        relay_r.append(rcopy(cg.at[xl, rb], cg.at[xl, rb], RELAY + i, right))
        relay_l.append(rcopy(cg.at[xr, rc], cg.at[xr, rc], RELAY + 2 + i, left))
    ag_r[0].wait_recv()
    relay_r[0].start()
    ag_l[3].wait_recv()
    relay_l[1].start()
    for copy in kd_6 + kd_7:
        copy.wait_recv()
    wide = r7[...].astype(F32)
    for t in range(2):
        kf[t, 320:384, :] = wide[:, 8 * t:8 * t + 8, :].reshape(64, W2).astype(BF)
    ks_z = rcopy(kf.at[:, pl.ds(256, 128)], kf.at[:, pl.ds(512, 128)], KS + 2, sib)
    ks_z.start()
    ag_r[1].wait_recv()
    relay_r[1].start()
    ag_l[2].wait_recv()
    relay_l[0].start()
    wc = []
    for s in range(4):
        piece = wt.at[s, pl.ds(pl.multiple_of(ozrow + crow, 128), 128)]
        wc.append(rcopy(piece, piece, WC + s, sib))
    for s in range(4):
        wz[s].wait_recv()
        wc[s].start()
    for copy in (ks_own, ks_y, ks_z):
        copy.wait_recv()

    def mx_copy(b):
        rb = rows_of(b)
        return rcopy(mx.at[z, rb], mx.at[z, rb], MX + b, pair)

    @pl.loop(0, NB)
    def _(b):
        rb = rows_of(b)
        for h in range(2):
            hs = slice(h * HD, h * HD + HD)
            qh = q[rb, hs]
            s_l = probs[b, h, :, 0:LOCAL]
            s_f = dot_nt(qh, kf[0, :, hs])
            top = jnp.maximum(jnp.max(s_l, axis=1, keepdims=True), jnp.max(s_f, axis=1, keepdims=True))
            e_l = jnp.exp2((s_l - top) * SCALE2)
            e_f = jnp.exp2((s_f - top) * SCALE2)
            total = jnp.sum(e_l, axis=1, keepdims=True) + jnp.sum(e_f, axis=1, keepdims=True)
            inv = 1.0 / total
            p_l = e_l * inv
            p_f = e_f * inv
            probs[b, h, :, 0:LOCAL] = p_l
            probs[b, h, :, LOCAL:] = p_f
            out = dot_nn(p_l.astype(BF), kl[1, b, :, hs]) + dot_nn(p_f.astype(BF), kf[1, :, hs])
            mx[z, rb, hs] = out.astype(BF)
        mx_copy(b).start()

    load_c.wait()
    for copy in load_w:
        copy.wait()
    for copy in wc:
        copy.wait_recv()
    for i in range(2):
        relay_r[i].wait_recv()
        relay_l[i].wait_recv()
        ag_r[2 + i].wait_recv()
        ag_l[i].wait_recv()

    def gm_copy(b):
        return rcopy(gms.at[b], gmr.at[b], GM + b, pair)

    @pl.loop(0, NB)
    def _(b):
        give = jnp.zeros((BLOCK, W2), F32)
        for s in range(4):
            give += dot_nt(cg[s, rows_of(b), :], wt[s, pl.ds(ozrow, W2), :])
        gms[b] = give.astype(BF)
        gm_copy(b).start()

    row_y = pl.multiple_of(64 * y, 64)
    row_z = pl.multiple_of(64 * y + 16 * zh, 16)
    own_cols = pl.ds(2 * core, 2)
    gw_core, gw_y, gw_z, gw_zg, gw_yg, gw_cg = [], [], [], [], [], []
    for i in range(2):
        base = GW + 14 * i
        side = z if i == 0 else oz
        gw_core.append(rcopy(gws.at[i], gwr.at[i], base, sib))
        gw_y.append([rcopy(s1b.at[i, :, pl.ds(pl.multiple_of(64 * yk[k], 64), 64)], yr.at[i, k], base + 1 + k, yp[k])
                     for k in range(3)])
        gw_z.append([rcopy(s2b.at[i, :, pl.ds(pl.multiple_of(16 * zk[k], 16), 16)], zr.at[i, k], base + 4 + k, zp[k])
                     for k in range(3)])
        piece = gwf.at[side, own_cols, pl.ds(row_z, 16)]
        gw_zg.append([rcopy(piece, piece, base + 7 + k, zp[k]) for k in range(3)])
        piece = gwf.at[side, own_cols, pl.ds(row_y, 64)]
        gw_yg.append([rcopy(piece, piece, base + 10 + k, yp[k]) for k in range(3)])
        piece = gwf.at[side, own_cols]
        gw_cg.append(rcopy(piece, piece, base + 13, sib))
    gw_p = rcopy(s3b, s4, GP, pair)

    def tile(i, side):
        @pl.loop(0, 2)
        def _(j):
            gws[i, j] = dot_tn(mx[side], cg[2 * oc + j]).astype(BF)
        gw_core[i].start()

        @pl.loop(0, 2)
        def _(j):
            gwo[i, j] = dot_tn(mx[side], cg[2 * core + j])

    def after_core(i):
        gw_core[i].wait_recv()
        total = gwo[i] + gwr[i].astype(F32)
        gwo[i] = total
        s1b[i] = total.astype(BF)
        for copy in gw_y[i]:
            copy.start()

    def after_y(i):
        for copy in gw_y[i]:
            copy.wait_recv()
        total = gwo[i, :, pl.ds(row_y, 64), :]
        for k in range(3):
            total += yr[i, k].astype(F32)
        gwo[i, :, pl.ds(row_y, 64), :] = total
        s2b[i] = total.astype(BF)
        for copy in gw_z[i]:
            copy.start()

    def after_z(i):
        for copy in gw_z[i]:
            copy.wait_recv()
        total = gwo[i, :, pl.ds(row_z, 16), :]
        for k in range(3):
            total += zr[i, k].astype(F32)
        if i == 0:
            gwf[z, own_cols, pl.ds(row_z, 16), :] = total.astype(BF)
            for copy in gw_zg[0]:
                copy.start()
        else:
            s3b[...] = total.astype(BF)
            gw_p.start()

    def after_pair():
        gw_p.wait_recv()
        gwf[oz, own_cols, pl.ds(row_z, 16), :] = s4[...]
        for copy in gw_zg[1]:
            copy.start()

    def after_zg(i):
        for copy in gw_zg[i]:
            copy.wait_recv()
        for copy in gw_yg[i]:
            copy.start()

    def after_yg(i):
        for copy in gw_yg[i]:
            copy.wait_recv()
        gw_cg[i].start()

    def out_w(i, s):
        side = z if i == 0 else oz
        return pltpu.make_async_copy(
            gwf.at[side, s], gw_hbm.at[:, pl.ds(pl.multiple_of(512 * s + W2 * side, W2), W2)], lsem.at[18 + 4 * i + s])

    def after_cg(i):
        gw_cg[i].wait_recv()
        for s in range(4):
            out_w(i, s).start()

    tile(0, z)

    for b in range(NB):
        mx_copy(b).wait_recv()

    def partial(s, b):
        rb = rows_of(b)
        return dot_nn(mx[0, rb, :], wt[s, 0:W2, :]) + dot_nn(mx[1, rb, :], wt[s, W2:2 * W2, :])

    rs1_r = [rcopy(rs_a.at[i], rs_ar.at[i], RS1 + i, right) for i in range(2)]
    rs1_l = [rcopy(rs_a.at[2 + i], rs_ar.at[2 + i], RS1 + 2 + i, left) for i in range(2)]

    @pl.loop(0, NB)
    def _(b):
        rs_a[b] = partial(xf, b).astype(BF)

    for i in range(2):
        rs1_r[i].start()
        rs1_l[i].start()
    rs2_r = [rcopy(rs_b.at[0, b], rs_br.at[0, b], RS2 + b, right) for b in range(NB)]
    rs2_l = [rcopy(rs_b.at[1, b], rs_br.at[1, b], RS2 + 4 + b, left) for b in range(NB)]

    tile(1, oz)

    @pl.loop(0, 2)
    def _(i):
        rs_b[0, 2 + i] = partial(xr, 2 + i).astype(BF)
        rs_b[1, i] = partial(xl, i).astype(BF)

    for i in range(2):
        rs2_r[2 + i].start()
        rs2_l[i].start()
    after_core(0)

    @pl.loop(0, 2)
    def _(i):
        part_r[i] = partial(xr, i)
        part_l[i] = partial(xl, 2 + i)

    after_core(1)

    @pl.loop(0, NB)
    def _(b):
        keep = jnp.zeros((BLOCK, W2), F32)
        for s in range(4):
            keep += dot_nt(cg[s, rows_of(b), :], wt[s, pl.ds(zrow, W2), :])
        gmo[b] = keep

    dkf[...] = jnp.zeros_like(dkf)

    @pl.loop(0, NB)
    def _(b):
        rb = rows_of(b)
        gm_copy(b).wait_recv()
        for h in range(2):
            hs = slice(h * HD, h * HD + HD)
            do = (gmo[b, :, hs] + gmr[b, :, hs].astype(F32)).astype(BF)
            qh = q[rb, hs]
            p_l = probs[b, h, :, 0:LOCAL]
            p_f = probs[b, h, :, LOCAL:]
            dp_l = dot_nt(do, kl[1, b, :, hs])
            dp_f = dot_nt(do, kf[1, :, hs])
            inner = jnp.sum(p_l * dp_l, axis=1, keepdims=True) + jnp.sum(p_f * dp_f, axis=1, keepdims=True)
            ds_l = (p_l * (dp_l - inner)).astype(BF)
            ds_f = (p_f * (dp_f - inner)).astype(BF)
            dq = dot_nn(ds_l, kl[0, b, :, hs]) + dot_nn(ds_f, kf[0, :, hs])
            ogq[rb, hs] = (dq * SCALE).astype(BF)
            dkf[0, :, hs] += dot_tn(ds_f, qh) * SCALE
            dkf[1, :, hs] += dot_tn(p_f.astype(BF), do)
            dkl[0, b, :, hs] = dot_tn(ds_l, qh) * SCALE
            dkl[1, b, :, hs] = dot_tn(p_l.astype(BF), do)

        @pl.when(b == 0)
        def _():
            after_y(0)
            for i in range(2):
                rs1_r[i].wait_recv()
                rs1_l[i].wait_recv()
                rs_b[0, i] = (part_r[i] + rs_ar[i].astype(F32)).astype(BF)
                rs_b[1, 2 + i] = (part_l[i] + rs_ar[2 + i].astype(F32)).astype(BF)
                rs2_r[i].start()
                rs2_l[2 + i].start()

        @pl.when(b == 1)
        def _():
            after_y(1)

        @pl.when(b == 2)
        def _():
            after_z(0)

    gs_s[:, 0:128, :] = dkf[:, 0:128, :].astype(BF)
    gs_s[:, 128:384, :] = dkf[:, 384:640, :].astype(BF)
    gk_s = rcopy(gs_s, gs_r, GS, sib)
    gk_s.start()
    out_q = pltpu.make_async_copy(ogq, gq_hbm, lsem.at[14])
    out_q.start()
    after_z(1)

    @pl.loop(0, NB)
    def _(b):
        part0[b] = partial(x, b)

    gk_s.wait_recv()
    parts7 = []
    for t in range(2):
        total = dkf[t, 128:384, :] + gs_r[t, 128:384, :].astype(F32)
        ga_s[t] = total[0:192, :].astype(BF)
        parts7.append(total[192:256, :].reshape(8, 8, W2))
    gs7[...] = jnp.concatenate(parts7, axis=1).astype(BF)
    gk_d = [rcopy(ga_s.at[:, pl.ds(0, 64)], ga_r.at[:, pl.ds(0, 64)], GD, yp[0]),
            rcopy(ga_s.at[:, pl.ds(64, 32)], ga_r.at[:, pl.ds(64, 32)], GD + 1, yp[1]),
            rcopy(ga_s.at[:, pl.ds(96, 32)], ga_r.at[:, pl.ds(96, 32)], GD + 2, yp[2])]
    gk_d += [rcopy(ga_s.at[:, pl.ds(128 + 16 * i, 16)], ga_r.at[:, pl.ds(128 + 16 * i, 16)], GD + 3 + i, far_chips[i])
             for i in range(4)]
    gk_d += [rcopy(gs7.at[i], gr7.at[i], GD + 7 + i, far_chips[4 + i]) for i in range(8)]
    for copy in gk_d:
        copy.start()
    after_zg(0)
    after_pair()

    for t in range(2):
        for p in range(2):
            g2 = dkl[t, 2 - 2 * p, 384:512, :] + dkl[t, 3 - 2 * p, 384:512, :]
            for i in range(2):
                b = 2 * p + i
                g1 = dkl[t, b ^ 1, 256:384, :] + spread(g2[64 * i:64 * i + 64, :], 2)
                tok[t, b] = dkl[t, b, 0:BLOCK, :] + spread(g1, 2)
    after_yg(0)
    after_zg(1)

    for b in range(NB):
        rs2_r[b].wait_recv()
        rs2_l[b].wait_recv()
        oatt[pl.ds(b * BLOCK, BLOCK), :] = (
            part0[b] + rs_br[0, b].astype(F32) + rs_br[1, b].astype(F32)).astype(BF)
    out_att = pltpu.make_async_copy(oatt, att_hbm, lsem.at[15])
    out_att.start()

    for copy in gk_d:
        copy.wait_recv()
    g7 = jnp.sum(gr7[...].astype(F32), axis=0)
    for t in range(2):
        g6 = spread(g7[8 * t:8 * t + 8, :], 2)
        for i in range(4):
            g6 += ga_r[t, 128 + 16 * i:144 + 16 * i, :].astype(F32)
        g5 = ga_r[t, 64:96, :].astype(F32) + ga_r[t, 96:128, :].astype(F32) + spread(g6, 2)
        g4 = ga_r[t, 0:64, :].astype(F32) + spread(g5, 2)
        g3 = gs_r[t, 0:128, :].astype(F32) + spread(g4, 2)
        for b in range(NB):
            ogk[t, pl.ds(b * BLOCK, BLOCK), :] = (tok[t, b] + spread(g3[32 * b:32 * b + 32, :], 8)).astype(BF)
    out_k = pltpu.make_async_copy(ogk.at[0], gk_hbm, lsem.at[16])
    out_v = pltpu.make_async_copy(ogk.at[1], gv_hbm, lsem.at[17])
    out_k.start()
    out_v.start()

    after_cg(0)
    after_yg(1)
    after_cg(1)

    for copy in (ag_r + ag_l + relay_r + relay_l + wz + wc + [ks_own, ks_y, ks_z] + kd_y + kd_6 + kd_7
                 + [mx_copy(b) for b in range(NB)] + [gm_copy(b) for b in range(NB)]
                 + rs1_r + rs1_l + rs2_r + rs2_l
                 + gw_core + gw_y[0] + gw_y[1] + gw_z[0] + gw_z[1] + [gw_p]
                 + gw_zg[0] + gw_zg[1] + gw_yg[0] + gw_yg[1] + gw_cg + [gk_s] + gk_d):
        copy.wait_send()
    for copy in [out_q, out_att, out_k, out_v] + [out_w(i, s) for i in range(2) for s in range(4)]:
        copy.wait()


SCRATCH = [
    ((ROWS, W2), BF),
    ((2, NB, LOCAL, W2), BF),
    ((2, FAR, W2), BF),
    ((2, 128, W2), BF),
    ((2, 64, W2), BF),
    ((2, 32, W2), BF),
    ((2, 16, W2), BF),
    ((16, W2), BF),
    ((8, 16, W2), BF),
    ((4, ROWS, W2), BF),
    ((4, 2 * W2, W2), BF),
    ((2, ROWS, W2), BF),
    ((NB, 2, BLOCK, LOCAL + FAR), F32),
    ((NB, BLOCK, W2), F32),
    ((NB, BLOCK, W2), BF),
    ((NB, BLOCK, W2), BF),
    ((NB, BLOCK, W2), BF),
    ((NB, BLOCK, W2), BF),
    ((2, NB, BLOCK, W2), BF),
    ((2, NB, BLOCK, W2), BF),
    ((NB, BLOCK, W2), F32),
    ((2, BLOCK, W2), F32),
    ((2, BLOCK, W2), F32),
    ((2, 2, W2, W2), BF),
    ((2, 2, W2, W2), BF),
    ((2, 2, W2, W2), F32),
    ((2, 2, W2, W2), BF),
    ((2, 3, 2, 64, W2), BF),
    ((2, 2, 64, W2), BF),
    ((2, 3, 2, 16, W2), BF),
    ((2, 16, W2), BF),
    ((2, 16, W2), BF),
    ((2, 4, W2, W2), BF),
    ((2, NB, LOCAL, W2), F32),
    ((2, FAR, W2), F32),
    ((2, NB, BLOCK, W2), F32),
    ((2, 384, W2), BF),
    ((2, 384, W2), BF),
    ((2, 192, W2), BF),
    ((2, 192, W2), BF),
    ((8, 16, W2), BF),
    ((8, 16, W2), BF),
    ((ROWS, W2), BF),
    ((ROWS, W2), BF),
    ((2, ROWS, W2), BF),
]


def body(queries, key_states, value_states, out_weight, cotangent):
    hbm = pl.BlockSpec(memory_space=pl.ANY)
    rows = jax.ShapeDtypeStruct((ROWS, W2), BF)
    outs = (rows, rows, rows, rows, jax.ShapeDtypeStruct((W2, 2048), BF))
    return pl.pallas_call(
        kernel,
        out_shape=outs,
        in_specs=[hbm] * 5,
        out_specs=(hbm,) * 5,
        scratch_shapes=[pltpu.VMEM(shape, kind) for shape, kind in SCRATCH]
        + [pltpu.SemaphoreType.DMA((N_SEM,)), pltpu.SemaphoreType.DMA((N_SEM,)), pltpu.SemaphoreType.DMA((26,))],
        compiler_params=pltpu.CompilerParams(
            collective_id=0, has_side_effects=True, vmem_limit_bytes=60 * 1024 * 1024),
        name="attention",
    )(queries, key_states, value_states, out_weight, cotangent)


def solution(mesh):
    return jax.shard_map(
        body,
        mesh=mesh,
        in_specs=(P("seq", "head"), P("seq", "head"), P("seq", "head"), P("head", None), P("seq", "head")),
        out_specs=(P("seq", "head"), P("seq", "head"), P("seq", "head"), P("seq", "head"), P("head", None)),
        check_vma=False,
    )
```

```python
import math

import jax
import jax.numpy as jnp
from jax import lax
from jax.experimental import pallas as pl
from jax.experimental.pallas import tpu as pltpu
from jax.sharding import PartitionSpec as P

BF = jnp.bfloat16
F32 = jnp.float32
HD = 128
BLOCK = 256
NB = 4
ROWS = NB * BLOCK
W2 = 256
LOCAL = 512
FAR = 640
SCALE = HD**-0.5
SCALE2 = SCALE * math.log2(math.e)

AG = 0
RELAY = 8
WZ = 12
WC = 16
KS = 20
KD = 23
MX = 38
GM = 42
RS1 = 46
RS2 = 50
GW = 58
GP = 86
GS = 87
GD = 88
N_SEM = 103


def dot_nt(a, b):
    return lax.dot_general(a, b, (((1,), (1,)), ((), ())), preferred_element_type=F32)


def dot_nn(a, b):
    return lax.dot_general(a, b, (((1,), (0,)), ((), ())), preferred_element_type=F32)


def dot_tn(a, b):
    return lax.dot_general(a, b, (((0,), (0,)), ((), ())), preferred_element_type=F32)


def pool_matrix(rows):
    r = lax.broadcasted_iota(jnp.int32, (rows // 2, rows), 0)
    c = lax.broadcasted_iota(jnp.int32, (rows // 2, rows), 1)
    return jnp.where((c == 2 * r) | (c == 2 * r + 1), 0.5, 0.0).astype(BF)


def pool(x):
    return dot_nn(pool_matrix(x.shape[0]), x).astype(BF)


def spread(x, factor):
    rows = x.shape[0]
    r = lax.broadcasted_iota(jnp.int32, (rows * factor, rows), 0)
    c = lax.broadcasted_iota(jnp.int32, (rows * factor, rows), 1)
    d = r - c * factor
    e = jnp.where((d >= 0) & (d < factor), 1.0 / factor, 0.0).astype(BF)
    high = x.astype(BF)
    low = (x - high.astype(F32)).astype(BF)
    return dot_nn(e, high) + dot_nn(e, low)


def kernel(q_hbm, k_hbm, v_hbm, w_hbm, c_hbm,
           att_hbm, gq_hbm, gk_hbm, gv_hbm, gw_hbm,
           q, kl, kf, c3, c4, c5, c6, c7, r7, cg, wt, mx, probs,
           gmo, gms, gmr, rs_a, rs_ar, rs_b, rs_br, part0, part_r, part_l,
           gws, gwr, gwo, s1b, yr, s2b, zr, s3b, s4, gwf,
           dkl, dkf, tok, gs_s, gs_r, ga_s, ga_r, gs7, gr7,
           oatt, ogq, ogk,
           ssem, rsem, lsem):
    seq = lax.axis_index("seq")
    head = lax.axis_index("head")
    core = lax.rem(seq, 2)
    y = lax.rem(seq // 2, 4)
    zh = seq // 8
    x = head // 2
    z = lax.rem(head, 2)
    oc = 1 - core
    oz = 1 - z

    def xor4(a, k):
        if k == 0:
            return a
        if k == 1:
            return a + 1 - 2 * lax.rem(a, 2)
        if k == 2:
            return lax.rem(a + 2, 4)
        return 3 - a

    xr = lax.rem(x + 1, 4)
    xl = lax.rem(x + 3, 4)
    xf = lax.rem(x + 2, 4)
    right = (seq, xr * 2 + z)
    left = (seq, xl * 2 + z)
    pair = (seq, x * 2 + oz)
    sib = (zh * 8 + y * 2 + oc, head)

    def chip(a, k):
        return (xor4(zh, a) * 8 + xor4(y, k) * 2 + core, head)

    yp = [chip(0, k) for k in (1, 2, 3)]
    zp = [chip(a, 0) for a in (1, 2, 3)]
    yk = [xor4(y, k) for k in (1, 2, 3)]
    zk = [xor4(zh, k) for k in (1, 2, 3)]
    far_chips = [chip(a, k) for a in (1, 2, 3) for k in range(4)]

    def rows_of(b):
        return pl.ds(pl.multiple_of(b * BLOCK, BLOCK), BLOCK)

    def rcopy(src, dst, slot, peer):
        return pltpu.make_async_remote_copy(
            src_ref=src, dst_ref=dst, send_sem=ssem.at[slot], recv_sem=rsem.at[slot],
            device_id=peer, device_id_type=pl.DeviceIdType.MESH)

    barrier = pltpu.get_barrier_semaphore()
    peers = [right, left, pair, sib] + yp + far_chips
    for peer in peers:
        pl.semaphore_signal(barrier, inc=1, device_id=peer, device_id_type=pl.DeviceIdType.MESH)

    loads = []
    for b in range(NB):
        loads.append(pltpu.make_async_copy(k_hbm.at[pl.ds(b * BLOCK, BLOCK)], kl.at[0, b, pl.ds(0, BLOCK)], lsem.at[2 * b]))
        loads.append(pltpu.make_async_copy(v_hbm.at[pl.ds(b * BLOCK, BLOCK)], kl.at[1, b, pl.ds(0, BLOCK)], lsem.at[2 * b + 1]))
    for copy in loads:
        copy.start()
    load_q = pltpu.make_async_copy(q_hbm, q, lsem.at[8])
    load_q.start()
    load_c = pltpu.make_async_copy(c_hbm, cg.at[x], lsem.at[9])
    load_c.start()
    zrow = pl.multiple_of(z * W2, W2)
    ozrow = pl.multiple_of(oz * W2, W2)
    load_w = [
        pltpu.make_async_copy(
            w_hbm.at[:, pl.ds(pl.multiple_of(512 * s + W2 * z, W2), W2)], wt.at[s, pl.ds(zrow, W2)], lsem.at[10 + s])
        for s in range(4)]
    for copy in load_w:
        copy.start()

    for copy in loads:
        copy.wait()
    last = []
    for t in range(2):
        c2 = []
        for b in range(NB):
            p1 = pool(kl[t, b, 0:BLOCK, :])
            kl[t, b ^ 1, 256:384, :] = p1
            c2.append(pool(p1))
        p3 = []
        for p in range(2):
            both = jnp.concatenate([c2[2 * p], c2[2 * p + 1]], axis=0)
            kl[t, 2 - 2 * p, 384:512, :] = both
            kl[t, 3 - 2 * p, 384:512, :] = both
            p3.append(pool(both))
        p3 = jnp.concatenate(p3, axis=0)
        p4 = pool(p3)
        p5 = pool(p4)
        p6 = pool(p5)
        c3[t] = p3
        c4[t] = p4
        c5[t] = p5
        c6[t] = p6
        last.append(dot_nn(pool_matrix(16), p6))
    c7[...] = jnp.concatenate(last, axis=0).astype(BF)

    pl.semaphore_wait(barrier, len(peers))

    ks_own = rcopy(c3, kf.at[:, pl.ds(0, 128)], KS, sib)
    ks_own.start()
    kd_y = [rcopy(c4, kf.at[:, pl.ds(128, 64)], KD, yp[0]),
            rcopy(c5, kf.at[:, pl.ds(192, 32)], KD + 1, yp[1]),
            rcopy(c5, kf.at[:, pl.ds(224, 32)], KD + 2, yp[2])]
    kd_6 = [rcopy(c6, kf.at[:, pl.ds(256 + 16 * i, 16)], KD + 3 + i, far_chips[i]) for i in range(4)]
    kd_7 = [rcopy(c7, r7.at[i], KD + 7 + i, far_chips[4 + i]) for i in range(8)]
    for copy in kd_6 + kd_7 + kd_y:
        copy.start()

    ag_r = []
    ag_l = []
    for b in range(NB):
        rb = pl.ds(b * BLOCK, BLOCK)
        ag_r.append(rcopy(c_hbm.at[rb], cg.at[x, rb], AG + b, right))
        ag_l.append(rcopy(c_hbm.at[rb], cg.at[x, rb], AG + 4 + b, left))
    for b in range(NB):
        ag_r[b].start()
        ag_l[3 - b].start()
    crow = pl.multiple_of(core * 128, 128)
    wz = [
        rcopy(w_hbm.at[pl.ds(crow, 128), pl.ds(pl.multiple_of(512 * s + W2 * oz, W2), W2)],
              wt.at[s, pl.ds(pl.multiple_of(zrow + crow, 128), 128)], WZ + s, pair)
        for s in range(4)]
    for copy in wz:
        copy.start()

    load_q.wait()

    @pl.loop(0, NB)
    def _(b):
        for h in range(2):
            hs = slice(h * HD, h * HD + HD)
            probs[b, h, :, 0:LOCAL] = dot_nt(q[rows_of(b), hs], kl[0, b, :, hs])

    for copy in kd_y:
        copy.wait_recv()
    ks_y = rcopy(kf.at[:, pl.ds(128, 128)], kf.at[:, pl.ds(384, 128)], KS + 1, sib)
    ks_y.start()
    relay_r = []
    relay_l = []
    for i in range(2):
        rb = pl.ds(i * BLOCK, BLOCK)
        rc = pl.ds((i + 2) * BLOCK, BLOCK)
        relay_r.append(rcopy(cg.at[xl, rb], cg.at[xl, rb], RELAY + i, right))
        relay_l.append(rcopy(cg.at[xr, rc], cg.at[xr, rc], RELAY + 2 + i, left))
    ag_r[0].wait_recv()
    relay_r[0].start()
    ag_l[3].wait_recv()
    relay_l[1].start()
    for copy in kd_6 + kd_7:
        copy.wait_recv()
    wide = r7[...].astype(F32)
    for t in range(2):
        kf[t, 320:384, :] = wide[:, 8 * t:8 * t + 8, :].reshape(64, W2).astype(BF)
    ks_z = rcopy(kf.at[:, pl.ds(256, 128)], kf.at[:, pl.ds(512, 128)], KS + 2, sib)
    ks_z.start()
    wc = []
    for s in range(4):
        piece = wt.at[s, pl.ds(pl.multiple_of(ozrow + crow, 128), 128)]
        wc.append(rcopy(piece, piece, WC + s, sib))
    for copy in (ks_own, ks_y, ks_z):
        copy.wait_recv()

    def mx_copy(b):
        rb = rows_of(b)
        return rcopy(mx.at[z, rb], mx.at[z, rb], MX + b, pair)

    @pl.loop(0, NB)
    def _(b):
        rb = rows_of(b)
        for h in range(2):
            hs = slice(h * HD, h * HD + HD)
            qh = q[rb, hs]
            s_l = probs[b, h, :, 0:LOCAL]
            s_f = dot_nt(qh, kf[0, :, hs])
            top = jnp.maximum(jnp.max(s_l, axis=1, keepdims=True), jnp.max(s_f, axis=1, keepdims=True))
            e_l = jnp.exp2((s_l - top) * SCALE2)
            e_f = jnp.exp2((s_f - top) * SCALE2)
            total = jnp.sum(e_l, axis=1, keepdims=True) + jnp.sum(e_f, axis=1, keepdims=True)
            inv = 1.0 / total
            p_l = e_l * inv
            p_f = e_f * inv
            probs[b, h, :, 0:LOCAL] = p_l
            probs[b, h, :, LOCAL:] = p_f
            out = dot_nn(p_l.astype(BF), kl[1, b, :, hs]) + dot_nn(p_f.astype(BF), kf[1, :, hs])
            mx[z, rb, hs] = out.astype(BF)
        mx_copy(b).start()

        @pl.when(b == 0)
        def _():
            ag_r[1].wait_recv()
            relay_r[1].start()
            ag_l[2].wait_recv()
            relay_l[0].start()

        @pl.when(b == 1)
        def _():
            for s in range(4):
                wz[s].wait_recv()
                wc[s].start()

    load_c.wait()
    for copy in load_w:
        copy.wait()
    for copy in wc:
        copy.wait_recv()
    for i in range(2):
        relay_r[i].wait_recv()
        relay_l[i].wait_recv()
        ag_r[2 + i].wait_recv()
        ag_l[i].wait_recv()

    def gm_copy(b):
        return rcopy(gms.at[b], gmr.at[b], GM + b, pair)

    @pl.loop(0, NB)
    def _(b):
        give = jnp.zeros((BLOCK, W2), F32)
        for s in range(4):
            give += dot_nt(cg[s, rows_of(b), :], wt[s, pl.ds(ozrow, W2), :])
        gms[b] = give.astype(BF)
        gm_copy(b).start()

    row_y = pl.multiple_of(64 * y, 64)
    row_z = pl.multiple_of(64 * y + 16 * zh, 16)
    own_cols = pl.ds(2 * core, 2)
    gw_core, gw_y, gw_z, gw_zg, gw_yg, gw_cg = [], [], [], [], [], []
    for i in range(2):
        base = GW + 14 * i
        side = z if i == 0 else oz
        gw_core.append(rcopy(gws.at[i], gwr.at[i], base, sib))
        gw_y.append([rcopy(s1b.at[i, :, pl.ds(pl.multiple_of(64 * yk[k], 64), 64)], yr.at[i, k], base + 1 + k, yp[k])
                     for k in range(3)])
        gw_z.append([rcopy(s2b.at[i, :, pl.ds(pl.multiple_of(16 * zk[k], 16), 16)], zr.at[i, k], base + 4 + k, zp[k])
                     for k in range(3)])
        piece = gwf.at[side, own_cols, pl.ds(row_z, 16)]
        gw_zg.append([rcopy(piece, piece, base + 7 + k, zp[k]) for k in range(3)])
        piece = gwf.at[side, own_cols, pl.ds(row_y, 64)]
        gw_yg.append([rcopy(piece, piece, base + 10 + k, yp[k]) for k in range(3)])
        piece = gwf.at[side, own_cols]
        gw_cg.append(rcopy(piece, piece, base + 13, sib))
    gw_p = rcopy(s3b, s4, GP, pair)

    def tile(i, side):
        @pl.loop(0, 2)
        def _(j):
            gws[i, j] = dot_tn(mx[side], cg[2 * oc + j]).astype(BF)
        gw_core[i].start()

        @pl.loop(0, 2)
        def _(j):
            gwo[i, j] = dot_tn(mx[side], cg[2 * core + j])

    def after_core(i):
        gw_core[i].wait_recv()
        total = gwo[i] + gwr[i].astype(F32)
        gwo[i] = total
        s1b[i] = total.astype(BF)
        for copy in gw_y[i]:
            copy.start()

    def after_y(i):
        for copy in gw_y[i]:
            copy.wait_recv()
        total = gwo[i, :, pl.ds(row_y, 64), :]
        for k in range(3):
            total += yr[i, k].astype(F32)
        gwo[i, :, pl.ds(row_y, 64), :] = total
        s2b[i] = total.astype(BF)
        for copy in gw_z[i]:
            copy.start()

    def after_z(i):
        for copy in gw_z[i]:
            copy.wait_recv()
        total = gwo[i, :, pl.ds(row_z, 16), :]
        for k in range(3):
            total += zr[i, k].astype(F32)
        if i == 0:
            gwf[z, own_cols, pl.ds(row_z, 16), :] = total.astype(BF)
            for copy in gw_zg[0]:
                copy.start()
        else:
            s3b[...] = total.astype(BF)
            gw_p.start()

    def after_pair():
        gw_p.wait_recv()
        gwf[oz, own_cols, pl.ds(row_z, 16), :] = s4[...]
        for copy in gw_zg[1]:
            copy.start()

    def after_zg(i):
        for copy in gw_zg[i]:
            copy.wait_recv()
        for copy in gw_yg[i]:
            copy.start()

    def after_yg(i):
        for copy in gw_yg[i]:
            copy.wait_recv()
        gw_cg[i].start()

    def out_w(i, s):
        side = z if i == 0 else oz
        return pltpu.make_async_copy(
            gwf.at[side, s], gw_hbm.at[:, pl.ds(pl.multiple_of(512 * s + W2 * side, W2), W2)], lsem.at[18 + 4 * i + s])

    def after_cg(i):
        gw_cg[i].wait_recv()
        for s in range(4):
            out_w(i, s).start()

    tile(0, z)

    for b in range(NB):
        mx_copy(b).wait_recv()

    def partial(s, b):
        rb = rows_of(b)
        return dot_nn(mx[0, rb, :], wt[s, 0:W2, :]) + dot_nn(mx[1, rb, :], wt[s, W2:2 * W2, :])

    rs1_r = [rcopy(rs_a.at[i], rs_ar.at[i], RS1 + i, right) for i in range(2)]
    rs1_l = [rcopy(rs_a.at[2 + i], rs_ar.at[2 + i], RS1 + 2 + i, left) for i in range(2)]

    @pl.loop(0, NB)
    def _(b):
        rs_a[b] = partial(xf, b).astype(BF)

    for i in range(2):
        rs1_r[i].start()
        rs1_l[i].start()
    rs2_r = [rcopy(rs_b.at[0, b], rs_br.at[0, b], RS2 + b, right) for b in range(NB)]
    rs2_l = [rcopy(rs_b.at[1, b], rs_br.at[1, b], RS2 + 4 + b, left) for b in range(NB)]

    after_core(0)
    tile(1, oz)

    @pl.loop(0, 2)
    def _(i):
        rs_b[0, 2 + i] = partial(xr, 2 + i).astype(BF)
        rs_b[1, i] = partial(xl, i).astype(BF)

    for i in range(2):
        rs2_r[2 + i].start()
        rs2_l[i].start()
    after_core(1)

    @pl.loop(0, 2)
    def _(i):
        part_r[i] = partial(xr, i)
        part_l[i] = partial(xl, 2 + i)

    @pl.loop(0, NB)
    def _(b):
        keep = jnp.zeros((BLOCK, W2), F32)
        for s in range(4):
            keep += dot_nt(cg[s, rows_of(b), :], wt[s, pl.ds(zrow, W2), :])
        gmo[b] = keep

    after_y(0)

    dkf[...] = jnp.zeros_like(dkf)

    @pl.loop(0, NB)
    def _(b):
        rb = rows_of(b)
        gm_copy(b).wait_recv()
        for h in range(2):
            hs = slice(h * HD, h * HD + HD)
            do = (gmo[b, :, hs] + gmr[b, :, hs].astype(F32)).astype(BF)
            qh = q[rb, hs]
            p_l = probs[b, h, :, 0:LOCAL]
            p_f = probs[b, h, :, LOCAL:]
            dp_l = dot_nt(do, kl[1, b, :, hs])
            dp_f = dot_nt(do, kf[1, :, hs])
            inner = jnp.sum(p_l * dp_l, axis=1, keepdims=True) + jnp.sum(p_f * dp_f, axis=1, keepdims=True)
            ds_l = (p_l * (dp_l - inner)).astype(BF)
            ds_f = (p_f * (dp_f - inner)).astype(BF)
            dq = dot_nn(ds_l, kl[0, b, :, hs]) + dot_nn(ds_f, kf[0, :, hs])
            ogq[rb, hs] = (dq * SCALE).astype(BF)
            dkf[0, :, hs] += dot_tn(ds_f, qh) * SCALE
            dkf[1, :, hs] += dot_tn(p_f.astype(BF), do)
            dkl[0, b, :, hs] = dot_tn(ds_l, qh) * SCALE
            dkl[1, b, :, hs] = dot_tn(p_l.astype(BF), do)

        @pl.when(b == 0)
        def _():
            after_y(1)
            after_z(0)
            for i in range(2):
                rs1_r[i].wait_recv()
                rs1_l[i].wait_recv()
                rs_b[0, i] = (part_r[i] + rs_ar[i].astype(F32)).astype(BF)
                rs_b[1, 2 + i] = (part_l[i] + rs_ar[2 + i].astype(F32)).astype(BF)
                rs2_r[i].start()
                rs2_l[2 + i].start()

        @pl.when(b == 1)
        def _():
            after_zg(0)
            after_z(1)

        @pl.when(b == 2)
        def _():
            after_yg(0)
            after_pair()

    gs_s[:, 0:128, :] = dkf[:, 0:128, :].astype(BF)
    gs_s[:, 128:384, :] = dkf[:, 384:640, :].astype(BF)
    gk_s = rcopy(gs_s, gs_r, GS, sib)
    gk_s.start()
    out_q = pltpu.make_async_copy(ogq, gq_hbm, lsem.at[14])
    out_q.start()
    after_zg(1)

    @pl.loop(0, NB)
    def _(b):
        part0[b] = partial(x, b)

    gk_s.wait_recv()
    parts7 = []
    for t in range(2):
        total = dkf[t, 128:384, :] + gs_r[t, 128:384, :].astype(F32)
        ga_s[t] = total[0:192, :].astype(BF)
        parts7.append(total[192:256, :].reshape(8, 8, W2))
    gs7[...] = jnp.concatenate(parts7, axis=1).astype(BF)
    gk_d = [rcopy(ga_s.at[:, pl.ds(0, 64)], ga_r.at[:, pl.ds(0, 64)], GD, yp[0]),
            rcopy(ga_s.at[:, pl.ds(64, 32)], ga_r.at[:, pl.ds(64, 32)], GD + 1, yp[1]),
            rcopy(ga_s.at[:, pl.ds(96, 32)], ga_r.at[:, pl.ds(96, 32)], GD + 2, yp[2])]
    gk_d += [rcopy(ga_s.at[:, pl.ds(128 + 16 * i, 16)], ga_r.at[:, pl.ds(128 + 16 * i, 16)], GD + 3 + i, far_chips[i])
             for i in range(4)]
    gk_d += [rcopy(gs7.at[i], gr7.at[i], GD + 7 + i, far_chips[4 + i]) for i in range(8)]
    for copy in gk_d:
        copy.start()
    after_cg(0)

    for t in range(2):
        for p in range(2):
            g2 = dkl[t, 2 - 2 * p, 384:512, :] + dkl[t, 3 - 2 * p, 384:512, :]
            for i in range(2):
                b = 2 * p + i
                g1 = dkl[t, b ^ 1, 256:384, :] + spread(g2[64 * i:64 * i + 64, :], 2)
                tok[t, b] = dkl[t, b, 0:BLOCK, :] + spread(g1, 2)
    after_yg(1)

    for b in range(NB):
        rs2_r[b].wait_recv()
        rs2_l[b].wait_recv()
        oatt[pl.ds(b * BLOCK, BLOCK), :] = (
            part0[b] + rs_br[0, b].astype(F32) + rs_br[1, b].astype(F32)).astype(BF)
    out_att = pltpu.make_async_copy(oatt, att_hbm, lsem.at[15])
    out_att.start()

    for copy in gk_d:
        copy.wait_recv()
    g7 = jnp.sum(gr7[...].astype(F32), axis=0)
    for t in range(2):
        g6 = spread(g7[8 * t:8 * t + 8, :], 2)
        for i in range(4):
            g6 += ga_r[t, 128 + 16 * i:144 + 16 * i, :].astype(F32)
        g5 = ga_r[t, 64:96, :].astype(F32) + ga_r[t, 96:128, :].astype(F32) + spread(g6, 2)
        g4 = ga_r[t, 0:64, :].astype(F32) + spread(g5, 2)
        g3 = gs_r[t, 0:128, :].astype(F32) + spread(g4, 2)
        for b in range(NB):
            ogk[t, pl.ds(b * BLOCK, BLOCK), :] = (tok[t, b] + spread(g3[32 * b:32 * b + 32, :], 8)).astype(BF)
    out_k = pltpu.make_async_copy(ogk.at[0], gk_hbm, lsem.at[16])
    out_v = pltpu.make_async_copy(ogk.at[1], gv_hbm, lsem.at[17])
    out_k.start()
    out_v.start()

    after_cg(1)

    for copy in (ag_r + ag_l + relay_r + relay_l + wz + wc + [ks_own, ks_y, ks_z] + kd_y + kd_6 + kd_7
                 + [mx_copy(b) for b in range(NB)] + [gm_copy(b) for b in range(NB)]
                 + rs1_r + rs1_l + rs2_r + rs2_l
                 + gw_core + gw_y[0] + gw_y[1] + gw_z[0] + gw_z[1] + [gw_p]
                 + gw_zg[0] + gw_zg[1] + gw_yg[0] + gw_yg[1] + gw_cg + [gk_s] + gk_d):
        copy.wait_send()
    for copy in [out_q, out_att, out_k, out_v] + [out_w(i, s) for i in range(2) for s in range(4)]:
        copy.wait()


SCRATCH = [
    ((ROWS, W2), BF),
    ((2, NB, LOCAL, W2), BF),
    ((2, FAR, W2), BF),
    ((2, 128, W2), BF),
    ((2, 64, W2), BF),
    ((2, 32, W2), BF),
    ((2, 16, W2), BF),
    ((16, W2), BF),
    ((8, 16, W2), BF),
    ((4, ROWS, W2), BF),
    ((4, 2 * W2, W2), BF),
    ((2, ROWS, W2), BF),
    ((NB, 2, BLOCK, LOCAL + FAR), F32),
    ((NB, BLOCK, W2), F32),
    ((NB, BLOCK, W2), BF),
    ((NB, BLOCK, W2), BF),
    ((NB, BLOCK, W2), BF),
    ((NB, BLOCK, W2), BF),
    ((2, NB, BLOCK, W2), BF),
    ((2, NB, BLOCK, W2), BF),
    ((NB, BLOCK, W2), F32),
    ((2, BLOCK, W2), F32),
    ((2, BLOCK, W2), F32),
    ((2, 2, W2, W2), BF),
    ((2, 2, W2, W2), BF),
    ((2, 2, W2, W2), F32),
    ((2, 2, W2, W2), BF),
    ((2, 3, 2, 64, W2), BF),
    ((2, 2, 64, W2), BF),
    ((2, 3, 2, 16, W2), BF),
    ((2, 16, W2), BF),
    ((2, 16, W2), BF),
    ((2, 4, W2, W2), BF),
    ((2, NB, LOCAL, W2), F32),
    ((2, FAR, W2), F32),
    ((2, NB, BLOCK, W2), F32),
    ((2, 384, W2), BF),
    ((2, 384, W2), BF),
    ((2, 192, W2), BF),
    ((2, 192, W2), BF),
    ((8, 16, W2), BF),
    ((8, 16, W2), BF),
    ((ROWS, W2), BF),
    ((ROWS, W2), BF),
    ((2, ROWS, W2), BF),
]


def body(queries, key_states, value_states, out_weight, cotangent):
    hbm = pl.BlockSpec(memory_space=pl.ANY)
    rows = jax.ShapeDtypeStruct((ROWS, W2), BF)
    outs = (rows, rows, rows, rows, jax.ShapeDtypeStruct((W2, 2048), BF))
    return pl.pallas_call(
        kernel,
        out_shape=outs,
        in_specs=[hbm] * 5,
        out_specs=(hbm,) * 5,
        scratch_shapes=[pltpu.VMEM(shape, kind) for shape, kind in SCRATCH]
        + [pltpu.SemaphoreType.DMA((N_SEM,)), pltpu.SemaphoreType.DMA((N_SEM,)), pltpu.SemaphoreType.DMA((26,))],
        compiler_params=pltpu.CompilerParams(
            collective_id=0, has_side_effects=True, vmem_limit_bytes=60 * 1024 * 1024),
        name="attention",
    )(queries, key_states, value_states, out_weight, cotangent)


def solution(mesh):
    return jax.shard_map(
        body,
        mesh=mesh,
        in_specs=(P("seq", "head"), P("seq", "head"), P("seq", "head"), P("head", None), P("seq", "head")),
        out_specs=(P("seq", "head"), P("seq", "head"), P("seq", "head"), P("seq", "head"), P("head", None)),
        check_vma=False,
    )
```

```python
import math

import jax
import jax.numpy as jnp
from jax import lax
from jax.experimental import pallas as pl
from jax.experimental.pallas import tpu as pltpu
from jax.sharding import PartitionSpec as P

BF = jnp.bfloat16
F32 = jnp.float32
HD = 128
BLOCK = 256
NB = 4
ROWS = NB * BLOCK
W2 = 256
LOCAL = 512
FAR = 640
SCALE = HD**-0.5
SCALE2 = SCALE * math.log2(math.e)

AG = 0
RELAY = 8
WZ = 12
WC = 16
KS = 20
KD = 23
MX = 38
GM = 42
RS1 = 46
RS2 = 50
GW = 58
GP = 86
GS = 87
GD = 88
N_SEM = 103


def dot_nt(a, b):
    return lax.dot_general(a, b, (((1,), (1,)), ((), ())), preferred_element_type=F32)


def dot_nn(a, b):
    return lax.dot_general(a, b, (((1,), (0,)), ((), ())), preferred_element_type=F32)


def dot_tn(a, b):
    return lax.dot_general(a, b, (((0,), (0,)), ((), ())), preferred_element_type=F32)


def pool_matrix(rows):
    r = lax.broadcasted_iota(jnp.int32, (rows // 2, rows), 0)
    c = lax.broadcasted_iota(jnp.int32, (rows // 2, rows), 1)
    return jnp.where((c == 2 * r) | (c == 2 * r + 1), 0.5, 0.0).astype(BF)


def pool(x):
    return dot_nn(pool_matrix(x.shape[0]), x).astype(BF)


def spread(x, factor):
    rows = x.shape[0]
    r = lax.broadcasted_iota(jnp.int32, (rows * factor, rows), 0)
    c = lax.broadcasted_iota(jnp.int32, (rows * factor, rows), 1)
    d = r - c * factor
    e = jnp.where((d >= 0) & (d < factor), 1.0 / factor, 0.0).astype(BF)
    high = x.astype(BF)
    low = (x - high.astype(F32)).astype(BF)
    return dot_nn(e, high) + dot_nn(e, low)


def kernel(q_hbm, k_hbm, v_hbm, w_hbm, c_hbm,
           att_hbm, gq_hbm, gk_hbm, gv_hbm, gw_hbm,
           q, kl, kf, c3, c4, c5, c6, c7, r7, cg, wt, mx, probs,
           gmo, gms, gmr, rs_a, rs_ar, rs_b, rs_br, part0, part_r, part_l,
           gws, gwr, gwo, s1b, yr, s2b, zr, gwf,
           dkl, dkf, tok, gs_s, gs_r, ga_s, ga_r, gs7, gr7,
           oatt, ogq, ogk,
           ssem, rsem, lsem):
    seq = lax.axis_index("seq")
    head = lax.axis_index("head")
    core = lax.rem(seq, 2)
    y = lax.rem(seq // 2, 4)
    zh = seq // 8
    x = head // 2
    z = lax.rem(head, 2)
    oc = 1 - core
    oz = 1 - z

    def xor4(a, k):
        if k == 0:
            return a
        if k == 1:
            return a + 1 - 2 * lax.rem(a, 2)
        if k == 2:
            return lax.rem(a + 2, 4)
        return 3 - a

    xr = lax.rem(x + 1, 4)
    xl = lax.rem(x + 3, 4)
    xf = lax.rem(x + 2, 4)
    right = (seq, xr * 2 + z)
    left = (seq, xl * 2 + z)
    pair = (seq, x * 2 + oz)
    sib = (zh * 8 + y * 2 + oc, head)

    def chip(a, k):
        return (xor4(zh, a) * 8 + xor4(y, k) * 2 + core, head)

    yp = [chip(0, k) for k in (1, 2, 3)]
    zp = [chip(a, 0) for a in (1, 2, 3)]
    zp_pair = [(xor4(zh, k) * 8 + y * 2 + core, x * 2 + oz) for k in (1, 2, 3)]
    yk = [xor4(y, k) for k in (1, 2, 3)]
    zk = [xor4(zh, k) for k in (1, 2, 3)]
    far_chips = [chip(a, k) for a in (1, 2, 3) for k in range(4)]

    def rows_of(b):
        return pl.ds(pl.multiple_of(b * BLOCK, BLOCK), BLOCK)

    def rcopy(src, dst, slot, peer):
        return pltpu.make_async_remote_copy(
            src_ref=src, dst_ref=dst, send_sem=ssem.at[slot], recv_sem=rsem.at[slot],
            device_id=peer, device_id_type=pl.DeviceIdType.MESH)

    barrier = pltpu.get_barrier_semaphore()
    peers = [right, left, pair, sib] + yp + far_chips + zp_pair
    for peer in peers:
        pl.semaphore_signal(barrier, inc=1, device_id=peer, device_id_type=pl.DeviceIdType.MESH)

    loads = []
    for b in range(NB):
        loads.append(pltpu.make_async_copy(k_hbm.at[pl.ds(b * BLOCK, BLOCK)], kl.at[0, b, pl.ds(0, BLOCK)], lsem.at[2 * b]))
        loads.append(pltpu.make_async_copy(v_hbm.at[pl.ds(b * BLOCK, BLOCK)], kl.at[1, b, pl.ds(0, BLOCK)], lsem.at[2 * b + 1]))
    for copy in loads:
        copy.start()
    load_q = pltpu.make_async_copy(q_hbm, q, lsem.at[8])
    load_q.start()
    load_c = pltpu.make_async_copy(c_hbm, cg.at[x], lsem.at[9])
    load_c.start()
    zrow = pl.multiple_of(z * W2, W2)
    ozrow = pl.multiple_of(oz * W2, W2)
    load_w = [
        pltpu.make_async_copy(
            w_hbm.at[:, pl.ds(pl.multiple_of(512 * s + W2 * z, W2), W2)], wt.at[s, pl.ds(zrow, W2)], lsem.at[10 + s])
        for s in range(4)]
    for copy in load_w:
        copy.start()

    for copy in loads:
        copy.wait()
    last = []
    for t in range(2):
        c2 = []
        for b in range(NB):
            p1 = pool(kl[t, b, 0:BLOCK, :])
            kl[t, b ^ 1, 256:384, :] = p1
            c2.append(pool(p1))
        p3 = []
        for p in range(2):
            both = jnp.concatenate([c2[2 * p], c2[2 * p + 1]], axis=0)
            kl[t, 2 - 2 * p, 384:512, :] = both
            kl[t, 3 - 2 * p, 384:512, :] = both
            p3.append(pool(both))
        p3 = jnp.concatenate(p3, axis=0)
        p4 = pool(p3)
        p5 = pool(p4)
        p6 = pool(p5)
        c3[t] = p3
        c4[t] = p4
        c5[t] = p5
        c6[t] = p6
        last.append(dot_nn(pool_matrix(16), p6))
    c7[...] = jnp.concatenate(last, axis=0).astype(BF)

    pl.semaphore_wait(barrier, len(peers))

    ks_own = rcopy(c3, kf.at[:, pl.ds(0, 128)], KS, sib)
    ks_own.start()
    kd_y = [rcopy(c4, kf.at[:, pl.ds(128, 64)], KD, yp[0]),
            rcopy(c5, kf.at[:, pl.ds(192, 32)], KD + 1, yp[1]),
            rcopy(c5, kf.at[:, pl.ds(224, 32)], KD + 2, yp[2])]
    kd_6 = [rcopy(c6, kf.at[:, pl.ds(256 + 16 * i, 16)], KD + 3 + i, far_chips[i]) for i in range(4)]
    kd_7 = [rcopy(c7, r7.at[i], KD + 7 + i, far_chips[4 + i]) for i in range(8)]
    for copy in kd_6 + kd_7 + kd_y:
        copy.start()

    ag_r = []
    ag_l = []
    for b in range(NB):
        rb = pl.ds(b * BLOCK, BLOCK)
        ag_r.append(rcopy(c_hbm.at[rb], cg.at[x, rb], AG + b, right))
        ag_l.append(rcopy(c_hbm.at[rb], cg.at[x, rb], AG + 4 + b, left))
    for b in range(NB):
        ag_r[b].start()
        ag_l[3 - b].start()
    crow = pl.multiple_of(core * 128, 128)
    wz = [
        rcopy(w_hbm.at[pl.ds(crow, 128), pl.ds(pl.multiple_of(512 * s + W2 * oz, W2), W2)],
              wt.at[s, pl.ds(pl.multiple_of(zrow + crow, 128), 128)], WZ + s, pair)
        for s in range(4)]
    for copy in wz:
        copy.start()

    load_q.wait()

    @pl.loop(0, NB)
    def _(b):
        for h in range(2):
            hs = slice(h * HD, h * HD + HD)
            probs[b, h, :, 0:LOCAL] = dot_nt(q[rows_of(b), hs], kl[0, b, :, hs])

    for copy in kd_y:
        copy.wait_recv()
    ks_y = rcopy(kf.at[:, pl.ds(128, 128)], kf.at[:, pl.ds(384, 128)], KS + 1, sib)
    ks_y.start()
    relay_r = []
    relay_l = []
    for i in range(2):
        rb = pl.ds(i * BLOCK, BLOCK)
        rc = pl.ds((i + 2) * BLOCK, BLOCK)
        relay_r.append(rcopy(cg.at[xl, rb], cg.at[xl, rb], RELAY + i, right))
        relay_l.append(rcopy(cg.at[xr, rc], cg.at[xr, rc], RELAY + 2 + i, left))
    ag_r[0].wait_recv()
    relay_r[0].start()
    ag_l[3].wait_recv()
    relay_l[1].start()
    for copy in kd_6 + kd_7:
        copy.wait_recv()
    wide = r7[...].astype(F32)
    for t in range(2):
        kf[t, 320:384, :] = wide[:, 8 * t:8 * t + 8, :].reshape(64, W2).astype(BF)
    ks_z = rcopy(kf.at[:, pl.ds(256, 128)], kf.at[:, pl.ds(512, 128)], KS + 2, sib)
    ks_z.start()
    wc = []
    for s in range(4):
        piece = wt.at[s, pl.ds(pl.multiple_of(ozrow + crow, 128), 128)]
        wc.append(rcopy(piece, piece, WC + s, sib))
    for copy in (ks_own, ks_y, ks_z):
        copy.wait_recv()

    def mx_copy(b):
        rb = rows_of(b)
        return rcopy(mx.at[z, rb], mx.at[z, rb], MX + b, pair)

    @pl.loop(0, NB)
    def _(b):
        rb = rows_of(b)
        for h in range(2):
            hs = slice(h * HD, h * HD + HD)
            qh = q[rb, hs]
            s_l = probs[b, h, :, 0:LOCAL]
            s_f = dot_nt(qh, kf[0, :, hs])
            top = jnp.maximum(jnp.max(s_l, axis=1, keepdims=True), jnp.max(s_f, axis=1, keepdims=True))
            e_l = jnp.exp2((s_l - top) * SCALE2)
            e_f = jnp.exp2((s_f - top) * SCALE2)
            total = jnp.sum(e_l, axis=1, keepdims=True) + jnp.sum(e_f, axis=1, keepdims=True)
            inv = 1.0 / total
            p_l = e_l * inv
            p_f = e_f * inv
            probs[b, h, :, 0:LOCAL] = p_l
            probs[b, h, :, LOCAL:] = p_f
            out = dot_nn(p_l.astype(BF), kl[1, b, :, hs]) + dot_nn(p_f.astype(BF), kf[1, :, hs])
            mx[z, rb, hs] = out.astype(BF)
        mx_copy(b).start()

        @pl.when(b == 0)
        def _():
            ag_r[1].wait_recv()
            relay_r[1].start()
            ag_l[2].wait_recv()
            relay_l[0].start()

        @pl.when(b == 1)
        def _():
            for s in range(4):
                wz[s].wait_recv()
                wc[s].start()

    load_c.wait()
    for copy in load_w:
        copy.wait()
    for copy in wc:
        copy.wait_recv()
    for i in range(2):
        relay_r[i].wait_recv()
        relay_l[i].wait_recv()
        ag_r[2 + i].wait_recv()
        ag_l[i].wait_recv()

    def gm_copy(b):
        return rcopy(gms.at[b], gmr.at[b], GM + b, pair)

    @pl.loop(0, NB)
    def _(b):
        give = jnp.zeros((BLOCK, W2), F32)
        for s in range(4):
            give += dot_nt(cg[s, rows_of(b), :], wt[s, pl.ds(ozrow, W2), :])
        gms[b] = give.astype(BF)
        gm_copy(b).start()

    row_y = pl.multiple_of(64 * y, 64)
    row_z = pl.multiple_of(64 * y + 16 * zh, 16)
    own_cols = pl.ds(2 * core, 2)
    gw_core, gw_y, gw_z, gw_zg, gw_yg, gw_cg = [], [], [], [], [], []
    for i in range(2):
        base = GW + 14 * i
        side = z if i == 0 else oz
        gw_core.append(rcopy(gws.at[i], gwr.at[i], base, sib))
        gw_y.append([rcopy(s1b.at[i, :, pl.ds(pl.multiple_of(64 * yk[k], 64), 64)], yr.at[i, k], base + 1 + k, yp[k])
                     for k in range(3)])
        to = zp if i == 0 else zp_pair
        gw_z.append([rcopy(s2b.at[i, :, pl.ds(pl.multiple_of(16 * zk[k], 16), 16)], zr.at[i, k], base + 4 + k, to[k])
                     for k in range(3)])
        piece = gwf.at[side, own_cols, pl.ds(row_z, 16)]
        gw_zg.append([rcopy(piece, piece, base + 7 + k, zp[k]) for k in range(3)])
        piece = gwf.at[side, own_cols, pl.ds(row_y, 64)]
        gw_yg.append([rcopy(piece, piece, base + 10 + k, yp[k]) for k in range(3)])
        piece = gwf.at[side, own_cols]
        gw_cg.append(rcopy(piece, piece, base + 13, sib))
    gw_z[1].append(rcopy(s2b.at[1, :, pl.ds(pl.multiple_of(16 * zh, 16), 16)], zr.at[1, 3], GP, pair))

    def tile(i, side):
        @pl.loop(0, 2)
        def _(j):
            gws[i, j] = dot_tn(mx[side], cg[2 * oc + j]).astype(BF)
        gw_core[i].start()

        @pl.loop(0, 2)
        def _(j):
            gwo[i, j] = dot_tn(mx[side], cg[2 * core + j])

    def after_core(i):
        gw_core[i].wait_recv()
        total = gwo[i] + gwr[i].astype(F32)
        gwo[i] = total
        s1b[i] = total.astype(BF)
        for copy in gw_y[i]:
            copy.start()

    def after_y(i):
        for copy in gw_y[i]:
            copy.wait_recv()
        total = gwo[i, :, pl.ds(row_y, 64), :]
        for k in range(3):
            total += yr[i, k].astype(F32)
        gwo[i, :, pl.ds(row_y, 64), :] = total
        s2b[i] = total.astype(BF)
        for copy in gw_z[i]:
            copy.start()

    def after_z(i):
        for copy in gw_z[i]:
            copy.wait_recv()
        if i == 0:
            total = gwo[0, :, pl.ds(row_z, 16), :]
        else:
            total = zr[1, 3].astype(F32)
        for k in range(3):
            total += zr[i, k].astype(F32)
        gwf[z if i == 0 else oz, own_cols, pl.ds(row_z, 16), :] = total.astype(BF)
        for copy in gw_zg[i]:
            copy.start()

    def after_zg(i):
        for copy in gw_zg[i]:
            copy.wait_recv()
        for copy in gw_yg[i]:
            copy.start()

    def after_yg(i):
        for copy in gw_yg[i]:
            copy.wait_recv()
        gw_cg[i].start()

    def out_w(i, s):
        side = z if i == 0 else oz
        return pltpu.make_async_copy(
            gwf.at[side, s], gw_hbm.at[:, pl.ds(pl.multiple_of(512 * s + W2 * side, W2), W2)], lsem.at[18 + 4 * i + s])

    def after_cg(i):
        gw_cg[i].wait_recv()
        for s in range(4):
            out_w(i, s).start()

    tile(0, z)

    for b in range(NB):
        mx_copy(b).wait_recv()

    def partial(s, b):
        rb = rows_of(b)
        return dot_nn(mx[0, rb, :], wt[s, 0:W2, :]) + dot_nn(mx[1, rb, :], wt[s, W2:2 * W2, :])

    rs1_r = [rcopy(rs_a.at[i], rs_ar.at[i], RS1 + i, right) for i in range(2)]
    rs1_l = [rcopy(rs_a.at[2 + i], rs_ar.at[2 + i], RS1 + 2 + i, left) for i in range(2)]

    @pl.loop(0, NB)
    def _(b):
        rs_a[b] = partial(xf, b).astype(BF)

    for i in range(2):
        rs1_r[i].start()
        rs1_l[i].start()
    rs2_r = [rcopy(rs_b.at[0, b], rs_br.at[0, b], RS2 + b, right) for b in range(NB)]
    rs2_l = [rcopy(rs_b.at[1, b], rs_br.at[1, b], RS2 + 4 + b, left) for b in range(NB)]

    after_core(0)
    tile(1, oz)

    @pl.loop(0, 2)
    def _(i):
        rs_b[0, 2 + i] = partial(xr, 2 + i).astype(BF)
        rs_b[1, i] = partial(xl, i).astype(BF)

    for i in range(2):
        rs2_r[2 + i].start()
        rs2_l[i].start()
    after_core(1)

    @pl.loop(0, 2)
    def _(i):
        part_r[i] = partial(xr, i)
        part_l[i] = partial(xl, 2 + i)

    @pl.loop(0, NB)
    def _(b):
        keep = jnp.zeros((BLOCK, W2), F32)
        for s in range(4):
            keep += dot_nt(cg[s, rows_of(b), :], wt[s, pl.ds(zrow, W2), :])
        gmo[b] = keep

    after_y(0)

    dkf[...] = jnp.zeros_like(dkf)

    @pl.loop(0, NB)
    def _(b):
        rb = rows_of(b)
        gm_copy(b).wait_recv()
        for h in range(2):
            hs = slice(h * HD, h * HD + HD)
            do = (gmo[b, :, hs] + gmr[b, :, hs].astype(F32)).astype(BF)
            qh = q[rb, hs]
            p_l = probs[b, h, :, 0:LOCAL]
            p_f = probs[b, h, :, LOCAL:]
            dp_l = dot_nt(do, kl[1, b, :, hs])
            dp_f = dot_nt(do, kf[1, :, hs])
            inner = jnp.sum(p_l * dp_l, axis=1, keepdims=True) + jnp.sum(p_f * dp_f, axis=1, keepdims=True)
            ds_l = (p_l * (dp_l - inner)).astype(BF)
            ds_f = (p_f * (dp_f - inner)).astype(BF)
            dq = dot_nn(ds_l, kl[0, b, :, hs]) + dot_nn(ds_f, kf[0, :, hs])
            ogq[rb, hs] = (dq * SCALE).astype(BF)
            dkf[0, :, hs] += dot_tn(ds_f, qh) * SCALE
            dkf[1, :, hs] += dot_tn(p_f.astype(BF), do)
            dkl[0, b, :, hs] = dot_tn(ds_l, qh) * SCALE
            dkl[1, b, :, hs] = dot_tn(p_l.astype(BF), do)

        @pl.when(b == 0)
        def _():
            after_y(1)
            for i in range(2):
                rs1_r[i].wait_recv()
                rs1_l[i].wait_recv()
                rs_b[0, i] = (part_r[i] + rs_ar[i].astype(F32)).astype(BF)
                rs_b[1, 2 + i] = (part_l[i] + rs_ar[2 + i].astype(F32)).astype(BF)
                rs2_r[i].start()
                rs2_l[2 + i].start()


        @pl.when(b == 2)
        def _():
            after_z(0)

    gs_s[:, 0:128, :] = dkf[:, 0:128, :].astype(BF)
    gs_s[:, 128:384, :] = dkf[:, 384:640, :].astype(BF)
    gk_s = rcopy(gs_s, gs_r, GS, sib)
    gk_s.start()
    out_q = pltpu.make_async_copy(ogq, gq_hbm, lsem.at[14])
    out_q.start()
    after_z(1)

    @pl.loop(0, NB)
    def _(b):
        part0[b] = partial(x, b)

    after_zg(0)

    gk_s.wait_recv()
    parts7 = []
    for t in range(2):
        total = dkf[t, 128:384, :] + gs_r[t, 128:384, :].astype(F32)
        ga_s[t] = total[0:192, :].astype(BF)
        parts7.append(total[192:256, :].reshape(8, 8, W2))
    gs7[...] = jnp.concatenate(parts7, axis=1).astype(BF)
    gk_d = [rcopy(ga_s.at[:, pl.ds(0, 64)], ga_r.at[:, pl.ds(0, 64)], GD, yp[0]),
            rcopy(ga_s.at[:, pl.ds(64, 32)], ga_r.at[:, pl.ds(64, 32)], GD + 1, yp[1]),
            rcopy(ga_s.at[:, pl.ds(96, 32)], ga_r.at[:, pl.ds(96, 32)], GD + 2, yp[2])]
    gk_d += [rcopy(ga_s.at[:, pl.ds(128 + 16 * i, 16)], ga_r.at[:, pl.ds(128 + 16 * i, 16)], GD + 3 + i, far_chips[i])
             for i in range(4)]
    gk_d += [rcopy(gs7.at[i], gr7.at[i], GD + 7 + i, far_chips[4 + i]) for i in range(8)]
    for copy in gk_d:
        copy.start()

    for t in range(2):
        for p in range(2):
            g2 = dkl[t, 2 - 2 * p, 384:512, :] + dkl[t, 3 - 2 * p, 384:512, :]
            for i in range(2):
                b = 2 * p + i
                g1 = dkl[t, b ^ 1, 256:384, :] + spread(g2[64 * i:64 * i + 64, :], 2)
                tok[t, b] = dkl[t, b, 0:BLOCK, :] + spread(g1, 2)
    after_zg(1)

    for b in range(NB):
        rs2_r[b].wait_recv()
        rs2_l[b].wait_recv()
        oatt[pl.ds(b * BLOCK, BLOCK), :] = (
            part0[b] + rs_br[0, b].astype(F32) + rs_br[1, b].astype(F32)).astype(BF)
    out_att = pltpu.make_async_copy(oatt, att_hbm, lsem.at[15])
    out_att.start()
    after_yg(0)

    for copy in gk_d:
        copy.wait_recv()
    g7 = jnp.sum(gr7[...].astype(F32), axis=0)
    for t in range(2):
        g6 = spread(g7[8 * t:8 * t + 8, :], 2)
        for i in range(4):
            g6 += ga_r[t, 128 + 16 * i:144 + 16 * i, :].astype(F32)
        g5 = ga_r[t, 64:96, :].astype(F32) + ga_r[t, 96:128, :].astype(F32) + spread(g6, 2)
        g4 = ga_r[t, 0:64, :].astype(F32) + spread(g5, 2)
        g3 = gs_r[t, 0:128, :].astype(F32) + spread(g4, 2)
        for b in range(NB):
            ogk[t, pl.ds(b * BLOCK, BLOCK), :] = (tok[t, b] + spread(g3[32 * b:32 * b + 32, :], 8)).astype(BF)
    out_k = pltpu.make_async_copy(ogk.at[0], gk_hbm, lsem.at[16])
    out_v = pltpu.make_async_copy(ogk.at[1], gv_hbm, lsem.at[17])
    out_k.start()
    out_v.start()

    after_cg(0)
    after_yg(1)
    after_cg(1)

    for copy in (ag_r + ag_l + relay_r + relay_l + wz + wc + [ks_own, ks_y, ks_z] + kd_y + kd_6 + kd_7
                 + [mx_copy(b) for b in range(NB)] + [gm_copy(b) for b in range(NB)]
                 + rs1_r + rs1_l + rs2_r + rs2_l
                 + gw_core + gw_y[0] + gw_y[1] + gw_z[0] + gw_z[1]
                 + gw_zg[0] + gw_zg[1] + gw_yg[0] + gw_yg[1] + gw_cg + [gk_s] + gk_d):
        copy.wait_send()
    for copy in [out_q, out_att, out_k, out_v] + [out_w(i, s) for i in range(2) for s in range(4)]:
        copy.wait()


SCRATCH = [
    ((ROWS, W2), BF),
    ((2, NB, LOCAL, W2), BF),
    ((2, FAR, W2), BF),
    ((2, 128, W2), BF),
    ((2, 64, W2), BF),
    ((2, 32, W2), BF),
    ((2, 16, W2), BF),
    ((16, W2), BF),
    ((8, 16, W2), BF),
    ((4, ROWS, W2), BF),
    ((4, 2 * W2, W2), BF),
    ((2, ROWS, W2), BF),
    ((NB, 2, BLOCK, LOCAL + FAR), F32),
    ((NB, BLOCK, W2), F32),
    ((NB, BLOCK, W2), BF),
    ((NB, BLOCK, W2), BF),
    ((NB, BLOCK, W2), BF),
    ((NB, BLOCK, W2), BF),
    ((2, NB, BLOCK, W2), BF),
    ((2, NB, BLOCK, W2), BF),
    ((NB, BLOCK, W2), F32),
    ((2, BLOCK, W2), F32),
    ((2, BLOCK, W2), F32),
    ((2, 2, W2, W2), BF),
    ((2, 2, W2, W2), BF),
    ((2, 2, W2, W2), F32),
    ((2, 2, W2, W2), BF),
    ((2, 3, 2, 64, W2), BF),
    ((2, 2, 64, W2), BF),
    ((2, 4, 2, 16, W2), BF),
    ((2, 4, W2, W2), BF),
    ((2, NB, LOCAL, W2), F32),
    ((2, FAR, W2), F32),
    ((2, NB, BLOCK, W2), F32),
    ((2, 384, W2), BF),
    ((2, 384, W2), BF),
    ((2, 192, W2), BF),
    ((2, 192, W2), BF),
    ((8, 16, W2), BF),
    ((8, 16, W2), BF),
    ((ROWS, W2), BF),
    ((ROWS, W2), BF),
    ((2, ROWS, W2), BF),
]


RESULTS = [(ROWS, W2)] * 4 + [(W2, 2048)]


def move(*refs):
    srcs, dsts, bufs, sem_in, sem_out = refs[:5], refs[5:10], refs[10:15], refs[15], refs[16]
    ins, outs = [], []
    for src, dst, buf in zip(srcs, dsts, bufs):
        step = src.shape[0] // 2
        for i in range(2):
            piece = pl.ds(i * step, step)
            ins.append(pltpu.make_async_copy(src.at[piece], buf.at[piece], sem_in.at[len(ins)]))
            outs.append(pltpu.make_async_copy(buf.at[piece], dst.at[piece], sem_out.at[len(outs)]))
    for copy in ins:
        copy.start()
    for copy, out in zip(ins, outs):
        copy.wait()
        out.start()
    for copy in outs:
        copy.wait()


def body(queries, key_states, value_states, out_weight, cotangent):
    hbm = pl.BlockSpec(memory_space=pl.ANY)
    outs = tuple(jax.ShapeDtypeStruct(shape, BF) for shape in RESULTS)
    results = pl.pallas_call(
        kernel,
        out_shape=outs,
        in_specs=[hbm] * 5,
        out_specs=(hbm,) * 5,
        scratch_shapes=[pltpu.VMEM(shape, kind) for shape, kind in SCRATCH]
        + [pltpu.SemaphoreType.DMA((N_SEM,)), pltpu.SemaphoreType.DMA((N_SEM,)), pltpu.SemaphoreType.DMA((26,))],
        compiler_params=pltpu.CompilerParams(
            collective_id=0, has_side_effects=True, vmem_limit_bytes=60 * 1024 * 1024),
        name="attention",
    )(queries, key_states, value_states, out_weight, cotangent)
    return pl.pallas_call(
        move,
        out_shape=outs,
        in_specs=[hbm] * 5,
        out_specs=(hbm,) * 5,
        scratch_shapes=[pltpu.VMEM(shape, BF) for shape in RESULTS] + [pltpu.SemaphoreType.DMA((10,))] * 2,
        compiler_params=pltpu.CompilerParams(vmem_limit_bytes=60 * 1024 * 1024),
        name="results",
    )(*results)


def solution(mesh):
    return jax.shard_map(
        body,
        mesh=mesh,
        in_specs=(P("seq", "head"), P("seq", "head"), P("seq", "head"), P("head", None), P("seq", "head")),
        out_specs=(P("seq", "head"), P("seq", "head"), P("seq", "head"), P("seq", "head"), P("head", None)),
        check_vma=False,
    )
```

```python
import math

import jax
import jax.numpy as jnp
from jax import lax
from jax.experimental import pallas as pl
from jax.experimental.pallas import tpu as pltpu
from jax.sharding import PartitionSpec as P

BF = jnp.bfloat16
F32 = jnp.float32
HD = 128
BLOCK = 256
NB = 4
ROWS = NB * BLOCK
W2 = 256
LOCAL = 512
FAR = 640
SCALE = HD**-0.5
SCALE2 = SCALE * math.log2(math.e)

AG = 0
RELAY = 8
WZ = 12
WC = 16
KS = 20
KD = 23
MX = 38
GM = 42
RS1 = 46
RS2 = 50
GW = 58
GP = 86
GS = 87
GD = 88
N_SEM = 103


def dot_nt(a, b):
    return lax.dot_general(a, b, (((1,), (1,)), ((), ())), preferred_element_type=F32)


def dot_nn(a, b):
    return lax.dot_general(a, b, (((1,), (0,)), ((), ())), preferred_element_type=F32)


def dot_tn(a, b):
    return lax.dot_general(a, b, (((0,), (0,)), ((), ())), preferred_element_type=F32)


def pool_matrix(rows):
    r = lax.broadcasted_iota(jnp.int32, (rows // 2, rows), 0)
    c = lax.broadcasted_iota(jnp.int32, (rows // 2, rows), 1)
    return jnp.where((c == 2 * r) | (c == 2 * r + 1), 0.5, 0.0).astype(BF)


def pool(x):
    return dot_nn(pool_matrix(x.shape[0]), x).astype(BF)


def spread(x, factor):
    rows = x.shape[0]
    r = lax.broadcasted_iota(jnp.int32, (rows * factor, rows), 0)
    c = lax.broadcasted_iota(jnp.int32, (rows * factor, rows), 1)
    d = r - c * factor
    e = jnp.where((d >= 0) & (d < factor), 1.0 / factor, 0.0).astype(BF)
    high = x.astype(BF)
    low = (x - high.astype(F32)).astype(BF)
    return dot_nn(e, high) + dot_nn(e, low)


def kernel(q_hbm, k_hbm, v_hbm, w_hbm, c_hbm,
           att_hbm, gq_hbm, gk_hbm, gv_hbm, gw_hbm,
           q, kl, kf, c3, c4, c5, c6, c7, r7, cg, wt, mx, probs, tops, sums, outs,
           gmo, gmt, gms, gmr, rs_a, rs_ar, rs_b, rs_br, part0, part_r, part_l,
           gws, gwr, gwo, s1b, yr, s2b, zr, gwf,
           dkl, dkf, tok, gs_s, gs_r, ga_s, ga_r, gs7, gr7,
           oatt, ogq, ogk,
           ssem, rsem, lsem):
    seq = lax.axis_index("seq")
    head = lax.axis_index("head")
    core = lax.rem(seq, 2)
    y = lax.rem(seq // 2, 4)
    zh = seq // 8
    x = head // 2
    z = lax.rem(head, 2)
    oc = 1 - core
    oz = 1 - z

    def xor4(a, k):
        if k == 0:
            return a
        if k == 1:
            return a + 1 - 2 * lax.rem(a, 2)
        if k == 2:
            return lax.rem(a + 2, 4)
        return 3 - a

    xr = lax.rem(x + 1, 4)
    xl = lax.rem(x + 3, 4)
    xf = lax.rem(x + 2, 4)
    right = (seq, xr * 2 + z)
    left = (seq, xl * 2 + z)
    pair = (seq, x * 2 + oz)
    sib = (zh * 8 + y * 2 + oc, head)

    def chip(a, k):
        return (xor4(zh, a) * 8 + xor4(y, k) * 2 + core, head)

    yp = [chip(0, k) for k in (1, 2, 3)]
    zp = [chip(a, 0) for a in (1, 2, 3)]
    zp_pair = [(xor4(zh, k) * 8 + y * 2 + core, x * 2 + oz) for k in (1, 2, 3)]
    yk = [xor4(y, k) for k in (1, 2, 3)]
    zk = [xor4(zh, k) for k in (1, 2, 3)]
    far_chips = [chip(a, k) for a in (1, 2, 3) for k in range(4)]

    def rows_of(b):
        return pl.ds(pl.multiple_of(b * BLOCK, BLOCK), BLOCK)

    def rcopy(src, dst, slot, peer):
        return pltpu.make_async_remote_copy(
            src_ref=src, dst_ref=dst, send_sem=ssem.at[slot], recv_sem=rsem.at[slot],
            device_id=peer, device_id_type=pl.DeviceIdType.MESH)

    barrier = pltpu.get_barrier_semaphore()
    peers = [right, left, pair, sib] + yp + far_chips + zp_pair
    for peer in peers:
        pl.semaphore_signal(barrier, inc=1, device_id=peer, device_id_type=pl.DeviceIdType.MESH)

    loads = []
    for b in range(NB):
        loads.append(pltpu.make_async_copy(k_hbm.at[pl.ds(b * BLOCK, BLOCK)], kl.at[0, b, pl.ds(0, BLOCK)], lsem.at[2 * b]))
        loads.append(pltpu.make_async_copy(v_hbm.at[pl.ds(b * BLOCK, BLOCK)], kl.at[1, b, pl.ds(0, BLOCK)], lsem.at[2 * b + 1]))
    for copy in loads:
        copy.start()
    load_q = pltpu.make_async_copy(q_hbm, q, lsem.at[8])
    load_q.start()
    load_c = pltpu.make_async_copy(c_hbm, cg.at[x], lsem.at[9])
    load_c.start()
    zrow = pl.multiple_of(z * W2, W2)
    ozrow = pl.multiple_of(oz * W2, W2)
    load_w = [
        pltpu.make_async_copy(
            w_hbm.at[:, pl.ds(pl.multiple_of(512 * s + W2 * z, W2), W2)], wt.at[s, pl.ds(zrow, W2)], lsem.at[10 + s])
        for s in range(4)]
    for copy in load_w:
        copy.start()

    for copy in loads:
        copy.wait()
    last = []
    for t in range(2):
        c2 = []
        for b in range(NB):
            p1 = pool(kl[t, b, 0:BLOCK, :])
            kl[t, b ^ 1, 256:384, :] = p1
            c2.append(pool(p1))
        p3 = []
        for p in range(2):
            both = jnp.concatenate([c2[2 * p], c2[2 * p + 1]], axis=0)
            kl[t, 2 - 2 * p, 384:512, :] = both
            kl[t, 3 - 2 * p, 384:512, :] = both
            p3.append(pool(both))
        p3 = jnp.concatenate(p3, axis=0)
        p4 = pool(p3)
        p5 = pool(p4)
        p6 = pool(p5)
        c3[t] = p3
        c4[t] = p4
        c5[t] = p5
        c6[t] = p6
        last.append(dot_nn(pool_matrix(16), p6))
    c7[...] = jnp.concatenate(last, axis=0).astype(BF)

    pl.semaphore_wait(barrier, len(peers))

    ks_own = rcopy(c3, kf.at[:, pl.ds(0, 128)], KS, sib)
    ks_own.start()
    kd_y = [rcopy(c4, kf.at[:, pl.ds(128, 64)], KD, yp[0]),
            rcopy(c5, kf.at[:, pl.ds(192, 32)], KD + 1, yp[1]),
            rcopy(c5, kf.at[:, pl.ds(224, 32)], KD + 2, yp[2])]
    kd_6 = [rcopy(c6, kf.at[:, pl.ds(256 + 16 * i, 16)], KD + 3 + i, far_chips[i]) for i in range(4)]
    kd_7 = [rcopy(c7, r7.at[i], KD + 7 + i, far_chips[4 + i]) for i in range(8)]
    for copy in kd_6 + kd_7 + kd_y:
        copy.start()

    ag_r = []
    ag_l = []
    for b in range(NB):
        rb = pl.ds(b * BLOCK, BLOCK)
        ag_r.append(rcopy(c_hbm.at[rb], cg.at[x, rb], AG + b, right))
        ag_l.append(rcopy(c_hbm.at[rb], cg.at[x, rb], AG + 4 + b, left))
    for b in range(NB):
        ag_r[b].start()
        ag_l[3 - b].start()
    crow = pl.multiple_of(core * 128, 128)
    wz = [
        rcopy(w_hbm.at[pl.ds(crow, 128), pl.ds(pl.multiple_of(512 * s + W2 * oz, W2), W2)],
              wt.at[s, pl.ds(pl.multiple_of(zrow + crow, 128), 128)], WZ + s, pair)
        for s in range(4)]
    for copy in wz:
        copy.start()

    load_q.wait()

    @pl.loop(0, NB)
    def _(b):
        for h in range(2):
            hs = slice(h * HD, h * HD + HD)
            s_l = dot_nt(q[rows_of(b), hs], kl[0, b, :, hs])
            top = jnp.max(s_l, axis=1, keepdims=True)
            e_l = jnp.exp2((s_l - top) * SCALE2)
            probs[b, h, :, 0:LOCAL] = e_l
            tops[b, h] = top
            sums[b, h] = jnp.sum(e_l, axis=1, keepdims=True)
            outs[b, :, hs] = dot_nn(e_l.astype(BF), kl[1, b, :, hs])

    for copy in kd_y:
        copy.wait_recv()
    ks_y = rcopy(kf.at[:, pl.ds(128, 128)], kf.at[:, pl.ds(384, 128)], KS + 1, sib)
    ks_y.start()
    relay_r = []
    relay_l = []
    for i in range(2):
        rb = pl.ds(i * BLOCK, BLOCK)
        rc = pl.ds((i + 2) * BLOCK, BLOCK)
        relay_r.append(rcopy(cg.at[xl, rb], cg.at[xl, rb], RELAY + i, right))
        relay_l.append(rcopy(cg.at[xr, rc], cg.at[xr, rc], RELAY + 2 + i, left))
    ag_r[0].wait_recv()
    relay_r[0].start()
    ag_l[3].wait_recv()
    relay_l[1].start()
    for copy in kd_6 + kd_7:
        copy.wait_recv()
    wide = r7[...].astype(F32)
    for t in range(2):
        kf[t, 320:384, :] = wide[:, 8 * t:8 * t + 8, :].reshape(64, W2).astype(BF)
    ks_z = rcopy(kf.at[:, pl.ds(256, 128)], kf.at[:, pl.ds(512, 128)], KS + 2, sib)
    ks_z.start()
    wc = []
    for s in range(4):
        piece = wt.at[s, pl.ds(pl.multiple_of(ozrow + crow, 128), 128)]
        wc.append(rcopy(piece, piece, WC + s, sib))
    for copy in (ks_own, ks_y, ks_z):
        copy.wait_recv()

    def mx_copy(b):
        rb = rows_of(b)
        return rcopy(mx.at[z, rb], mx.at[z, rb], MX + b, pair)

    @pl.loop(0, NB)
    def _(b):
        rb = rows_of(b)
        for h in range(2):
            hs = slice(h * HD, h * HD + HD)
            qh = q[rb, hs]
            s_f = dot_nt(qh, kf[0, :, hs])
            top_l = tops[b, h]
            top = jnp.maximum(top_l, jnp.max(s_f, axis=1, keepdims=True))
            e_f = jnp.exp2((s_f - top) * SCALE2)
            scale_l = jnp.exp2((top_l - top) * SCALE2)
            inv = 1.0 / (sums[b, h] * scale_l + jnp.sum(e_f, axis=1, keepdims=True))
            scale_l = scale_l * inv
            probs[b, h, :, 0:LOCAL] = probs[b, h, :, 0:LOCAL] * scale_l
            p_f = e_f * inv
            probs[b, h, :, LOCAL:] = p_f
            out = outs[b, :, hs] * scale_l + dot_nn(p_f.astype(BF), kf[1, :, hs])
            mx[z, rb, hs] = out.astype(BF)
        mx_copy(b).start()

        @pl.when(b == 0)
        def _():
            ag_r[1].wait_recv()
            relay_r[1].start()
            ag_l[2].wait_recv()
            relay_l[0].start()

        @pl.when(b == 1)
        def _():
            for s in range(4):
                wz[s].wait_recv()
                wc[s].start()

    load_c.wait()
    for copy in load_w:
        copy.wait()
    for copy in wc:
        copy.wait_recv()
    for i in range(2):
        ag_r[2 + i].wait_recv()
        ag_l[i].wait_recv()

    def gm_copy(b):
        return rcopy(gms.at[b], gmr.at[b], GM + b, pair)

    def gm_part(s, b, side):
        return dot_nt(cg[s, rows_of(b), :], wt[s, pl.ds(side, W2), :])

    @pl.loop(0, NB)
    def _(b):
        gmt[b] = gm_part(x, b, ozrow) + gm_part(xl, b, ozrow) + gm_part(xr, b, ozrow)
        gmo[b] = gm_part(x, b, zrow) + gm_part(xl, b, zrow) + gm_part(xr, b, zrow)

    for i in range(2):
        relay_r[i].wait_recv()
        relay_l[i].wait_recv()

    @pl.loop(0, NB)
    def _(b):
        gms[b] = (gmt[b] + gm_part(xf, b, ozrow)).astype(BF)
        gm_copy(b).start()

    row_y = pl.multiple_of(64 * y, 64)
    row_z = pl.multiple_of(64 * y + 16 * zh, 16)
    own_cols = pl.ds(2 * core, 2)
    gw_core, gw_y, gw_z, gw_zg, gw_yg, gw_cg = [], [], [], [], [], []
    for i in range(2):
        base = GW + 14 * i
        side = z if i == 0 else oz
        gw_core.append(rcopy(gws.at[i], gwr.at[i], base, sib))
        gw_y.append([rcopy(s1b.at[i, :, pl.ds(pl.multiple_of(64 * yk[k], 64), 64)], yr.at[i, k], base + 1 + k, yp[k])
                     for k in range(3)])
        to = zp if i == 0 else zp_pair
        gw_z.append([rcopy(s2b.at[i, :, pl.ds(pl.multiple_of(16 * zk[k], 16), 16)], zr.at[i, k], base + 4 + k, to[k])
                     for k in range(3)])
        piece = gwf.at[side, own_cols, pl.ds(row_z, 16)]
        gw_zg.append([rcopy(piece, piece, base + 7 + k, zp[k]) for k in range(3)])
        piece = gwf.at[side, own_cols, pl.ds(row_y, 64)]
        gw_yg.append([rcopy(piece, piece, base + 10 + k, yp[k]) for k in range(3)])
        piece = gwf.at[side, own_cols]
        gw_cg.append(rcopy(piece, piece, base + 13, sib))
    gw_z[1].append(rcopy(s2b.at[1, :, pl.ds(pl.multiple_of(16 * zh, 16), 16)], zr.at[1, 3], GP, pair))

    def tile(i, side):
        @pl.loop(0, 2)
        def _(j):
            gws[i, j] = dot_tn(mx[side], cg[2 * oc + j]).astype(BF)
        gw_core[i].start()

        @pl.loop(0, 2)
        def _(j):
            gwo[i, j] = dot_tn(mx[side], cg[2 * core + j])

    def after_core(i):
        gw_core[i].wait_recv()
        total = gwo[i] + gwr[i].astype(F32)
        gwo[i] = total
        s1b[i] = total.astype(BF)
        for copy in gw_y[i]:
            copy.start()

    def after_y(i):
        for copy in gw_y[i]:
            copy.wait_recv()
        total = gwo[i, :, pl.ds(row_y, 64), :]
        for k in range(3):
            total += yr[i, k].astype(F32)
        gwo[i, :, pl.ds(row_y, 64), :] = total
        s2b[i] = total.astype(BF)
        for copy in gw_z[i]:
            copy.start()

    def after_z(i):
        for copy in gw_z[i]:
            copy.wait_recv()
        if i == 0:
            total = gwo[0, :, pl.ds(row_z, 16), :]
        else:
            total = zr[1, 3].astype(F32)
        for k in range(3):
            total += zr[i, k].astype(F32)
        gwf[z if i == 0 else oz, own_cols, pl.ds(row_z, 16), :] = total.astype(BF)
        for copy in gw_zg[i]:
            copy.start()

    def after_zg(i):
        for copy in gw_zg[i]:
            copy.wait_recv()
        for copy in gw_yg[i]:
            copy.start()

    def after_yg(i):
        for copy in gw_yg[i]:
            copy.wait_recv()
        gw_cg[i].start()

    def out_w(i, s):
        side = z if i == 0 else oz
        return pltpu.make_async_copy(
            gwf.at[side, s], gw_hbm.at[:, pl.ds(pl.multiple_of(512 * s + W2 * side, W2), W2)], lsem.at[18 + 4 * i + s])

    def after_cg(i):
        gw_cg[i].wait_recv()
        for s in range(4):
            out_w(i, s).start()

    tile(0, z)

    for b in range(NB):
        mx_copy(b).wait_recv()

    def partial(s, b):
        rb = rows_of(b)
        return dot_nn(mx[0, rb, :], wt[s, 0:W2, :]) + dot_nn(mx[1, rb, :], wt[s, W2:2 * W2, :])

    rs1_r = [rcopy(rs_a.at[i], rs_ar.at[i], RS1 + i, right) for i in range(2)]
    rs1_l = [rcopy(rs_a.at[2 + i], rs_ar.at[2 + i], RS1 + 2 + i, left) for i in range(2)]

    @pl.loop(0, NB)
    def _(b):
        rs_a[b] = partial(xf, b).astype(BF)

    for i in range(2):
        rs1_r[i].start()
        rs1_l[i].start()
    rs2_r = [rcopy(rs_b.at[0, b], rs_br.at[0, b], RS2 + b, right) for b in range(NB)]
    rs2_l = [rcopy(rs_b.at[1, b], rs_br.at[1, b], RS2 + 4 + b, left) for b in range(NB)]

    after_core(0)
    tile(1, oz)

    @pl.loop(0, 2)
    def _(i):
        rs_b[0, 2 + i] = partial(xr, 2 + i).astype(BF)
        rs_b[1, i] = partial(xl, i).astype(BF)

    for i in range(2):
        rs2_r[2 + i].start()
        rs2_l[i].start()
    after_core(1)

    @pl.loop(0, 2)
    def _(i):
        part_r[i] = partial(xr, i)
        part_l[i] = partial(xl, 2 + i)

    @pl.loop(0, NB)
    def _(b):
        gmo[b] += gm_part(xf, b, zrow)

    after_y(0)

    dkf[...] = jnp.zeros_like(dkf)

    @pl.loop(0, NB)
    def _(b):
        rb = rows_of(b)
        gm_copy(b).wait_recv()
        for h in range(2):
            hs = slice(h * HD, h * HD + HD)
            do = (gmo[b, :, hs] + gmr[b, :, hs].astype(F32)).astype(BF)
            qh = q[rb, hs]
            p_l = probs[b, h, :, 0:LOCAL]
            p_f = probs[b, h, :, LOCAL:]
            dp_l = dot_nt(do, kl[1, b, :, hs])
            dp_f = dot_nt(do, kf[1, :, hs])
            inner = jnp.sum(p_l * dp_l, axis=1, keepdims=True) + jnp.sum(p_f * dp_f, axis=1, keepdims=True)
            ds_l = (p_l * (dp_l - inner)).astype(BF)
            ds_f = (p_f * (dp_f - inner)).astype(BF)
            dq = dot_nn(ds_l, kl[0, b, :, hs]) + dot_nn(ds_f, kf[0, :, hs])
            ogq[rb, hs] = (dq * SCALE).astype(BF)
            dkf[0, :, hs] += dot_tn(ds_f, qh) * SCALE
            dkf[1, :, hs] += dot_tn(p_f.astype(BF), do)
            dkl[0, b, :, hs] = dot_tn(ds_l, qh) * SCALE
            dkl[1, b, :, hs] = dot_tn(p_l.astype(BF), do)

        @pl.when(b == 0)
        def _():
            after_y(1)
            for i in range(2):
                rs1_r[i].wait_recv()
                rs1_l[i].wait_recv()
                rs_b[0, i] = (part_r[i] + rs_ar[i].astype(F32)).astype(BF)
                rs_b[1, 2 + i] = (part_l[i] + rs_ar[2 + i].astype(F32)).astype(BF)
                rs2_r[i].start()
                rs2_l[2 + i].start()


        @pl.when(b == 2)
        def _():
            after_z(0)

    gs_s[:, 0:128, :] = dkf[:, 0:128, :].astype(BF)
    gs_s[:, 128:384, :] = dkf[:, 384:640, :].astype(BF)
    gk_s = rcopy(gs_s, gs_r, GS, sib)
    gk_s.start()
    out_q = pltpu.make_async_copy(ogq, gq_hbm, lsem.at[14])
    out_q.start()
    after_z(1)

    @pl.loop(0, NB)
    def _(b):
        part0[b] = partial(x, b)

    after_zg(0)

    gk_s.wait_recv()
    parts7 = []
    for t in range(2):
        total = dkf[t, 128:384, :] + gs_r[t, 128:384, :].astype(F32)
        ga_s[t] = total[0:192, :].astype(BF)
        parts7.append(total[192:256, :].reshape(8, 8, W2))
    gs7[...] = jnp.concatenate(parts7, axis=1).astype(BF)
    gk_d = [rcopy(ga_s.at[:, pl.ds(0, 64)], ga_r.at[:, pl.ds(0, 64)], GD, yp[0]),
            rcopy(ga_s.at[:, pl.ds(64, 32)], ga_r.at[:, pl.ds(64, 32)], GD + 1, yp[1]),
            rcopy(ga_s.at[:, pl.ds(96, 32)], ga_r.at[:, pl.ds(96, 32)], GD + 2, yp[2])]
    gk_d += [rcopy(ga_s.at[:, pl.ds(128 + 16 * i, 16)], ga_r.at[:, pl.ds(128 + 16 * i, 16)], GD + 3 + i, far_chips[i])
             for i in range(4)]
    gk_d += [rcopy(gs7.at[i], gr7.at[i], GD + 7 + i, far_chips[4 + i]) for i in range(8)]
    for copy in gk_d:
        copy.start()

    for t in range(2):
        for p in range(2):
            g2 = dkl[t, 2 - 2 * p, 384:512, :] + dkl[t, 3 - 2 * p, 384:512, :]
            for i in range(2):
                b = 2 * p + i
                g1 = dkl[t, b ^ 1, 256:384, :] + spread(g2[64 * i:64 * i + 64, :], 2)
                tok[t, b] = dkl[t, b, 0:BLOCK, :] + spread(g1, 2)
    after_zg(1)

    for b in range(NB):
        rs2_r[b].wait_recv()
        rs2_l[b].wait_recv()
        oatt[pl.ds(b * BLOCK, BLOCK), :] = (
            part0[b] + rs_br[0, b].astype(F32) + rs_br[1, b].astype(F32)).astype(BF)
    out_att = pltpu.make_async_copy(oatt, att_hbm, lsem.at[15])
    out_att.start()
    for copy in (ag_r + ag_l + relay_r + relay_l + wz + wc + [ks_own, ks_y, ks_z] + kd_y + kd_6 + kd_7
                 + [mx_copy(b) for b in range(NB)] + [gm_copy(b) for b in range(NB)]
                 + rs1_r + rs1_l + rs2_r + rs2_l
                 + gw_core + gw_y[0] + gw_y[1] + gw_z[0] + gw_z[1] + [gk_s]):
        copy.wait_send()
    after_yg(0)

    for copy in gk_d:
        copy.wait_recv()
    g7 = jnp.sum(gr7[...].astype(F32), axis=0)
    for t in range(2):
        g6 = spread(g7[8 * t:8 * t + 8, :], 2)
        for i in range(4):
            g6 += ga_r[t, 128 + 16 * i:144 + 16 * i, :].astype(F32)
        g5 = ga_r[t, 64:96, :].astype(F32) + ga_r[t, 96:128, :].astype(F32) + spread(g6, 2)
        g4 = ga_r[t, 0:64, :].astype(F32) + spread(g5, 2)
        g3 = gs_r[t, 0:128, :].astype(F32) + spread(g4, 2)
        for b in range(NB):
            ogk[t, pl.ds(b * BLOCK, BLOCK), :] = (tok[t, b] + spread(g3[32 * b:32 * b + 32, :], 8)).astype(BF)
    out_k = pltpu.make_async_copy(ogk.at[0], gk_hbm, lsem.at[16])
    out_v = pltpu.make_async_copy(ogk.at[1], gv_hbm, lsem.at[17])
    out_k.start()
    out_v.start()

    after_cg(0)
    after_yg(1)
    after_cg(1)

    for copy in gw_zg[0] + gw_zg[1] + gw_yg[0] + gw_yg[1] + gw_cg + gk_d:
        copy.wait_send()
    for copy in [out_q, out_att, out_k, out_v] + [out_w(i, s) for i in range(2) for s in range(4)]:
        copy.wait()


SCRATCH = [
    ((ROWS, W2), BF),
    ((2, NB, LOCAL, W2), BF),
    ((2, FAR, W2), BF),
    ((2, 128, W2), BF),
    ((2, 64, W2), BF),
    ((2, 32, W2), BF),
    ((2, 16, W2), BF),
    ((16, W2), BF),
    ((8, 16, W2), BF),
    ((4, ROWS, W2), BF),
    ((4, 2 * W2, W2), BF),
    ((2, ROWS, W2), BF),
    ((NB, 2, BLOCK, LOCAL + FAR), F32),
    ((NB, 2, BLOCK, 1), F32),
    ((NB, 2, BLOCK, 1), F32),
    ((NB, BLOCK, W2), F32),
    ((NB, BLOCK, W2), F32),
    ((NB, BLOCK, W2), F32),
    ((NB, BLOCK, W2), BF),
    ((NB, BLOCK, W2), BF),
    ((NB, BLOCK, W2), BF),
    ((NB, BLOCK, W2), BF),
    ((2, NB, BLOCK, W2), BF),
    ((2, NB, BLOCK, W2), BF),
    ((NB, BLOCK, W2), F32),
    ((2, BLOCK, W2), F32),
    ((2, BLOCK, W2), F32),
    ((2, 2, W2, W2), BF),
    ((2, 2, W2, W2), BF),
    ((2, 2, W2, W2), F32),
    ((2, 2, W2, W2), BF),
    ((2, 3, 2, 64, W2), BF),
    ((2, 2, 64, W2), BF),
    ((2, 4, 2, 16, W2), BF),
    ((2, 4, W2, W2), BF),
    ((2, NB, LOCAL, W2), F32),
    ((2, FAR, W2), F32),
    ((2, NB, BLOCK, W2), F32),
    ((2, 384, W2), BF),
    ((2, 384, W2), BF),
    ((2, 192, W2), BF),
    ((2, 192, W2), BF),
    ((8, 16, W2), BF),
    ((8, 16, W2), BF),
    ((ROWS, W2), BF),
    ((ROWS, W2), BF),
    ((2, ROWS, W2), BF),
]


RESULTS = [(ROWS, W2)] * 4 + [(W2, 2048)]


def move(*refs):
    srcs, dsts, bufs, sem_in, sem_out = refs[:5], refs[5:10], refs[10:15], refs[15], refs[16]
    ins, outs = [], []
    for src, dst, buf in zip(srcs, dsts, bufs):
        step = src.shape[0] // 2
        for i in range(2):
            piece = pl.ds(i * step, step)
            ins.append(pltpu.make_async_copy(src.at[piece], buf.at[piece], sem_in.at[len(ins)]))
            outs.append(pltpu.make_async_copy(buf.at[piece], dst.at[piece], sem_out.at[len(outs)]))
    for copy in ins:
        copy.start()
    for copy, out in zip(ins, outs):
        copy.wait()
        out.start()
    for copy in outs:
        copy.wait()


def body(queries, key_states, value_states, out_weight, cotangent):
    hbm = pl.BlockSpec(memory_space=pl.ANY)
    outs = tuple(jax.ShapeDtypeStruct(shape, BF) for shape in RESULTS)
    results = pl.pallas_call(
        kernel,
        out_shape=outs,
        in_specs=[hbm] * 5,
        out_specs=(hbm,) * 5,
        scratch_shapes=[pltpu.VMEM(shape, kind) for shape, kind in SCRATCH]
        + [pltpu.SemaphoreType.DMA((N_SEM,)), pltpu.SemaphoreType.DMA((N_SEM,)), pltpu.SemaphoreType.DMA((26,))],
        compiler_params=pltpu.CompilerParams(
            collective_id=0, has_side_effects=True, vmem_limit_bytes=60 * 1024 * 1024),
        name="attention",
    )(queries, key_states, value_states, out_weight, cotangent)
    return pl.pallas_call(
        move,
        out_shape=outs,
        in_specs=[hbm] * 5,
        out_specs=(hbm,) * 5,
        scratch_shapes=[pltpu.VMEM(shape, BF) for shape in RESULTS] + [pltpu.SemaphoreType.DMA((10,))] * 2,
        compiler_params=pltpu.CompilerParams(vmem_limit_bytes=60 * 1024 * 1024),
        name="results",
    )(*results)


def solution(mesh):
    return jax.shard_map(
        body,
        mesh=mesh,
        in_specs=(P("seq", "head"), P("seq", "head"), P("seq", "head"), P("head", None), P("seq", "head")),
        out_specs=(P("seq", "head"), P("seq", "head"), P("seq", "head"), P("seq", "head"), P("head", None)),
        check_vma=False,
    )
```

```python
import math

import jax
import jax.numpy as jnp
from jax import lax
from jax.experimental import pallas as pl
from jax.experimental.pallas import tpu as pltpu
from jax.sharding import PartitionSpec as P

BF = jnp.bfloat16
F32 = jnp.float32
HD = 128
BLOCK = 256
NB = 4
ROWS = NB * BLOCK
W2 = 256
LOCAL = 512
FAR = 640
SCALE = HD**-0.5
SCALE2 = SCALE * math.log2(math.e)

AG = 0
RELAY = 8
WZ = 12
WC = 16
KS = 20
KD = 23
MX = 38
GM = 42
RS1 = 46
RS2 = 50
GW = 58
GP = 86
GS = 87
GD = 88
N_SEM = 103


def dot_nt(a, b):
    return lax.dot_general(a, b, (((1,), (1,)), ((), ())), preferred_element_type=F32)


def dot_nn(a, b):
    return lax.dot_general(a, b, (((1,), (0,)), ((), ())), preferred_element_type=F32)


def dot_tn(a, b):
    return lax.dot_general(a, b, (((0,), (0,)), ((), ())), preferred_element_type=F32)


def pool_matrix(rows):
    r = lax.broadcasted_iota(jnp.int32, (rows // 2, rows), 0)
    c = lax.broadcasted_iota(jnp.int32, (rows // 2, rows), 1)
    return jnp.where((c == 2 * r) | (c == 2 * r + 1), 0.5, 0.0).astype(BF)


def pool(x):
    return dot_nn(pool_matrix(x.shape[0]), x).astype(BF)


def spread(x, factor):
    rows = x.shape[0]
    r = lax.broadcasted_iota(jnp.int32, (rows * factor, rows), 0)
    c = lax.broadcasted_iota(jnp.int32, (rows * factor, rows), 1)
    d = r - c * factor
    e = jnp.where((d >= 0) & (d < factor), 1.0 / factor, 0.0).astype(BF)
    high = x.astype(BF)
    low = (x - high.astype(F32)).astype(BF)
    return dot_nn(e, high) + dot_nn(e, low)


def kernel(q_hbm, k_hbm, v_hbm, w_hbm, c_hbm,
           att_hbm, gq_hbm, gk_hbm, gv_hbm, gw_hbm,
           q, kl, kf, c3, c4, c5, c6, c7, r7, cg, wt, mx, probs,
           gmo, gmt, gms, gmr, rs_a, rs_ar, rs_b, rs_br, part0, part_r, part_l,
           gws, gwr, gwo, s1b, yr, s2b, zr, gwf,
           dkl, dkf, tok, gs_s, gs_r, ga_s, ga_r, gs7, gr7,
           oatt, ogq, ogk,
           ssem, rsem, lsem):
    seq = lax.axis_index("seq")
    head = lax.axis_index("head")
    core = lax.rem(seq, 2)
    y = lax.rem(seq // 2, 4)
    zh = seq // 8
    x = head // 2
    z = lax.rem(head, 2)
    oc = 1 - core
    oz = 1 - z

    def xor4(a, k):
        if k == 0:
            return a
        if k == 1:
            return a + 1 - 2 * lax.rem(a, 2)
        if k == 2:
            return lax.rem(a + 2, 4)
        return 3 - a

    xr = lax.rem(x + 1, 4)
    xl = lax.rem(x + 3, 4)
    xf = lax.rem(x + 2, 4)
    right = (seq, xr * 2 + z)
    left = (seq, xl * 2 + z)
    pair = (seq, x * 2 + oz)
    sib = (zh * 8 + y * 2 + oc, head)

    def chip(a, k):
        return (xor4(zh, a) * 8 + xor4(y, k) * 2 + core, head)

    yp = [chip(0, k) for k in (1, 2, 3)]
    zp = [chip(a, 0) for a in (1, 2, 3)]
    zp_pair = [(xor4(zh, k) * 8 + y * 2 + core, x * 2 + oz) for k in (1, 2, 3)]
    yk = [xor4(y, k) for k in (1, 2, 3)]
    zk = [xor4(zh, k) for k in (1, 2, 3)]
    far_chips = [chip(a, k) for a in (1, 2, 3) for k in range(4)]

    def rows_of(b):
        return pl.ds(pl.multiple_of(b * BLOCK, BLOCK), BLOCK)

    def rcopy(src, dst, slot, peer):
        return pltpu.make_async_remote_copy(
            src_ref=src, dst_ref=dst, send_sem=ssem.at[slot], recv_sem=rsem.at[slot],
            device_id=peer, device_id_type=pl.DeviceIdType.MESH)

    barrier = pltpu.get_barrier_semaphore()
    peers = [right, left, pair, sib] + yp + far_chips + zp_pair
    for peer in peers:
        pl.semaphore_signal(barrier, inc=1, device_id=peer, device_id_type=pl.DeviceIdType.MESH)

    loads = []
    for b in range(NB):
        loads.append(pltpu.make_async_copy(k_hbm.at[pl.ds(b * BLOCK, BLOCK)], kl.at[0, b, pl.ds(0, BLOCK)], lsem.at[2 * b]))
        loads.append(pltpu.make_async_copy(v_hbm.at[pl.ds(b * BLOCK, BLOCK)], kl.at[1, b, pl.ds(0, BLOCK)], lsem.at[2 * b + 1]))
    for copy in loads:
        copy.start()
    load_q = pltpu.make_async_copy(q_hbm, q, lsem.at[8])
    load_q.start()
    load_c = pltpu.make_async_copy(c_hbm, cg.at[x], lsem.at[9])
    load_c.start()
    zrow = pl.multiple_of(z * W2, W2)
    ozrow = pl.multiple_of(oz * W2, W2)
    load_w = [
        pltpu.make_async_copy(
            w_hbm.at[:, pl.ds(pl.multiple_of(512 * s + W2 * z, W2), W2)], wt.at[s, pl.ds(zrow, W2)], lsem.at[10 + s])
        for s in range(4)]
    for copy in load_w:
        copy.start()

    for copy in loads:
        copy.wait()
    last = []
    for t in range(2):
        c2 = []
        for b in range(NB):
            p1 = pool(kl[t, b, 0:BLOCK, :])
            kl[t, b ^ 1, 256:384, :] = p1
            c2.append(pool(p1))
        p3 = []
        for p in range(2):
            both = jnp.concatenate([c2[2 * p], c2[2 * p + 1]], axis=0)
            kl[t, 2 - 2 * p, 384:512, :] = both
            kl[t, 3 - 2 * p, 384:512, :] = both
            p3.append(pool(both))
        p3 = jnp.concatenate(p3, axis=0)
        p4 = pool(p3)
        p5 = pool(p4)
        p6 = pool(p5)
        c3[t] = p3
        c4[t] = p4
        c5[t] = p5
        c6[t] = p6
        last.append(dot_nn(pool_matrix(16), p6))
    c7[...] = jnp.concatenate(last, axis=0).astype(BF)

    pl.semaphore_wait(barrier, len(peers))

    ks_own = rcopy(c3, kf.at[:, pl.ds(0, 128)], KS, sib)
    ks_own.start()
    kd_y = [rcopy(c4, kf.at[:, pl.ds(128, 64)], KD, yp[0]),
            rcopy(c5, kf.at[:, pl.ds(192, 32)], KD + 1, yp[1]),
            rcopy(c5, kf.at[:, pl.ds(224, 32)], KD + 2, yp[2])]
    kd_6 = [rcopy(c6, kf.at[:, pl.ds(256 + 16 * i, 16)], KD + 3 + i, far_chips[i]) for i in range(4)]
    kd_7 = [rcopy(c7, r7.at[i], KD + 7 + i, far_chips[4 + i]) for i in range(8)]
    for copy in kd_6 + kd_7 + kd_y:
        copy.start()

    ag_r = []
    ag_l = []
    for b in range(NB):
        rb = pl.ds(b * BLOCK, BLOCK)
        ag_r.append(rcopy(c_hbm.at[rb], cg.at[x, rb], AG + b, right))
        ag_l.append(rcopy(c_hbm.at[rb], cg.at[x, rb], AG + 4 + b, left))
    for b in range(NB):
        ag_r[b].start()
        ag_l[3 - b].start()
    crow = pl.multiple_of(core * 128, 128)
    wz = [
        rcopy(w_hbm.at[pl.ds(crow, 128), pl.ds(pl.multiple_of(512 * s + W2 * oz, W2), W2)],
              wt.at[s, pl.ds(pl.multiple_of(zrow + crow, 128), 128)], WZ + s, pair)
        for s in range(4)]
    for copy in wz:
        copy.start()

    load_q.wait()

    @pl.loop(0, NB)
    def _(b):
        for h in range(2):
            hs = slice(h * HD, h * HD + HD)
            probs[b, h, :, 0:LOCAL] = dot_nt(q[rows_of(b), hs], kl[0, b, :, hs])

    for copy in kd_y:
        copy.wait_recv()
    ks_y = rcopy(kf.at[:, pl.ds(128, 128)], kf.at[:, pl.ds(384, 128)], KS + 1, sib)
    ks_y.start()
    relay_r = []
    relay_l = []
    for i in range(2):
        rb = pl.ds(i * BLOCK, BLOCK)
        rc = pl.ds((i + 2) * BLOCK, BLOCK)
        relay_r.append(rcopy(cg.at[xl, rb], cg.at[xl, rb], RELAY + i, right))
        relay_l.append(rcopy(cg.at[xr, rc], cg.at[xr, rc], RELAY + 2 + i, left))
    ag_r[0].wait_recv()
    relay_r[0].start()
    ag_l[3].wait_recv()
    relay_l[1].start()
    for copy in kd_6 + kd_7:
        copy.wait_recv()
    wide = r7[...].astype(F32)
    for t in range(2):
        kf[t, 320:384, :] = wide[:, 8 * t:8 * t + 8, :].reshape(64, W2).astype(BF)
    ks_z = rcopy(kf.at[:, pl.ds(256, 128)], kf.at[:, pl.ds(512, 128)], KS + 2, sib)
    ks_z.start()
    wc = []
    for s in range(4):
        piece = wt.at[s, pl.ds(pl.multiple_of(ozrow + crow, 128), 128)]
        wc.append(rcopy(piece, piece, WC + s, sib))
    for copy in (ks_own, ks_y, ks_z):
        copy.wait_recv()

    def mx_copy(b):
        rb = rows_of(b)
        return rcopy(mx.at[z, rb], mx.at[z, rb], MX + b, pair)

    @pl.loop(0, NB)
    def _(b):
        rb = rows_of(b)
        for h in range(2):
            hs = slice(h * HD, h * HD + HD)
            qh = q[rb, hs]
            s_l = probs[b, h, :, 0:LOCAL]
            s_f = dot_nt(qh, kf[0, :, hs])
            top = jnp.maximum(jnp.max(s_l, axis=1, keepdims=True), jnp.max(s_f, axis=1, keepdims=True))
            e_l = jnp.exp2((s_l - top) * SCALE2)
            e_f = jnp.exp2((s_f - top) * SCALE2)
            total = jnp.sum(e_l, axis=1, keepdims=True) + jnp.sum(e_f, axis=1, keepdims=True)
            inv = 1.0 / total
            p_l = e_l * inv
            p_f = e_f * inv
            probs[b, h, :, 0:LOCAL] = p_l
            probs[b, h, :, LOCAL:] = p_f
            out = dot_nn(p_l.astype(BF), kl[1, b, :, hs]) + dot_nn(p_f.astype(BF), kf[1, :, hs])
            mx[z, rb, hs] = out.astype(BF)
        mx_copy(b).start()

        @pl.when(b == 0)
        def _():
            ag_r[1].wait_recv()
            relay_r[1].start()
            ag_l[2].wait_recv()
            relay_l[0].start()

        @pl.when(b == 1)
        def _():
            for s in range(4):
                wz[s].wait_recv()
                wc[s].start()

    load_c.wait()
    for copy in load_w:
        copy.wait()
    for copy in wc:
        copy.wait_recv()
    for i in range(2):
        ag_r[2 + i].wait_recv()
        ag_l[i].wait_recv()

    def gm_copy(b):
        return rcopy(gms.at[b], gmr.at[b], GM + b, pair)

    def gm_part(s, b, side):
        return dot_nt(cg[s, rows_of(b), :], wt[s, pl.ds(side, W2), :])

    @pl.loop(0, NB)
    def _(b):
        gmt[b] = gm_part(x, b, ozrow) + gm_part(xl, b, ozrow) + gm_part(xr, b, ozrow)
        gmo[b] = gm_part(x, b, zrow) + gm_part(xl, b, zrow) + gm_part(xr, b, zrow)

    for i in range(2):
        relay_r[i].wait_recv()
        relay_l[i].wait_recv()

    @pl.loop(0, NB)
    def _(b):
        gms[b] = (gmt[b] + gm_part(xf, b, ozrow)).astype(BF)
        gm_copy(b).start()

    row_y = pl.multiple_of(64 * y, 64)
    row_z = pl.multiple_of(64 * y + 16 * zh, 16)
    own_cols = pl.ds(2 * core, 2)
    gw_core, gw_y, gw_z, gw_zg, gw_yg, gw_cg = [], [], [], [], [], []
    for i in range(2):
        base = GW + 14 * i
        side = z if i == 0 else oz
        gw_core.append(rcopy(gws.at[i], gwr.at[i], base, sib))
        gw_y.append([rcopy(s1b.at[i, :, pl.ds(pl.multiple_of(64 * yk[k], 64), 64)], yr.at[i, k], base + 1 + k, yp[k])
                     for k in range(3)])
        to = zp if i == 0 else zp_pair
        gw_z.append([rcopy(s2b.at[i, :, pl.ds(pl.multiple_of(16 * zk[k], 16), 16)], zr.at[i, k], base + 4 + k, to[k])
                     for k in range(3)])
        piece = gwf.at[side, own_cols, pl.ds(row_z, 16)]
        gw_zg.append([rcopy(piece, piece, base + 7 + k, zp[k]) for k in range(3)])
        piece = gwf.at[side, own_cols, pl.ds(row_y, 64)]
        gw_yg.append([rcopy(piece, piece, base + 10 + k, yp[k]) for k in range(3)])
        piece = gwf.at[side, own_cols]
        gw_cg.append(rcopy(piece, piece, base + 13, sib))
    gw_z[1].append(rcopy(s2b.at[1, :, pl.ds(pl.multiple_of(16 * zh, 16), 16)], zr.at[1, 3], GP, pair))

    def tile(i, side):
        @pl.loop(0, 2)
        def _(j):
            gws[i, j] = dot_tn(mx[side], cg[2 * oc + j]).astype(BF)
        gw_core[i].start()

        @pl.loop(0, 2)
        def _(j):
            gwo[i, j] = dot_tn(mx[side], cg[2 * core + j])

    def after_core(i):
        gw_core[i].wait_recv()
        total = gwo[i] + gwr[i].astype(F32)
        gwo[i] = total
        s1b[i] = total.astype(BF)
        for copy in gw_y[i]:
            copy.start()

    def after_y(i):
        for copy in gw_y[i]:
            copy.wait_recv()
        total = gwo[i, :, pl.ds(row_y, 64), :]
        for k in range(3):
            total += yr[i, k].astype(F32)
        gwo[i, :, pl.ds(row_y, 64), :] = total
        s2b[i] = total.astype(BF)
        for copy in gw_z[i]:
            copy.start()

    def after_z(i):
        for copy in gw_z[i]:
            copy.wait_recv()
        if i == 0:
            total = gwo[0, :, pl.ds(row_z, 16), :]
        else:
            total = zr[1, 3].astype(F32)
        for k in range(3):
            total += zr[i, k].astype(F32)
        gwf[z if i == 0 else oz, own_cols, pl.ds(row_z, 16), :] = total.astype(BF)
        for copy in gw_zg[i]:
            copy.start()

    def after_zg(i):
        for copy in gw_zg[i]:
            copy.wait_recv()
        for copy in gw_yg[i]:
            copy.start()

    def after_yg(i):
        for copy in gw_yg[i]:
            copy.wait_recv()
        gw_cg[i].start()

    def out_w(i, s):
        side = z if i == 0 else oz
        return pltpu.make_async_copy(
            gwf.at[side, s], gw_hbm.at[:, pl.ds(pl.multiple_of(512 * s + W2 * side, W2), W2)], lsem.at[18 + 4 * i + s])

    def after_cg(i):
        gw_cg[i].wait_recv()
        for s in range(4):
            out_w(i, s).start()

    tile(0, z)

    for b in range(NB):
        mx_copy(b).wait_recv()

    def partial(s, b):
        rb = rows_of(b)
        return dot_nn(mx[0, rb, :], wt[s, 0:W2, :]) + dot_nn(mx[1, rb, :], wt[s, W2:2 * W2, :])

    rs1_r = [rcopy(rs_a.at[i], rs_ar.at[i], RS1 + i, right) for i in range(2)]
    rs1_l = [rcopy(rs_a.at[2 + i], rs_ar.at[2 + i], RS1 + 2 + i, left) for i in range(2)]

    @pl.loop(0, NB)
    def _(b):
        rs_a[b] = partial(xf, b).astype(BF)

    for i in range(2):
        rs1_r[i].start()
        rs1_l[i].start()
    rs2_r = [rcopy(rs_b.at[0, b], rs_br.at[0, b], RS2 + b, right) for b in range(NB)]
    rs2_l = [rcopy(rs_b.at[1, b], rs_br.at[1, b], RS2 + 4 + b, left) for b in range(NB)]

    after_core(0)
    tile(1, oz)

    @pl.loop(0, 2)
    def _(i):
        rs_b[0, 2 + i] = partial(xr, 2 + i).astype(BF)
        rs_b[1, i] = partial(xl, i).astype(BF)

    for i in range(2):
        rs2_r[2 + i].start()
        rs2_l[i].start()
    after_core(1)

    @pl.loop(0, 2)
    def _(i):
        part_r[i] = partial(xr, i)
        part_l[i] = partial(xl, 2 + i)

    @pl.loop(0, NB)
    def _(b):
        gmo[b] += gm_part(xf, b, zrow)

    after_y(0)

    dkf[...] = jnp.zeros_like(dkf)

    @pl.loop(0, NB)
    def _(b):
        rb = rows_of(b)
        gm_copy(b).wait_recv()
        for h in range(2):
            hs = slice(h * HD, h * HD + HD)
            do = (gmo[b, :, hs] + gmr[b, :, hs].astype(F32)).astype(BF)
            qh = q[rb, hs]
            p_l = probs[b, h, :, 0:LOCAL]
            p_f = probs[b, h, :, LOCAL:]
            dp_l = dot_nt(do, kl[1, b, :, hs])
            dp_f = dot_nt(do, kf[1, :, hs])
            inner = jnp.sum(p_l * dp_l, axis=1, keepdims=True) + jnp.sum(p_f * dp_f, axis=1, keepdims=True)
            ds_l = (p_l * (dp_l - inner)).astype(BF)
            ds_f = (p_f * (dp_f - inner)).astype(BF)
            dq = dot_nn(ds_l, kl[0, b, :, hs]) + dot_nn(ds_f, kf[0, :, hs])
            ogq[rb, hs] = (dq * SCALE).astype(BF)
            dkf[0, :, hs] += dot_tn(ds_f, qh) * SCALE
            dkf[1, :, hs] += dot_tn(p_f.astype(BF), do)
            dkl[0, b, :, hs] = dot_tn(ds_l, qh) * SCALE
            dkl[1, b, :, hs] = dot_tn(p_l.astype(BF), do)

        @pl.when(b == 0)
        def _():
            after_y(1)
            for i in range(2):
                rs1_r[i].wait_recv()
                rs1_l[i].wait_recv()
                rs_b[0, i] = (part_r[i] + rs_ar[i].astype(F32)).astype(BF)
                rs_b[1, 2 + i] = (part_l[i] + rs_ar[2 + i].astype(F32)).astype(BF)
                rs2_r[i].start()
                rs2_l[2 + i].start()


        @pl.when(b == 2)
        def _():
            after_z(0)
            after_z(1)

    gs_s[:, 0:128, :] = dkf[:, 0:128, :].astype(BF)
    gs_s[:, 128:384, :] = dkf[:, 384:640, :].astype(BF)
    gk_s = rcopy(gs_s, gs_r, GS, sib)
    gk_s.start()
    out_q = pltpu.make_async_copy(ogq, gq_hbm, lsem.at[14])
    out_q.start()

    @pl.loop(0, NB)
    def _(b):
        part0[b] = partial(x, b)

    after_zg(0)

    gk_s.wait_recv()
    parts7 = []
    for t in range(2):
        total = dkf[t, 128:384, :] + gs_r[t, 128:384, :].astype(F32)
        ga_s[t] = total[0:192, :].astype(BF)
        parts7.append(total[192:256, :].reshape(8, 8, W2))
    gs7[...] = jnp.concatenate(parts7, axis=1).astype(BF)
    gk_d = [rcopy(ga_s.at[:, pl.ds(0, 64)], ga_r.at[:, pl.ds(0, 64)], GD, yp[0]),
            rcopy(ga_s.at[:, pl.ds(64, 32)], ga_r.at[:, pl.ds(64, 32)], GD + 1, yp[1]),
            rcopy(ga_s.at[:, pl.ds(96, 32)], ga_r.at[:, pl.ds(96, 32)], GD + 2, yp[2])]
    gk_d += [rcopy(ga_s.at[:, pl.ds(128 + 16 * i, 16)], ga_r.at[:, pl.ds(128 + 16 * i, 16)], GD + 3 + i, far_chips[i])
             for i in range(4)]
    gk_d += [rcopy(gs7.at[i], gr7.at[i], GD + 7 + i, far_chips[4 + i]) for i in range(8)]
    for copy in gk_d:
        copy.start()
    after_zg(1)

    for t in range(2):
        for p in range(2):
            g2 = dkl[t, 2 - 2 * p, 384:512, :] + dkl[t, 3 - 2 * p, 384:512, :]
            for i in range(2):
                b = 2 * p + i
                g1 = dkl[t, b ^ 1, 256:384, :] + spread(g2[64 * i:64 * i + 64, :], 2)
                tok[t, b] = dkl[t, b, 0:BLOCK, :] + spread(g1, 2)

    for b in range(NB):
        rs2_r[b].wait_recv()
        rs2_l[b].wait_recv()
        oatt[pl.ds(b * BLOCK, BLOCK), :] = (
            part0[b] + rs_br[0, b].astype(F32) + rs_br[1, b].astype(F32)).astype(BF)
    out_att = pltpu.make_async_copy(oatt, att_hbm, lsem.at[15])
    out_att.start()
    for copy in (ag_r + ag_l + relay_r + relay_l + wz + wc + [ks_own, ks_y, ks_z] + kd_y + kd_6 + kd_7
                 + [mx_copy(b) for b in range(NB)] + [gm_copy(b) for b in range(NB)]
                 + rs1_r + rs1_l + rs2_r + rs2_l
                 + gw_core + gw_y[0] + gw_y[1] + gw_z[0] + gw_z[1] + [gk_s]):
        copy.wait_send()
    after_yg(0)

    for copy in gk_d:
        copy.wait_recv()
    g7 = jnp.sum(gr7[...].astype(F32), axis=0)
    for t in range(2):
        g6 = ga_r[t, 128:144, :].astype(F32)
        for i in range(1, 4):
            g6 += ga_r[t, 128 + 16 * i:144 + 16 * i, :].astype(F32)
        g5 = ga_r[t, 64:96, :].astype(F32) + ga_r[t, 96:128, :].astype(F32)
        g4 = ga_r[t, 0:64, :].astype(F32)
        g3 = (gs_r[t, 0:128, :].astype(F32) + spread(g4, 2) + spread(g5, 4) + spread(g6, 8)
              + spread(g7[8 * t:8 * t + 8, :], 16))
        for b in range(NB):
            ogk[t, pl.ds(b * BLOCK, BLOCK), :] = (tok[t, b] + spread(g3[32 * b:32 * b + 32, :], 8)).astype(BF)
    out_k = pltpu.make_async_copy(ogk.at[0], gk_hbm, lsem.at[16])
    out_v = pltpu.make_async_copy(ogk.at[1], gv_hbm, lsem.at[17])
    out_k.start()
    out_v.start()

    after_cg(0)
    after_yg(1)
    after_cg(1)

    for copy in gw_zg[0] + gw_zg[1] + gw_yg[0] + gw_yg[1] + gw_cg + gk_d:
        copy.wait_send()
    for copy in [out_q, out_att, out_k, out_v] + [out_w(i, s) for i in range(2) for s in range(4)]:
        copy.wait()


SCRATCH = [
    ((ROWS, W2), BF),
    ((2, NB, LOCAL, W2), BF),
    ((2, FAR, W2), BF),
    ((2, 128, W2), BF),
    ((2, 64, W2), BF),
    ((2, 32, W2), BF),
    ((2, 16, W2), BF),
    ((16, W2), BF),
    ((8, 16, W2), BF),
    ((4, ROWS, W2), BF),
    ((4, 2 * W2, W2), BF),
    ((2, ROWS, W2), BF),
    ((NB, 2, BLOCK, LOCAL + FAR), F32),
    ((NB, BLOCK, W2), F32),
    ((NB, BLOCK, W2), F32),
    ((NB, BLOCK, W2), BF),
    ((NB, BLOCK, W2), BF),
    ((NB, BLOCK, W2), BF),
    ((NB, BLOCK, W2), BF),
    ((2, NB, BLOCK, W2), BF),
    ((2, NB, BLOCK, W2), BF),
    ((NB, BLOCK, W2), F32),
    ((2, BLOCK, W2), F32),
    ((2, BLOCK, W2), F32),
    ((2, 2, W2, W2), BF),
    ((2, 2, W2, W2), BF),
    ((2, 2, W2, W2), F32),
    ((2, 2, W2, W2), BF),
    ((2, 3, 2, 64, W2), BF),
    ((2, 2, 64, W2), BF),
    ((2, 4, 2, 16, W2), BF),
    ((2, 4, W2, W2), BF),
    ((2, NB, LOCAL, W2), F32),
    ((2, FAR, W2), F32),
    ((2, NB, BLOCK, W2), F32),
    ((2, 384, W2), BF),
    ((2, 384, W2), BF),
    ((2, 192, W2), BF),
    ((2, 192, W2), BF),
    ((8, 16, W2), BF),
    ((8, 16, W2), BF),
    ((ROWS, W2), BF),
    ((ROWS, W2), BF),
    ((2, ROWS, W2), BF),
]


RESULTS = [(ROWS, W2)] * 4 + [(W2, 2048)]


def move(*refs):
    srcs, dsts, bufs, sem_in, sem_out = refs[:5], refs[5:10], refs[10:15], refs[15], refs[16]
    ins, outs = [], []
    for src, dst, buf in zip(srcs, dsts, bufs):
        step = src.shape[0] // 2
        for i in range(2):
            piece = pl.ds(i * step, step)
            ins.append(pltpu.make_async_copy(src.at[piece], buf.at[piece], sem_in.at[len(ins)]))
            outs.append(pltpu.make_async_copy(buf.at[piece], dst.at[piece], sem_out.at[len(outs)]))
    for copy in ins:
        copy.start()
    for copy, out in zip(ins, outs):
        copy.wait()
        out.start()
    for copy in outs:
        copy.wait()


def body(queries, key_states, value_states, out_weight, cotangent):
    hbm = pl.BlockSpec(memory_space=pl.ANY)
    outs = tuple(jax.ShapeDtypeStruct(shape, BF) for shape in RESULTS)
    results = pl.pallas_call(
        kernel,
        out_shape=outs,
        in_specs=[hbm] * 5,
        out_specs=(hbm,) * 5,
        scratch_shapes=[pltpu.VMEM(shape, kind) for shape, kind in SCRATCH]
        + [pltpu.SemaphoreType.DMA((N_SEM,)), pltpu.SemaphoreType.DMA((N_SEM,)), pltpu.SemaphoreType.DMA((26,))],
        compiler_params=pltpu.CompilerParams(
            collective_id=0, has_side_effects=True, vmem_limit_bytes=60 * 1024 * 1024),
        name="attention",
    )(queries, key_states, value_states, out_weight, cotangent)
    return pl.pallas_call(
        move,
        out_shape=outs,
        in_specs=[hbm] * 5,
        out_specs=(hbm,) * 5,
        scratch_shapes=[pltpu.VMEM(shape, BF) for shape in RESULTS] + [pltpu.SemaphoreType.DMA((10,))] * 2,
        compiler_params=pltpu.CompilerParams(vmem_limit_bytes=60 * 1024 * 1024),
        name="results",
    )(*results)


def solution(mesh):
    return jax.shard_map(
        body,
        mesh=mesh,
        in_specs=(P("seq", "head"), P("seq", "head"), P("seq", "head"), P("head", None), P("seq", "head")),
        out_specs=(P("seq", "head"), P("seq", "head"), P("seq", "head"), P("seq", "head"), P("head", None)),
        check_vma=False,
    )
```

```python
import math

import jax
import jax.numpy as jnp
from jax import lax
from jax.experimental import pallas as pl
from jax.experimental.pallas import tpu as pltpu
from jax.sharding import PartitionSpec as P

BF = jnp.bfloat16
F32 = jnp.float32
HD = 128
BLOCK = 256
NB = 4
ROWS = NB * BLOCK
W2 = 256
LOCAL = 512
FAR = 640
SCALE = HD**-0.5
SCALE2 = SCALE * math.log2(math.e)

AG = 0
RELAY = 8
WZ = 12
WC = 16
KS = 20
KD = 23
MX = 38
GM = 42
RS1 = 46
RS2 = 50
GW = 58
GP = 86
GS = 87
GD = 88
N_SEM = 103


def dot_nt(a, b):
    return lax.dot_general(a, b, (((1,), (1,)), ((), ())), preferred_element_type=F32)


def dot_nn(a, b):
    return lax.dot_general(a, b, (((1,), (0,)), ((), ())), preferred_element_type=F32)


def dot_tn(a, b):
    return lax.dot_general(a, b, (((0,), (0,)), ((), ())), preferred_element_type=F32)


def pool_matrix(rows):
    r = lax.broadcasted_iota(jnp.int32, (rows // 2, rows), 0)
    c = lax.broadcasted_iota(jnp.int32, (rows // 2, rows), 1)
    return jnp.where((c == 2 * r) | (c == 2 * r + 1), 0.5, 0.0).astype(BF)


def pool(x):
    return dot_nn(pool_matrix(x.shape[0]), x).astype(BF)


def spread(x, factor):
    rows = x.shape[0]
    r = lax.broadcasted_iota(jnp.int32, (rows * factor, rows), 0)
    c = lax.broadcasted_iota(jnp.int32, (rows * factor, rows), 1)
    d = r - c * factor
    e = jnp.where((d >= 0) & (d < factor), 1.0 / factor, 0.0).astype(BF)
    high = x.astype(BF)
    low = (x - high.astype(F32)).astype(BF)
    return dot_nn(e, high) + dot_nn(e, low)


def kernel(q_hbm, k_hbm, v_hbm, w_hbm, c_hbm,
           att_hbm, gq_hbm, gk_hbm, gv_hbm, gw_hbm,
           q, kl, kf, c3, c4, c5, c6, c7, r7, cg, wt, mx, probs,
           gmo, gmt, gms, gmr, rs_a, rs_ar, rs_b, rs_br, part0, part_r, part_l,
           gws, gwr, gwo, s1b, yr, s2b, zr, gwf,
           dkl, dkf, tok, gs_s, gs_r, ga_s, ga_r, gs7, gr7,
           oatt, ogq, ogk,
           ssem, rsem, lsem):
    seq = lax.axis_index("seq")
    head = lax.axis_index("head")
    core = lax.rem(seq, 2)
    y = lax.rem(seq // 2, 4)
    zh = seq // 8
    x = head // 2
    z = lax.rem(head, 2)
    oc = 1 - core
    oz = 1 - z

    def xor4(a, k):
        if k == 0:
            return a
        if k == 1:
            return a + 1 - 2 * lax.rem(a, 2)
        if k == 2:
            return lax.rem(a + 2, 4)
        return 3 - a

    xr = lax.rem(x + 1, 4)
    xl = lax.rem(x + 3, 4)
    xf = lax.rem(x + 2, 4)
    right = (seq, xr * 2 + z)
    left = (seq, xl * 2 + z)
    pair = (seq, x * 2 + oz)
    sib = (zh * 8 + y * 2 + oc, head)

    def chip(a, k):
        return (xor4(zh, a) * 8 + xor4(y, k) * 2 + core, head)

    yp = [chip(0, k) for k in (1, 2, 3)]
    zp = [chip(a, 0) for a in (1, 2, 3)]
    zp_pair = [(xor4(zh, k) * 8 + y * 2 + core, x * 2 + oz) for k in (1, 2, 3)]
    yk = [xor4(y, k) for k in (1, 2, 3)]
    zk = [xor4(zh, k) for k in (1, 2, 3)]
    far_chips = [chip(a, k) for a in (1, 2, 3) for k in range(4)]

    def rows_of(b):
        return pl.ds(pl.multiple_of(b * BLOCK, BLOCK), BLOCK)

    def rcopy(src, dst, slot, peer):
        return pltpu.make_async_remote_copy(
            src_ref=src, dst_ref=dst, send_sem=ssem.at[slot], recv_sem=rsem.at[slot],
            device_id=peer, device_id_type=pl.DeviceIdType.MESH)

    barrier = pltpu.get_barrier_semaphore()
    peers = [right, left, pair, sib] + yp + far_chips + zp_pair
    for peer in peers:
        pl.semaphore_signal(barrier, inc=1, device_id=peer, device_id_type=pl.DeviceIdType.MESH)

    loads = []
    for b in range(NB):
        loads.append(pltpu.make_async_copy(k_hbm.at[pl.ds(b * BLOCK, BLOCK)], kl.at[0, b, pl.ds(0, BLOCK)], lsem.at[2 * b]))
        loads.append(pltpu.make_async_copy(v_hbm.at[pl.ds(b * BLOCK, BLOCK)], kl.at[1, b, pl.ds(0, BLOCK)], lsem.at[2 * b + 1]))
    for copy in loads:
        copy.start()
    load_q = pltpu.make_async_copy(q_hbm, q, lsem.at[8])
    load_q.start()
    load_c = pltpu.make_async_copy(c_hbm, cg.at[x], lsem.at[9])
    load_c.start()
    zrow = pl.multiple_of(z * W2, W2)
    ozrow = pl.multiple_of(oz * W2, W2)
    load_w = [
        pltpu.make_async_copy(
            w_hbm.at[:, pl.ds(pl.multiple_of(512 * s + W2 * z, W2), W2)], wt.at[s, pl.ds(zrow, W2)], lsem.at[10 + s])
        for s in range(4)]
    for copy in load_w:
        copy.start()

    for copy in loads:
        copy.wait()
    last = []
    for t in range(2):
        c2 = []
        for b in range(NB):
            p1 = pool(kl[t, b, 0:BLOCK, :])
            kl[t, b ^ 1, 256:384, :] = p1
            c2.append(pool(p1))
        p3 = []
        for p in range(2):
            both = jnp.concatenate([c2[2 * p], c2[2 * p + 1]], axis=0)
            kl[t, 2 - 2 * p, 384:512, :] = both
            kl[t, 3 - 2 * p, 384:512, :] = both
            p3.append(pool(both))
        p3 = jnp.concatenate(p3, axis=0)
        p4 = pool(p3)
        p5 = pool(p4)
        p6 = pool(p5)
        c3[t] = p3
        c4[t] = p4
        c5[t] = p5
        c6[t] = p6
        last.append(dot_nn(pool_matrix(16), p6))
    c7[...] = jnp.concatenate(last, axis=0).astype(BF)

    pl.semaphore_wait(barrier, len(peers))

    ks_own = rcopy(c3, kf.at[:, pl.ds(0, 128)], KS, sib)
    ks_own.start()
    kd_y = [rcopy(c4, kf.at[:, pl.ds(128, 64)], KD, yp[0]),
            rcopy(c5, kf.at[:, pl.ds(192, 32)], KD + 1, yp[1]),
            rcopy(c5, kf.at[:, pl.ds(224, 32)], KD + 2, yp[2])]
    kd_6 = [rcopy(c6, kf.at[:, pl.ds(256 + 16 * i, 16)], KD + 3 + i, far_chips[i]) for i in range(4)]
    kd_7 = [rcopy(c7, r7.at[i], KD + 7 + i, far_chips[4 + i]) for i in range(8)]
    for copy in kd_6 + kd_7 + kd_y:
        copy.start()

    ag_r = []
    ag_l = []
    for b in range(NB):
        rb = pl.ds(b * BLOCK, BLOCK)
        ag_r.append(rcopy(c_hbm.at[rb], cg.at[x, rb], AG + b, right))
        ag_l.append(rcopy(c_hbm.at[rb], cg.at[x, rb], AG + 4 + b, left))
    for b in range(NB):
        ag_r[b].start()
        ag_l[3 - b].start()
    crow = pl.multiple_of(core * 128, 128)
    wz = [
        rcopy(w_hbm.at[pl.ds(crow, 128), pl.ds(pl.multiple_of(512 * s + W2 * oz, W2), W2)],
              wt.at[s, pl.ds(pl.multiple_of(zrow + crow, 128), 128)], WZ + s, pair)
        for s in range(4)]
    for copy in wz:
        copy.start()

    load_q.wait()

    @pl.loop(0, NB)
    def _(b):
        for h in range(2):
            hs = slice(h * HD, h * HD + HD)
            probs[b, h, :, 0:LOCAL] = dot_nt(q[rows_of(b), hs], kl[0, b, :, hs])

    for copy in kd_y:
        copy.wait_recv()
    ks_y = rcopy(kf.at[:, pl.ds(128, 128)], kf.at[:, pl.ds(384, 128)], KS + 1, sib)
    ks_y.start()
    relay_r = []
    relay_l = []
    for i in range(2):
        rb = pl.ds(i * BLOCK, BLOCK)
        rc = pl.ds((i + 2) * BLOCK, BLOCK)
        relay_r.append(rcopy(cg.at[xl, rb], cg.at[xl, rb], RELAY + i, right))
        relay_l.append(rcopy(cg.at[xr, rc], cg.at[xr, rc], RELAY + 2 + i, left))
    ag_r[0].wait_recv()
    relay_r[0].start()
    ag_l[3].wait_recv()
    relay_l[1].start()
    for copy in kd_6 + kd_7:
        copy.wait_recv()
    wide = r7[...].astype(F32)
    for t in range(2):
        kf[t, 320:384, :] = wide[:, 8 * t:8 * t + 8, :].reshape(64, W2).astype(BF)
    ks_z = rcopy(kf.at[:, pl.ds(256, 128)], kf.at[:, pl.ds(512, 128)], KS + 2, sib)
    ks_z.start()
    wc = []
    for s in range(4):
        piece = wt.at[s, pl.ds(pl.multiple_of(ozrow + crow, 128), 128)]
        wc.append(rcopy(piece, piece, WC + s, sib))
    for copy in (ks_own, ks_y, ks_z):
        copy.wait_recv()

    def mx_copy(b):
        rb = rows_of(b)
        return rcopy(mx.at[z, rb], mx.at[z, rb], MX + b, pair)

    @pl.loop(0, NB)
    def _(b):
        rb = rows_of(b)
        for h in range(2):
            hs = slice(h * HD, h * HD + HD)
            qh = q[rb, hs]
            s_l = probs[b, h, :, 0:LOCAL]
            s_f = dot_nt(qh, kf[0, :, hs])
            top = jnp.maximum(jnp.max(s_l, axis=1, keepdims=True), jnp.max(s_f, axis=1, keepdims=True))
            e_l = jnp.exp2((s_l - top) * SCALE2)
            e_f = jnp.exp2((s_f - top) * SCALE2)
            total = jnp.sum(e_l, axis=1, keepdims=True) + jnp.sum(e_f, axis=1, keepdims=True)
            inv = 1.0 / total
            p_l = e_l * inv
            p_f = e_f * inv
            probs[b, h, :, 0:LOCAL] = p_l
            probs[b, h, :, LOCAL:] = p_f
            out = dot_nn(p_l.astype(BF), kl[1, b, :, hs]) + dot_nn(p_f.astype(BF), kf[1, :, hs])
            mx[z, rb, hs] = out.astype(BF)
        mx_copy(b).start()

        @pl.when(b == 0)
        def _():
            ag_r[1].wait_recv()
            relay_r[1].start()
            ag_l[2].wait_recv()
            relay_l[0].start()

        @pl.when(b == 1)
        def _():
            for s in range(4):
                wz[s].wait_recv()
                wc[s].start()

    load_c.wait()
    for copy in load_w:
        copy.wait()
    for copy in wc:
        copy.wait_recv()
    for i in range(2):
        ag_r[2 + i].wait_recv()
        ag_l[i].wait_recv()

    def gm_copy(b):
        return rcopy(gms.at[b], gmr.at[b], GM + b, pair)

    def gm_part(s, b, side):
        return dot_nt(cg[s, rows_of(b), :], wt[s, pl.ds(side, W2), :])

    @pl.loop(0, NB)
    def _(b):
        gmt[b] = gm_part(x, b, ozrow) + gm_part(xl, b, ozrow) + gm_part(xr, b, ozrow)
        gmo[b] = gm_part(x, b, zrow) + gm_part(xl, b, zrow) + gm_part(xr, b, zrow)

    for i in range(2):
        relay_r[i].wait_recv()
        relay_l[i].wait_recv()

    @pl.loop(0, NB)
    def _(b):
        gms[b] = (gmt[b] + gm_part(xf, b, ozrow)).astype(BF)

        @pl.when(b < 2)
        def _():
            gm_copy(b).start()

    row_y = pl.multiple_of(64 * y, 64)
    row_z = pl.multiple_of(64 * y + 16 * zh, 16)
    own_cols = pl.ds(2 * core, 2)
    gw_core, gw_y, gw_z, gw_zg, gw_yg, gw_cg = [], [], [], [], [], []
    for i in range(2):
        base = GW + 14 * i
        side = z if i == 0 else oz
        gw_core.append(rcopy(gws.at[i], gwr.at[i], base, sib))
        gw_y.append([rcopy(s1b.at[i, :, pl.ds(pl.multiple_of(64 * yk[k], 64), 64)], yr.at[i, k], base + 1 + k, yp[k])
                     for k in range(3)])
        to = zp if i == 0 else zp_pair
        gw_z.append([rcopy(s2b.at[i, :, pl.ds(pl.multiple_of(16 * zk[k], 16), 16)], zr.at[i, k], base + 4 + k, to[k])
                     for k in range(3)])
        piece = gwf.at[side, own_cols, pl.ds(row_z, 16)]
        gw_zg.append([rcopy(piece, piece, base + 7 + k, zp[k]) for k in range(3)])
        piece = gwf.at[side, own_cols, pl.ds(row_y, 64)]
        gw_yg.append([rcopy(piece, piece, base + 10 + k, yp[k]) for k in range(3)])
        piece = gwf.at[side, own_cols]
        gw_cg.append(rcopy(piece, piece, base + 13, sib))
    gw_z[1].append(rcopy(s2b.at[1, :, pl.ds(pl.multiple_of(16 * zh, 16), 16)], zr.at[1, 3], GP, pair))

    def tile(i, side):
        @pl.loop(0, 2)
        def _(j):
            gws[i, j] = dot_tn(mx[side], cg[2 * oc + j]).astype(BF)
        gw_core[i].start()

        @pl.loop(0, 2)
        def _(j):
            gwo[i, j] = dot_tn(mx[side], cg[2 * core + j])

    def after_core(i):
        gw_core[i].wait_recv()
        total = gwo[i] + gwr[i].astype(F32)
        gwo[i] = total
        s1b[i] = total.astype(BF)
        for copy in gw_y[i]:
            copy.start()

    def after_y(i):
        for copy in gw_y[i]:
            copy.wait_recv()
        total = gwo[i, :, pl.ds(row_y, 64), :]
        for k in range(3):
            total += yr[i, k].astype(F32)
        gwo[i, :, pl.ds(row_y, 64), :] = total
        s2b[i] = total.astype(BF)
        for copy in gw_z[i]:
            copy.start()

    def after_z(i):
        for copy in gw_z[i]:
            copy.wait_recv()
        if i == 0:
            total = gwo[0, :, pl.ds(row_z, 16), :]
        else:
            total = zr[1, 3].astype(F32)
        for k in range(3):
            total += zr[i, k].astype(F32)
        gwf[z if i == 0 else oz, own_cols, pl.ds(row_z, 16), :] = total.astype(BF)
        for copy in gw_zg[i]:
            copy.start()

    def after_zg(i):
        for copy in gw_zg[i]:
            copy.wait_recv()
        for copy in gw_yg[i]:
            copy.start()

    def after_yg(i):
        for copy in gw_yg[i]:
            copy.wait_recv()
        gw_cg[i].start()

    def out_w(i, s):
        side = z if i == 0 else oz
        return pltpu.make_async_copy(
            gwf.at[side, s], gw_hbm.at[:, pl.ds(pl.multiple_of(512 * s + W2 * side, W2), W2)], lsem.at[18 + 4 * i + s])

    def after_cg(i):
        gw_cg[i].wait_recv()
        for s in range(4):
            out_w(i, s).start()

    tile(0, z)

    for b in range(NB):
        mx_copy(b).wait_recv()

    def partial(s, b):
        rb = rows_of(b)
        return dot_nn(mx[0, rb, :], wt[s, 0:W2, :]) + dot_nn(mx[1, rb, :], wt[s, W2:2 * W2, :])

    rs1_r = [rcopy(rs_a.at[i], rs_ar.at[i], RS1 + i, right) for i in range(2)]
    rs1_l = [rcopy(rs_a.at[2 + i], rs_ar.at[2 + i], RS1 + 2 + i, left) for i in range(2)]

    @pl.loop(0, NB)
    def _(b):
        rs_a[b] = partial(xf, b).astype(BF)

    for i in range(2):
        rs1_r[i].start()
        rs1_l[i].start()
    rs2_r = [rcopy(rs_b.at[0, b], rs_br.at[0, b], RS2 + b, right) for b in range(NB)]
    rs2_l = [rcopy(rs_b.at[1, b], rs_br.at[1, b], RS2 + 4 + b, left) for b in range(NB)]

    after_core(0)
    tile(1, oz)

    @pl.loop(0, 2)
    def _(i):
        rs_b[0, 2 + i] = partial(xr, 2 + i).astype(BF)
        rs_b[1, i] = partial(xl, i).astype(BF)

    for i in range(2):
        rs2_r[2 + i].start()
        rs2_l[i].start()
    after_core(1)

    @pl.loop(0, 2)
    def _(i):
        part_r[i] = partial(xr, i)
        part_l[i] = partial(xl, 2 + i)

    @pl.loop(0, NB)
    def _(b):
        gmo[b] += gm_part(xf, b, zrow)

    after_y(0)
    gm_copy(2).start()
    gm_copy(3).start()

    dkf[...] = jnp.zeros_like(dkf)

    @pl.loop(0, NB)
    def _(b):
        rb = rows_of(b)
        gm_copy(b).wait_recv()
        for h in range(2):
            hs = slice(h * HD, h * HD + HD)
            do = (gmo[b, :, hs] + gmr[b, :, hs].astype(F32)).astype(BF)
            qh = q[rb, hs]
            p_l = probs[b, h, :, 0:LOCAL]
            p_f = probs[b, h, :, LOCAL:]
            dp_l = dot_nt(do, kl[1, b, :, hs])
            dp_f = dot_nt(do, kf[1, :, hs])
            inner = jnp.sum(p_l * dp_l, axis=1, keepdims=True) + jnp.sum(p_f * dp_f, axis=1, keepdims=True)
            ds_l = (p_l * (dp_l - inner)).astype(BF)
            ds_f = (p_f * (dp_f - inner)).astype(BF)
            dq = dot_nn(ds_l, kl[0, b, :, hs]) + dot_nn(ds_f, kf[0, :, hs])
            ogq[rb, hs] = (dq * SCALE).astype(BF)
            dkf[0, :, hs] += dot_tn(ds_f, qh) * SCALE
            dkf[1, :, hs] += dot_tn(p_f.astype(BF), do)
            dkl[0, b, :, hs] = dot_tn(ds_l, qh) * SCALE
            dkl[1, b, :, hs] = dot_tn(p_l.astype(BF), do)

        @pl.when(b == 0)
        def _():
            after_y(1)
            for i in range(2):
                rs1_r[i].wait_recv()
                rs1_l[i].wait_recv()
                rs_b[0, i] = (part_r[i] + rs_ar[i].astype(F32)).astype(BF)
                rs_b[1, 2 + i] = (part_l[i] + rs_ar[2 + i].astype(F32)).astype(BF)
                rs2_r[i].start()
                rs2_l[2 + i].start()


        @pl.when(b == 1)
        def _():
            after_z(0)

        @pl.when(b == 2)
        def _():
            after_z(1)

        @pl.when(b == 3)
        def _():
            after_zg(0)

    gs_s[:, 0:128, :] = dkf[:, 0:128, :].astype(BF)
    gs_s[:, 128:384, :] = dkf[:, 384:640, :].astype(BF)
    gk_s = rcopy(gs_s, gs_r, GS, sib)
    gk_s.start()
    out_q = pltpu.make_async_copy(ogq, gq_hbm, lsem.at[14])
    out_q.start()

    @pl.loop(0, NB)
    def _(b):
        part0[b] = partial(x, b)

    gk_s.wait_recv()
    parts7 = []
    for t in range(2):
        total = dkf[t, 128:384, :] + gs_r[t, 128:384, :].astype(F32)
        ga_s[t] = total[0:192, :].astype(BF)
        parts7.append(total[192:256, :].reshape(8, 8, W2))
    gs7[...] = jnp.concatenate(parts7, axis=1).astype(BF)
    gk_d = [rcopy(ga_s.at[:, pl.ds(0, 64)], ga_r.at[:, pl.ds(0, 64)], GD, yp[0]),
            rcopy(ga_s.at[:, pl.ds(64, 32)], ga_r.at[:, pl.ds(64, 32)], GD + 1, yp[1]),
            rcopy(ga_s.at[:, pl.ds(96, 32)], ga_r.at[:, pl.ds(96, 32)], GD + 2, yp[2])]
    gk_d += [rcopy(ga_s.at[:, pl.ds(128 + 16 * i, 16)], ga_r.at[:, pl.ds(128 + 16 * i, 16)], GD + 3 + i, far_chips[i])
             for i in range(4)]
    gk_d += [rcopy(gs7.at[i], gr7.at[i], GD + 7 + i, far_chips[4 + i]) for i in range(8)]
    for copy in gk_d:
        copy.start()
    after_zg(1)

    for t in range(2):
        for p in range(2):
            g2 = dkl[t, 2 - 2 * p, 384:512, :] + dkl[t, 3 - 2 * p, 384:512, :]
            for i in range(2):
                b = 2 * p + i
                g1 = dkl[t, b ^ 1, 256:384, :] + spread(g2[64 * i:64 * i + 64, :], 2)
                tok[t, b] = dkl[t, b, 0:BLOCK, :] + spread(g1, 2)

    for b in range(NB):
        rs2_r[b].wait_recv()
        rs2_l[b].wait_recv()
        oatt[pl.ds(b * BLOCK, BLOCK), :] = (
            part0[b] + rs_br[0, b].astype(F32) + rs_br[1, b].astype(F32)).astype(BF)
    out_att = pltpu.make_async_copy(oatt, att_hbm, lsem.at[15])
    out_att.start()
    for copy in (ag_r + ag_l + relay_r + relay_l + wz + wc + [ks_own, ks_y, ks_z] + kd_y + kd_6 + kd_7
                 + [mx_copy(b) for b in range(NB)] + [gm_copy(b) for b in range(NB)]
                 + rs1_r + rs1_l + rs2_r + rs2_l
                 + gw_core + gw_y[0] + gw_y[1] + gw_z[0] + gw_z[1] + [gk_s]):
        copy.wait_send()
    after_yg(0)

    for copy in gk_d:
        copy.wait_recv()
    g7 = jnp.sum(gr7[...].astype(F32), axis=0)
    for t in range(2):
        g6 = ga_r[t, 128:144, :].astype(F32)
        for i in range(1, 4):
            g6 += ga_r[t, 128 + 16 * i:144 + 16 * i, :].astype(F32)
        g5 = ga_r[t, 64:96, :].astype(F32) + ga_r[t, 96:128, :].astype(F32)
        g4 = ga_r[t, 0:64, :].astype(F32)
        g3 = (gs_r[t, 0:128, :].astype(F32) + spread(g4, 2) + spread(g5, 4) + spread(g6, 8)
              + spread(g7[8 * t:8 * t + 8, :], 16))
        for b in range(NB):
            ogk[t, pl.ds(b * BLOCK, BLOCK), :] = (tok[t, b] + spread(g3[32 * b:32 * b + 32, :], 8)).astype(BF)
    out_k = pltpu.make_async_copy(ogk.at[0], gk_hbm, lsem.at[16])
    out_v = pltpu.make_async_copy(ogk.at[1], gv_hbm, lsem.at[17])
    out_k.start()
    out_v.start()

    after_cg(0)
    after_yg(1)
    after_cg(1)

    for copy in gw_zg[0] + gw_zg[1] + gw_yg[0] + gw_yg[1] + gw_cg + gk_d:
        copy.wait_send()
    for copy in [out_q, out_att, out_k, out_v] + [out_w(i, s) for i in range(2) for s in range(4)]:
        copy.wait()


SCRATCH = [
    ((ROWS, W2), BF),
    ((2, NB, LOCAL, W2), BF),
    ((2, FAR, W2), BF),
    ((2, 128, W2), BF),
    ((2, 64, W2), BF),
    ((2, 32, W2), BF),
    ((2, 16, W2), BF),
    ((16, W2), BF),
    ((8, 16, W2), BF),
    ((4, ROWS, W2), BF),
    ((4, 2 * W2, W2), BF),
    ((2, ROWS, W2), BF),
    ((NB, 2, BLOCK, LOCAL + FAR), F32),
    ((NB, BLOCK, W2), F32),
    ((NB, BLOCK, W2), F32),
    ((NB, BLOCK, W2), BF),
    ((NB, BLOCK, W2), BF),
    ((NB, BLOCK, W2), BF),
    ((NB, BLOCK, W2), BF),
    ((2, NB, BLOCK, W2), BF),
    ((2, NB, BLOCK, W2), BF),
    ((NB, BLOCK, W2), F32),
    ((2, BLOCK, W2), F32),
    ((2, BLOCK, W2), F32),
    ((2, 2, W2, W2), BF),
    ((2, 2, W2, W2), BF),
    ((2, 2, W2, W2), F32),
    ((2, 2, W2, W2), BF),
    ((2, 3, 2, 64, W2), BF),
    ((2, 2, 64, W2), BF),
    ((2, 4, 2, 16, W2), BF),
    ((2, 4, W2, W2), BF),
    ((2, NB, LOCAL, W2), F32),
    ((2, FAR, W2), F32),
    ((2, NB, BLOCK, W2), F32),
    ((2, 384, W2), BF),
    ((2, 384, W2), BF),
    ((2, 192, W2), BF),
    ((2, 192, W2), BF),
    ((8, 16, W2), BF),
    ((8, 16, W2), BF),
    ((ROWS, W2), BF),
    ((ROWS, W2), BF),
    ((2, ROWS, W2), BF),
]


RESULTS = [(ROWS, W2)] * 4 + [(W2, 2048)]


def move(*refs):
    srcs, dsts, bufs, sem_in, sem_out = refs[:5], refs[5:10], refs[10:15], refs[15], refs[16]
    ins, outs = [], []
    for src, dst, buf in zip(srcs, dsts, bufs):
        step = src.shape[0] // 2
        for i in range(2):
            piece = pl.ds(i * step, step)
            ins.append(pltpu.make_async_copy(src.at[piece], buf.at[piece], sem_in.at[len(ins)]))
            outs.append(pltpu.make_async_copy(buf.at[piece], dst.at[piece], sem_out.at[len(outs)]))
    for copy in ins:
        copy.start()
    for copy, out in zip(ins, outs):
        copy.wait()
        out.start()
    for copy in outs:
        copy.wait()


def body(queries, key_states, value_states, out_weight, cotangent):
    hbm = pl.BlockSpec(memory_space=pl.ANY)
    outs = tuple(jax.ShapeDtypeStruct(shape, BF) for shape in RESULTS)
    results = pl.pallas_call(
        kernel,
        out_shape=outs,
        in_specs=[hbm] * 5,
        out_specs=(hbm,) * 5,
        scratch_shapes=[pltpu.VMEM(shape, kind) for shape, kind in SCRATCH]
        + [pltpu.SemaphoreType.DMA((N_SEM,)), pltpu.SemaphoreType.DMA((N_SEM,)), pltpu.SemaphoreType.DMA((26,))],
        compiler_params=pltpu.CompilerParams(
            collective_id=0, has_side_effects=True, vmem_limit_bytes=60 * 1024 * 1024),
        name="attention",
    )(queries, key_states, value_states, out_weight, cotangent)
    return pl.pallas_call(
        move,
        out_shape=outs,
        in_specs=[hbm] * 5,
        out_specs=(hbm,) * 5,
        scratch_shapes=[pltpu.VMEM(shape, BF) for shape in RESULTS] + [pltpu.SemaphoreType.DMA((10,))] * 2,
        compiler_params=pltpu.CompilerParams(vmem_limit_bytes=60 * 1024 * 1024),
        name="results",
    )(*results)


def solution(mesh):
    return jax.shard_map(
        body,
        mesh=mesh,
        in_specs=(P("seq", "head"), P("seq", "head"), P("seq", "head"), P("head", None), P("seq", "head")),
        out_specs=(P("seq", "head"), P("seq", "head"), P("seq", "head"), P("seq", "head"), P("head", None)),
        check_vma=False,
    )
```

```python
import math

import jax
import jax.numpy as jnp
from jax import lax
from jax.experimental import pallas as pl
from jax.experimental.pallas import tpu as pltpu
from jax.sharding import PartitionSpec as P

BF = jnp.bfloat16
F32 = jnp.float32
HD = 128
BLOCK = 256
NB = 4
ROWS = NB * BLOCK
W2 = 256
LOCAL = 512
FAR = 640
SCALE = HD**-0.5
SCALE2 = SCALE * math.log2(math.e)

AG = 0
RELAY = 8
WZ = 12
WC = 16
KS = 20
KD = 23
MX = 38
GM = 42
RS1 = 46
RS2 = 50
GW = 58
GP = 86
GS = 87
GD = 88
N_SEM = 103


def dot_nt(a, b):
    return lax.dot_general(a, b, (((1,), (1,)), ((), ())), preferred_element_type=F32)


def dot_nn(a, b):
    return lax.dot_general(a, b, (((1,), (0,)), ((), ())), preferred_element_type=F32)


def dot_tn(a, b):
    return lax.dot_general(a, b, (((0,), (0,)), ((), ())), preferred_element_type=F32)


def pool_matrix(rows):
    r = lax.broadcasted_iota(jnp.int32, (rows // 2, rows), 0)
    c = lax.broadcasted_iota(jnp.int32, (rows // 2, rows), 1)
    return jnp.where((c == 2 * r) | (c == 2 * r + 1), 0.5, 0.0).astype(BF)


def pool(x):
    return dot_nn(pool_matrix(x.shape[0]), x).astype(BF)


def spread(x, factor):
    rows = x.shape[0]
    r = lax.broadcasted_iota(jnp.int32, (rows * factor, rows), 0)
    c = lax.broadcasted_iota(jnp.int32, (rows * factor, rows), 1)
    d = r - c * factor
    e = jnp.where((d >= 0) & (d < factor), 1.0 / factor, 0.0).astype(BF)
    high = x.astype(BF)
    low = (x - high.astype(F32)).astype(BF)
    return dot_nn(e, high) + dot_nn(e, low)


def kernel(q_hbm, k_hbm, v_hbm, w_hbm, c_hbm,
           att_hbm, gq_hbm, gk_hbm, gv_hbm, gw_hbm,
           q, kl, kf, c3, c4, c5, c6, c7, r7, cg, wt, mx, probs,
           gmo, gms, gmr, rs_a, rs_ar, rs_b, rs_br, part0, part_r, part_l,
           gws, gwr, gwo, s1b, yr, s2b, zr, gwf,
           dkl, dkf, tok, gs_s, gs_r, ga_s, ga_r, gs7, gr7,
           oatt, ogq, ogk,
           ssem, rsem, lsem):
    seq = lax.axis_index("seq")
    head = lax.axis_index("head")
    core = lax.rem(seq, 2)
    y = lax.rem(seq // 2, 4)
    zh = seq // 8
    x = head // 2
    z = lax.rem(head, 2)
    oc = 1 - core
    oz = 1 - z

    def xor4(a, k):
        if k == 0:
            return a
        if k == 1:
            return a + 1 - 2 * lax.rem(a, 2)
        if k == 2:
            return lax.rem(a + 2, 4)
        return 3 - a

    xr = lax.rem(x + 1, 4)
    xl = lax.rem(x + 3, 4)
    xf = lax.rem(x + 2, 4)
    right = (seq, xr * 2 + z)
    left = (seq, xl * 2 + z)
    pair = (seq, x * 2 + oz)
    sib = (zh * 8 + y * 2 + oc, head)

    def chip(a, k):
        return (xor4(zh, a) * 8 + xor4(y, k) * 2 + core, head)

    yp = [chip(0, k) for k in (1, 2, 3)]
    zp = [chip(a, 0) for a in (1, 2, 3)]
    zp_pair = [(xor4(zh, k) * 8 + y * 2 + core, x * 2 + oz) for k in (1, 2, 3)]
    yk = [xor4(y, k) for k in (1, 2, 3)]
    zk = [xor4(zh, k) for k in (1, 2, 3)]
    far_chips = [chip(a, k) for a in (1, 2, 3) for k in range(4)]

    def rows_of(b):
        return pl.ds(pl.multiple_of(b * BLOCK, BLOCK), BLOCK)

    def rcopy(src, dst, slot, peer):
        return pltpu.make_async_remote_copy(
            src_ref=src, dst_ref=dst, send_sem=ssem.at[slot], recv_sem=rsem.at[slot],
            device_id=peer, device_id_type=pl.DeviceIdType.MESH)

    barrier = pltpu.get_barrier_semaphore()
    peers = [right, left, pair, sib] + yp + far_chips + zp_pair
    for peer in peers:
        pl.semaphore_signal(barrier, inc=1, device_id=peer, device_id_type=pl.DeviceIdType.MESH)

    loads = []
    for b in range(NB):
        loads.append(pltpu.make_async_copy(k_hbm.at[pl.ds(b * BLOCK, BLOCK)], kl.at[0, b, pl.ds(0, BLOCK)], lsem.at[2 * b]))
        loads.append(pltpu.make_async_copy(v_hbm.at[pl.ds(b * BLOCK, BLOCK)], kl.at[1, b, pl.ds(0, BLOCK)], lsem.at[2 * b + 1]))
    for copy in loads:
        copy.start()
    load_q = pltpu.make_async_copy(q_hbm, q, lsem.at[8])
    load_q.start()
    load_c = pltpu.make_async_copy(c_hbm, cg.at[x], lsem.at[9])
    load_c.start()
    zrow = pl.multiple_of(z * W2, W2)
    ozrow = pl.multiple_of(oz * W2, W2)
    load_w = [
        pltpu.make_async_copy(
            w_hbm.at[:, pl.ds(pl.multiple_of(512 * s + W2 * z, W2), W2)], wt.at[s, pl.ds(zrow, W2)], lsem.at[10 + s])
        for s in range(4)]
    for copy in load_w:
        copy.start()

    for copy in loads:
        copy.wait()
    last = []
    for t in range(2):
        c2 = []
        for b in range(NB):
            p1 = pool(kl[t, b, 0:BLOCK, :])
            kl[t, b ^ 1, 256:384, :] = p1
            c2.append(pool(p1))
        p3 = []
        for p in range(2):
            both = jnp.concatenate([c2[2 * p], c2[2 * p + 1]], axis=0)
            kl[t, 2 - 2 * p, 384:512, :] = both
            kl[t, 3 - 2 * p, 384:512, :] = both
            p3.append(pool(both))
        p3 = jnp.concatenate(p3, axis=0)
        p4 = pool(p3)
        p5 = pool(p4)
        p6 = pool(p5)
        c3[t] = p3
        c4[t] = p4
        c5[t] = p5
        c6[t] = p6
        last.append(dot_nn(pool_matrix(16), p6))
    c7[...] = jnp.concatenate(last, axis=0).astype(BF)

    pl.semaphore_wait(barrier, len(peers))

    ks_own = rcopy(c3, kf.at[:, pl.ds(0, 128)], KS, sib)
    ks_own.start()
    kd_y = [rcopy(c4, kf.at[:, pl.ds(128, 64)], KD, yp[0]),
            rcopy(c5, kf.at[:, pl.ds(192, 32)], KD + 1, yp[1]),
            rcopy(c5, kf.at[:, pl.ds(224, 32)], KD + 2, yp[2])]
    kd_6 = [rcopy(c6, kf.at[:, pl.ds(256 + 16 * i, 16)], KD + 3 + i, far_chips[i]) for i in range(4)]
    kd_7 = [rcopy(c7, r7.at[i], KD + 7 + i, far_chips[4 + i]) for i in range(8)]
    for copy in kd_6 + kd_7 + kd_y:
        copy.start()

    ag_r = []
    ag_l = []
    for b in range(NB):
        rb = pl.ds(b * BLOCK, BLOCK)
        ag_r.append(rcopy(c_hbm.at[rb], cg.at[x, rb], AG + b, right))
        ag_l.append(rcopy(c_hbm.at[rb], cg.at[x, rb], AG + 4 + b, left))
    for b in range(NB):
        ag_r[b].start()
        ag_l[3 - b].start()
    crow = pl.multiple_of(core * 128, 128)
    wz = [
        rcopy(w_hbm.at[pl.ds(crow, 128), pl.ds(pl.multiple_of(512 * s + W2 * oz, W2), W2)],
              wt.at[s, pl.ds(pl.multiple_of(zrow + crow, 128), 128)], WZ + s, pair)
        for s in range(4)]
    for copy in wz:
        copy.start()

    load_q.wait()

    @pl.loop(0, NB)
    def _(b):
        for h in range(2):
            hs = slice(h * HD, h * HD + HD)
            probs[b, h, :, 0:LOCAL] = dot_nt(q[rows_of(b), hs], kl[0, b, :, hs])

    for copy in kd_y:
        copy.wait_recv()
    ks_y = rcopy(kf.at[:, pl.ds(128, 128)], kf.at[:, pl.ds(384, 128)], KS + 1, sib)
    ks_y.start()
    relay_r = []
    relay_l = []
    for i in range(2):
        rb = pl.ds(i * BLOCK, BLOCK)
        rc = pl.ds((i + 2) * BLOCK, BLOCK)
        relay_r.append(rcopy(cg.at[xl, rb], cg.at[xl, rb], RELAY + i, right))
        relay_l.append(rcopy(cg.at[xr, rc], cg.at[xr, rc], RELAY + 2 + i, left))
    ag_r[0].wait_recv()
    relay_r[0].start()
    ag_l[3].wait_recv()
    relay_l[1].start()
    for copy in kd_6 + kd_7:
        copy.wait_recv()
    wide = r7[...].astype(F32)
    for t in range(2):
        kf[t, 320:384, :] = wide[:, 8 * t:8 * t + 8, :].reshape(64, W2).astype(BF)
    ks_z = rcopy(kf.at[:, pl.ds(256, 128)], kf.at[:, pl.ds(512, 128)], KS + 2, sib)
    ks_z.start()
    wc = []
    for s in range(4):
        piece = wt.at[s, pl.ds(pl.multiple_of(ozrow + crow, 128), 128)]
        wc.append(rcopy(piece, piece, WC + s, sib))
    for copy in (ks_own, ks_y, ks_z):
        copy.wait_recv()

    def mx_copy(b):
        rb = rows_of(b)
        return rcopy(mx.at[z, rb], mx.at[z, rb], MX + b, pair)

    @pl.loop(0, NB)
    def _(b):
        rb = rows_of(b)
        for h in range(2):
            hs = slice(h * HD, h * HD + HD)
            qh = q[rb, hs]
            s_l = probs[b, h, :, 0:LOCAL]
            s_f = dot_nt(qh, kf[0, :, hs])
            top = jnp.maximum(jnp.max(s_l, axis=1, keepdims=True), jnp.max(s_f, axis=1, keepdims=True))
            e_l = jnp.exp2((s_l - top) * SCALE2)
            e_f = jnp.exp2((s_f - top) * SCALE2)
            total = jnp.sum(e_l, axis=1, keepdims=True) + jnp.sum(e_f, axis=1, keepdims=True)
            inv = 1.0 / total
            p_l = e_l * inv
            p_f = e_f * inv
            probs[b, h, :, 0:LOCAL] = p_l
            probs[b, h, :, LOCAL:] = p_f
            out = dot_nn(p_l.astype(BF), kl[1, b, :, hs]) + dot_nn(p_f.astype(BF), kf[1, :, hs])
            mx[z, rb, hs] = out.astype(BF)
        mx_copy(b).start()

        @pl.when(b == 0)
        def _():
            ag_r[1].wait_recv()
            relay_r[1].start()
            ag_l[2].wait_recv()
            relay_l[0].start()

        @pl.when(b == 1)
        def _():
            for s in range(4):
                wz[s].wait_recv()
                wc[s].start()

    load_c.wait()
    for copy in load_w:
        copy.wait()
    for copy in wc:
        copy.wait_recv()
    for i in range(2):
        relay_r[i].wait_recv()
        relay_l[i].wait_recv()
        ag_r[2 + i].wait_recv()
        ag_l[i].wait_recv()

    def gm_copy(b):
        return rcopy(gms.at[b], gmr.at[b], GM + b, pair)

    @pl.loop(0, NB)
    def _(b):
        give = jnp.zeros((BLOCK, W2), F32)
        for s in range(4):
            give += dot_nt(cg[s, rows_of(b), :], wt[s, pl.ds(ozrow, W2), :])
        gms[b] = give.astype(BF)
        gm_copy(b).start()

    row_y = pl.multiple_of(64 * y, 64)
    row_z = pl.multiple_of(64 * y + 16 * zh, 16)
    own_cols = pl.ds(2 * core, 2)
    gw_core, gw_y, gw_z, gw_zg, gw_yg, gw_cg = [], [], [], [], [], []
    for i in range(2):
        base = GW + 14 * i
        side = z if i == 0 else oz
        gw_core.append(rcopy(gws.at[i], gwr.at[i], base, sib))
        gw_y.append([rcopy(s1b.at[i, :, pl.ds(pl.multiple_of(64 * yk[k], 64), 64)], yr.at[i, k], base + 1 + k, yp[k])
                     for k in range(3)])
        to = zp if i == 0 else zp_pair
        gw_z.append([rcopy(s2b.at[i, :, pl.ds(pl.multiple_of(16 * zk[k], 16), 16)], zr.at[i, k], base + 4 + k, to[k])
                     for k in range(3)])
        piece = gwf.at[side, own_cols, pl.ds(row_z, 16)]
        gw_zg.append([rcopy(piece, piece, base + 7 + k, zp[k]) for k in range(3)])
        piece = gwf.at[side, own_cols, pl.ds(row_y, 64)]
        gw_yg.append([rcopy(piece, piece, base + 10 + k, yp[k]) for k in range(3)])
        piece = gwf.at[side, own_cols]
        gw_cg.append(rcopy(piece, piece, base + 13, sib))
    gw_z[1].append(rcopy(s2b.at[1, :, pl.ds(pl.multiple_of(16 * zh, 16), 16)], zr.at[1, 3], GP, pair))

    def tile(i, side):
        @pl.loop(0, 2)
        def _(j):
            gws[i, j] = dot_tn(mx[side], cg[2 * oc + j]).astype(BF)
        gw_core[i].start()

        @pl.loop(0, 2)
        def _(j):
            gwo[i, j] = dot_tn(mx[side], cg[2 * core + j])

    def after_core(i):
        gw_core[i].wait_recv()
        total = gwo[i] + gwr[i].astype(F32)
        gwo[i] = total
        s1b[i] = total.astype(BF)
        for copy in gw_y[i]:
            copy.start()

    def after_y(i):
        for copy in gw_y[i]:
            copy.wait_recv()
        total = gwo[i, :, pl.ds(row_y, 64), :]
        for k in range(3):
            total += yr[i, k].astype(F32)
        gwo[i, :, pl.ds(row_y, 64), :] = total
        s2b[i] = total.astype(BF)
        for copy in gw_z[i]:
            copy.start()

    def after_z(i):
        for copy in gw_z[i]:
            copy.wait_recv()
        if i == 0:
            total = gwo[0, :, pl.ds(row_z, 16), :]
        else:
            total = zr[1, 3].astype(F32)
        for k in range(3):
            total += zr[i, k].astype(F32)
        gwf[z if i == 0 else oz, own_cols, pl.ds(row_z, 16), :] = total.astype(BF)
        for copy in gw_zg[i]:
            copy.start()

    def after_zg(i):
        for copy in gw_zg[i]:
            copy.wait_recv()
        for copy in gw_yg[i]:
            copy.start()

    def after_yg(i):
        for copy in gw_yg[i]:
            copy.wait_recv()
        gw_cg[i].start()

    def out_w(i, s):
        side = z if i == 0 else oz
        return pltpu.make_async_copy(
            gwf.at[side, s], gw_hbm.at[:, pl.ds(pl.multiple_of(512 * s + W2 * side, W2), W2)], lsem.at[18 + 4 * i + s])

    def after_cg(i):
        gw_cg[i].wait_recv()
        for s in range(4):
            out_w(i, s).start()

    tile(0, z)

    for b in range(NB):
        mx_copy(b).wait_recv()

    def partial(s, b):
        rb = rows_of(b)
        return dot_nn(mx[0, rb, :], wt[s, 0:W2, :]) + dot_nn(mx[1, rb, :], wt[s, W2:2 * W2, :])

    rs1_r = [rcopy(rs_a.at[i], rs_ar.at[i], RS1 + i, right) for i in range(2)]
    rs1_l = [rcopy(rs_a.at[2 + i], rs_ar.at[2 + i], RS1 + 2 + i, left) for i in range(2)]

    @pl.loop(0, NB)
    def _(b):
        rs_a[b] = partial(xf, b).astype(BF)

    for i in range(2):
        rs1_r[i].start()
        rs1_l[i].start()
    rs2_r = [rcopy(rs_b.at[0, b], rs_br.at[0, b], RS2 + b, right) for b in range(NB)]
    rs2_l = [rcopy(rs_b.at[1, b], rs_br.at[1, b], RS2 + 4 + b, left) for b in range(NB)]

    after_core(0)
    tile(1, oz)

    @pl.loop(0, 2)
    def _(i):
        rs_b[0, 2 + i] = partial(xr, 2 + i).astype(BF)
        rs_b[1, i] = partial(xl, i).astype(BF)

    for i in range(2):
        rs2_r[2 + i].start()
        rs2_l[i].start()
    after_core(1)

    @pl.loop(0, 2)
    def _(i):
        part_r[i] = partial(xr, i)
        part_l[i] = partial(xl, 2 + i)

    @pl.loop(0, NB)
    def _(b):
        keep = jnp.zeros((BLOCK, W2), F32)
        for s in range(4):
            keep += dot_nt(cg[s, rows_of(b), :], wt[s, pl.ds(zrow, W2), :])
        gmo[b] = keep

    after_y(0)

    dkf[...] = jnp.zeros_like(dkf)

    @pl.loop(0, NB)
    def _(b):
        rb = rows_of(b)
        gm_copy(b).wait_recv()
        for h in range(2):
            hs = slice(h * HD, h * HD + HD)
            do = (gmo[b, :, hs] + gmr[b, :, hs].astype(F32)).astype(BF)
            qh = q[rb, hs]
            p_l = probs[b, h, :, 0:LOCAL]
            p_f = probs[b, h, :, LOCAL:]
            dp_l = dot_nt(do, kl[1, b, :, hs])
            dp_f = dot_nt(do, kf[1, :, hs])
            inner = jnp.sum(p_l * dp_l, axis=1, keepdims=True) + jnp.sum(p_f * dp_f, axis=1, keepdims=True)
            ds_l = (p_l * (dp_l - inner)).astype(BF)
            ds_f = (p_f * (dp_f - inner)).astype(BF)
            dq = dot_nn(ds_l, kl[0, b, :, hs]) + dot_nn(ds_f, kf[0, :, hs])
            ogq[rb, hs] = (dq * SCALE).astype(BF)
            dkf[0, :, hs] += dot_tn(ds_f, qh) * SCALE
            dkf[1, :, hs] += dot_tn(p_f.astype(BF), do)
            dkl[0, b, :, hs] = dot_tn(ds_l, qh) * SCALE
            dkl[1, b, :, hs] = dot_tn(p_l.astype(BF), do)

        @pl.when(b == 0)
        def _():
            after_y(1)
            for i in range(2):
                rs1_r[i].wait_recv()
                rs1_l[i].wait_recv()
                rs_b[0, i] = (part_r[i] + rs_ar[i].astype(F32)).astype(BF)
                rs_b[1, 2 + i] = (part_l[i] + rs_ar[2 + i].astype(F32)).astype(BF)
                rs2_r[i].start()
                rs2_l[2 + i].start()


        @pl.when(b == 2)
        def _():
            after_z(0)

    gs_s[:, 0:128, :] = dkf[:, 0:128, :].astype(BF)
    gs_s[:, 128:384, :] = dkf[:, 384:640, :].astype(BF)
    gk_s = rcopy(gs_s, gs_r, GS, sib)
    gk_s.start()
    out_q = pltpu.make_async_copy(ogq, gq_hbm, lsem.at[14])
    out_q.start()
    after_z(1)

    @pl.loop(0, NB)
    def _(b):
        part0[b] = partial(x, b)

    after_zg(0)

    gk_s.wait_recv()
    parts7 = []
    for t in range(2):
        total = dkf[t, 128:384, :] + gs_r[t, 128:384, :].astype(F32)
        ga_s[t] = total[0:192, :].astype(BF)
        parts7.append(total[192:256, :].reshape(8, 8, W2))
    gs7[...] = jnp.concatenate(parts7, axis=1).astype(BF)
    gk_d = [rcopy(ga_s.at[:, pl.ds(0, 64)], ga_r.at[:, pl.ds(0, 64)], GD, yp[0]),
            rcopy(ga_s.at[:, pl.ds(64, 32)], ga_r.at[:, pl.ds(64, 32)], GD + 1, yp[1]),
            rcopy(ga_s.at[:, pl.ds(96, 32)], ga_r.at[:, pl.ds(96, 32)], GD + 2, yp[2])]
    gk_d += [rcopy(ga_s.at[:, pl.ds(128 + 16 * i, 16)], ga_r.at[:, pl.ds(128 + 16 * i, 16)], GD + 3 + i, far_chips[i])
             for i in range(4)]
    gk_d += [rcopy(gs7.at[i], gr7.at[i], GD + 7 + i, far_chips[4 + i]) for i in range(8)]
    for copy in gk_d:
        copy.start()

    for t in range(2):
        for p in range(2):
            g2 = dkl[t, 2 - 2 * p, 384:512, :] + dkl[t, 3 - 2 * p, 384:512, :]
            for i in range(2):
                b = 2 * p + i
                g1 = dkl[t, b ^ 1, 256:384, :] + spread(g2[64 * i:64 * i + 64, :], 2)
                tok[t, b] = dkl[t, b, 0:BLOCK, :] + spread(g1, 2)
    after_zg(1)

    for b in range(NB):
        rs2_r[b].wait_recv()
        rs2_l[b].wait_recv()
        oatt[pl.ds(b * BLOCK, BLOCK), :] = (
            part0[b] + rs_br[0, b].astype(F32) + rs_br[1, b].astype(F32)).astype(BF)
    out_att = pltpu.make_async_copy(oatt, att_hbm, lsem.at[15])
    out_att.start()
    for copy in (ag_r + ag_l + relay_r + relay_l + wz + wc + [ks_own, ks_y, ks_z] + kd_y + kd_6 + kd_7
                 + [mx_copy(b) for b in range(NB)] + [gm_copy(b) for b in range(NB)]
                 + rs1_r + rs1_l + rs2_r + rs2_l
                 + gw_core + gw_y[0] + gw_y[1] + gw_z[0] + gw_z[1] + [gk_s]):
        copy.wait_send()
    after_yg(0)

    for copy in gk_d:
        copy.wait_recv()
    g7 = jnp.sum(gr7[...].astype(F32), axis=0)
    for t in range(2):
        g6 = ga_r[t, 128:144, :].astype(F32)
        for i in range(1, 4):
            g6 += ga_r[t, 128 + 16 * i:144 + 16 * i, :].astype(F32)
        g5 = ga_r[t, 64:96, :].astype(F32) + ga_r[t, 96:128, :].astype(F32)
        g4 = ga_r[t, 0:64, :].astype(F32)
        g3 = (gs_r[t, 0:128, :].astype(F32) + spread(g4, 2) + spread(g5, 4) + spread(g6, 8)
              + spread(g7[8 * t:8 * t + 8, :], 16))
        for b in range(NB):
            ogk[t, pl.ds(b * BLOCK, BLOCK), :] = (tok[t, b] + spread(g3[32 * b:32 * b + 32, :], 8)).astype(BF)
    out_k = pltpu.make_async_copy(ogk.at[0], gk_hbm, lsem.at[16])
    out_v = pltpu.make_async_copy(ogk.at[1], gv_hbm, lsem.at[17])
    out_k.start()
    out_v.start()

    after_cg(0)
    after_yg(1)
    after_cg(1)

    for copy in gw_zg[0] + gw_zg[1] + gw_yg[0] + gw_yg[1] + gw_cg + gk_d:
        copy.wait_send()
    for copy in [out_q, out_att, out_k, out_v] + [out_w(i, s) for i in range(2) for s in range(4)]:
        copy.wait()


SCRATCH = [
    ((ROWS, W2), BF),
    ((2, NB, LOCAL, W2), BF),
    ((2, FAR, W2), BF),
    ((2, 128, W2), BF),
    ((2, 64, W2), BF),
    ((2, 32, W2), BF),
    ((2, 16, W2), BF),
    ((16, W2), BF),
    ((8, 16, W2), BF),
    ((4, ROWS, W2), BF),
    ((4, 2 * W2, W2), BF),
    ((2, ROWS, W2), BF),
    ((NB, 2, BLOCK, LOCAL + FAR), F32),
    ((NB, BLOCK, W2), F32),
    ((NB, BLOCK, W2), BF),
    ((NB, BLOCK, W2), BF),
    ((NB, BLOCK, W2), BF),
    ((NB, BLOCK, W2), BF),
    ((2, NB, BLOCK, W2), BF),
    ((2, NB, BLOCK, W2), BF),
    ((NB, BLOCK, W2), F32),
    ((2, BLOCK, W2), F32),
    ((2, BLOCK, W2), F32),
    ((2, 2, W2, W2), BF),
    ((2, 2, W2, W2), BF),
    ((2, 2, W2, W2), F32),
    ((2, 2, W2, W2), BF),
    ((2, 3, 2, 64, W2), BF),
    ((2, 2, 64, W2), BF),
    ((2, 4, 2, 16, W2), BF),
    ((2, 4, W2, W2), BF),
    ((2, NB, LOCAL, W2), F32),
    ((2, FAR, W2), F32),
    ((2, NB, BLOCK, W2), F32),
    ((2, 384, W2), BF),
    ((2, 384, W2), BF),
    ((2, 192, W2), BF),
    ((2, 192, W2), BF),
    ((8, 16, W2), BF),
    ((8, 16, W2), BF),
    ((ROWS, W2), BF),
    ((ROWS, W2), BF),
    ((2, ROWS, W2), BF),
]


RESULTS = [(ROWS, W2)] * 4 + [(W2, 2048)]


def move(*refs):
    srcs, dsts, bufs, sem_in, sem_out = refs[:5], refs[5:10], refs[10:15], refs[15], refs[16]
    ins, outs = [], []
    for src, dst, buf in zip(srcs, dsts, bufs):
        step = src.shape[0] // 2
        for i in range(2):
            piece = pl.ds(i * step, step)
            ins.append(pltpu.make_async_copy(src.at[piece], buf.at[piece], sem_in.at[len(ins)]))
            outs.append(pltpu.make_async_copy(buf.at[piece], dst.at[piece], sem_out.at[len(outs)]))
    for copy in ins:
        copy.start()
    for copy, out in zip(ins, outs):
        copy.wait()
        out.start()
    for copy in outs:
        copy.wait()


def body(queries, key_states, value_states, out_weight, cotangent):
    hbm = pl.BlockSpec(memory_space=pl.ANY)
    outs = tuple(jax.ShapeDtypeStruct(shape, BF) for shape in RESULTS)
    results = pl.pallas_call(
        kernel,
        out_shape=outs,
        in_specs=[hbm] * 5,
        out_specs=(hbm,) * 5,
        scratch_shapes=[pltpu.VMEM(shape, kind) for shape, kind in SCRATCH]
        + [pltpu.SemaphoreType.DMA((N_SEM,)), pltpu.SemaphoreType.DMA((N_SEM,)), pltpu.SemaphoreType.DMA((26,))],
        compiler_params=pltpu.CompilerParams(
            collective_id=0, has_side_effects=True, vmem_limit_bytes=60 * 1024 * 1024),
        name="attention",
    )(queries, key_states, value_states, out_weight, cotangent)
    return pl.pallas_call(
        move,
        out_shape=outs,
        in_specs=[hbm] * 5,
        out_specs=(hbm,) * 5,
        scratch_shapes=[pltpu.VMEM(shape, BF) for shape in RESULTS] + [pltpu.SemaphoreType.DMA((10,))] * 2,
        compiler_params=pltpu.CompilerParams(vmem_limit_bytes=60 * 1024 * 1024),
        name="results",
    )(*results)


def solution(mesh):
    return jax.shard_map(
        body,
        mesh=mesh,
        in_specs=(P("seq", "head"), P("seq", "head"), P("seq", "head"), P("head", None), P("seq", "head")),
        out_specs=(P("seq", "head"), P("seq", "head"), P("seq", "head"), P("seq", "head"), P("head", None)),
        check_vma=False,
    )
```

```python
import math

import jax
import jax.numpy as jnp
from jax import lax
from jax.experimental import pallas as pl
from jax.experimental.pallas import tpu as pltpu
from jax.sharding import PartitionSpec as P

BF = jnp.bfloat16
F32 = jnp.float32
HD = 128
BLOCK = 256
NB = 4
ROWS = NB * BLOCK
W2 = 256
LOCAL = 512
FAR = 640
SCALE = HD**-0.5
SCALE2 = SCALE * math.log2(math.e)

AG = 0
RELAY = 8
WZ = 12
WC = 16
KS = 20
KD = 23
MX = 38
GM = 42
RS1 = 46
RS2 = 50
GW = 58
GP = 86
GS = 87
GD = 88
N_SEM = 103


def dot_nt(a, b):
    return lax.dot_general(a, b, (((1,), (1,)), ((), ())), preferred_element_type=F32)


def dot_nn(a, b):
    return lax.dot_general(a, b, (((1,), (0,)), ((), ())), preferred_element_type=F32)


def dot_tn(a, b):
    return lax.dot_general(a, b, (((0,), (0,)), ((), ())), preferred_element_type=F32)


def pool_matrix(rows):
    r = lax.broadcasted_iota(jnp.int32, (rows // 2, rows), 0)
    c = lax.broadcasted_iota(jnp.int32, (rows // 2, rows), 1)
    return jnp.where((c == 2 * r) | (c == 2 * r + 1), 0.5, 0.0).astype(BF)


def pool(x):
    return dot_nn(pool_matrix(x.shape[0]), x).astype(BF)


def spread(x, factor):
    rows = x.shape[0]
    r = lax.broadcasted_iota(jnp.int32, (rows * factor, rows), 0)
    c = lax.broadcasted_iota(jnp.int32, (rows * factor, rows), 1)
    d = r - c * factor
    e = jnp.where((d >= 0) & (d < factor), 1.0 / factor, 0.0).astype(BF)
    high = x.astype(BF)
    low = (x - high.astype(F32)).astype(BF)
    return dot_nn(e, high) + dot_nn(e, low)


def kernel(q_hbm, k_hbm, v_hbm, w_hbm, c_hbm,
           att_hbm, gq_hbm, gk_hbm, gv_hbm, gw_hbm,
           q, kl, kf, c3, c4, c5, c6, c7, r7, cg, wt, mx, probs,
           gmo, gms, gmr, rs_a, rs_ar, rs_b, rs_br, part0, part_r, part_l,
           gws, gwr, gwo, s1b, yr, s2b, zr, gwf,
           dkl, dkf, tok, gs_s, gs_r, ga_s, ga_r, gs7, gr7,
           oatt, ogq, ogk,
           ssem, rsem, lsem):
    seq = lax.axis_index("seq")
    head = lax.axis_index("head")
    core = lax.rem(seq, 2)
    y = lax.rem(seq // 2, 4)
    zh = seq // 8
    x = head // 2
    z = lax.rem(head, 2)
    oc = 1 - core
    oz = 1 - z

    def xor4(a, k):
        if k == 0:
            return a
        if k == 1:
            return a + 1 - 2 * lax.rem(a, 2)
        if k == 2:
            return lax.rem(a + 2, 4)
        return 3 - a

    xr = lax.rem(x + 1, 4)
    xl = lax.rem(x + 3, 4)
    xf = lax.rem(x + 2, 4)
    right = (seq, xr * 2 + z)
    left = (seq, xl * 2 + z)
    pair = (seq, x * 2 + oz)
    sib = (zh * 8 + y * 2 + oc, head)

    def chip(a, k):
        return (xor4(zh, a) * 8 + xor4(y, k) * 2 + core, head)

    yp = [chip(0, k) for k in (1, 2, 3)]
    zp = [chip(a, 0) for a in (1, 2, 3)]
    zp_pair = [(xor4(zh, k) * 8 + y * 2 + core, x * 2 + oz) for k in (1, 2, 3)]
    yk = [xor4(y, k) for k in (1, 2, 3)]
    zk = [xor4(zh, k) for k in (1, 2, 3)]
    far_chips = [chip(a, k) for a in (1, 2, 3) for k in range(4)]

    def rows_of(b):
        return pl.ds(pl.multiple_of(b * BLOCK, BLOCK), BLOCK)

    def rcopy(src, dst, slot, peer):
        return pltpu.make_async_remote_copy(
            src_ref=src, dst_ref=dst, send_sem=ssem.at[slot], recv_sem=rsem.at[slot],
            device_id=peer, device_id_type=pl.DeviceIdType.MESH)

    barrier = pltpu.get_barrier_semaphore()
    peers = [right, left, pair, sib] + yp + far_chips + zp_pair
    for peer in peers:
        pl.semaphore_signal(barrier, inc=1, device_id=peer, device_id_type=pl.DeviceIdType.MESH)

    loads = []
    for b in range(NB):
        loads.append(pltpu.make_async_copy(k_hbm.at[pl.ds(b * BLOCK, BLOCK)], kl.at[0, b, pl.ds(0, BLOCK)], lsem.at[2 * b]))
        loads.append(pltpu.make_async_copy(v_hbm.at[pl.ds(b * BLOCK, BLOCK)], kl.at[1, b, pl.ds(0, BLOCK)], lsem.at[2 * b + 1]))
    for copy in loads:
        copy.start()
    load_q = pltpu.make_async_copy(q_hbm, q, lsem.at[8])
    load_q.start()
    load_c = pltpu.make_async_copy(c_hbm, cg.at[x], lsem.at[9])
    load_c.start()
    zrow = pl.multiple_of(z * W2, W2)
    ozrow = pl.multiple_of(oz * W2, W2)
    load_w = [
        pltpu.make_async_copy(
            w_hbm.at[:, pl.ds(pl.multiple_of(512 * s + W2 * z, W2), W2)], wt.at[s, pl.ds(zrow, W2)], lsem.at[10 + s])
        for s in range(4)]
    for copy in load_w:
        copy.start()

    for copy in loads:
        copy.wait()
    last = []
    for t in range(2):
        c2 = []
        for b in range(NB):
            p1 = pool(kl[t, b, 0:BLOCK, :])
            kl[t, b ^ 1, 256:384, :] = p1
            c2.append(pool(p1))
        p3 = []
        for p in range(2):
            both = jnp.concatenate([c2[2 * p], c2[2 * p + 1]], axis=0)
            kl[t, 2 - 2 * p, 384:512, :] = both
            kl[t, 3 - 2 * p, 384:512, :] = both
            p3.append(pool(both))
        p3 = jnp.concatenate(p3, axis=0)
        p4 = pool(p3)
        p5 = pool(p4)
        p6 = pool(p5)
        c3[t] = p3
        c4[t] = p4
        c5[t] = p5
        c6[t] = p6
        last.append(dot_nn(pool_matrix(16), p6))
    c7[...] = jnp.concatenate(last, axis=0).astype(BF)

    pl.semaphore_wait(barrier, len(peers))

    ks_own = rcopy(c3, kf.at[:, pl.ds(0, 128)], KS, sib)
    ks_own.start()
    kd_y = [rcopy(c4, kf.at[:, pl.ds(128, 64)], KD, yp[0]),
            rcopy(c5, kf.at[:, pl.ds(192, 32)], KD + 1, yp[1]),
            rcopy(c5, kf.at[:, pl.ds(224, 32)], KD + 2, yp[2])]
    kd_6 = [rcopy(c6, kf.at[:, pl.ds(256 + 16 * i, 16)], KD + 3 + i, far_chips[i]) for i in range(4)]
    kd_7 = [rcopy(c7, r7.at[i], KD + 7 + i, far_chips[4 + i]) for i in range(8)]
    for copy in kd_y + kd_6 + kd_7:
        copy.start()

    ag_r = []
    ag_l = []
    for b in range(NB):
        rb = pl.ds(b * BLOCK, BLOCK)
        ag_r.append(rcopy(c_hbm.at[rb], cg.at[x, rb], AG + b, right))
        ag_l.append(rcopy(c_hbm.at[rb], cg.at[x, rb], AG + 4 + b, left))
    for b in range(NB):
        ag_r[b].start()
        ag_l[3 - b].start()
    crow = pl.multiple_of(core * 128, 128)
    wz = [
        rcopy(w_hbm.at[pl.ds(crow, 128), pl.ds(pl.multiple_of(512 * s + W2 * oz, W2), W2)],
              wt.at[s, pl.ds(pl.multiple_of(zrow + crow, 128), 128)], WZ + s, pair)
        for s in range(4)]
    for copy in wz:
        copy.start()

    load_q.wait()

    @pl.loop(0, NB)
    def _(b):
        for h in range(2):
            hs = slice(h * HD, h * HD + HD)
            probs[b, h, :, 0:LOCAL] = dot_nt(q[rows_of(b), hs], kl[0, b, :, hs])

    for copy in kd_y:
        copy.wait_recv()
    ks_y = rcopy(kf.at[:, pl.ds(128, 128)], kf.at[:, pl.ds(384, 128)], KS + 1, sib)
    ks_y.start()
    relay_r = []
    relay_l = []
    for i in range(2):
        rb = pl.ds(i * BLOCK, BLOCK)
        rc = pl.ds((i + 2) * BLOCK, BLOCK)
        relay_r.append(rcopy(cg.at[xl, rb], cg.at[xl, rb], RELAY + i, right))
        relay_l.append(rcopy(cg.at[xr, rc], cg.at[xr, rc], RELAY + 2 + i, left))
    ag_r[0].wait_recv()
    relay_r[0].start()
    ag_l[3].wait_recv()
    relay_l[1].start()
    for copy in kd_6 + kd_7:
        copy.wait_recv()
    wide = r7[...].astype(F32)
    for t in range(2):
        kf[t, 320:384, :] = wide[:, 8 * t:8 * t + 8, :].reshape(64, W2).astype(BF)
    ks_z = rcopy(kf.at[:, pl.ds(256, 128)], kf.at[:, pl.ds(512, 128)], KS + 2, sib)
    ks_z.start()
    wc = []
    for s in range(4):
        piece = wt.at[s, pl.ds(pl.multiple_of(ozrow + crow, 128), 128)]
        wc.append(rcopy(piece, piece, WC + s, sib))
    for copy in (ks_own, ks_y, ks_z):
        copy.wait_recv()

    def mx_copy(b):
        rb = rows_of(b)
        return rcopy(mx.at[z, rb], mx.at[z, rb], MX + b, pair)

    @pl.loop(0, NB)
    def _(b):
        rb = rows_of(b)
        for h in range(2):
            hs = slice(h * HD, h * HD + HD)
            qh = q[rb, hs]
            s_l = probs[b, h, :, 0:LOCAL]
            s_f = dot_nt(qh, kf[0, :, hs])
            top = jnp.maximum(jnp.max(s_l, axis=1, keepdims=True), jnp.max(s_f, axis=1, keepdims=True))
            e_l = jnp.exp2((s_l - top) * SCALE2)
            e_f = jnp.exp2((s_f - top) * SCALE2)
            total = jnp.sum(e_l, axis=1, keepdims=True) + jnp.sum(e_f, axis=1, keepdims=True)
            inv = 1.0 / total
            p_l = e_l * inv
            p_f = e_f * inv
            probs[b, h, :, 0:LOCAL] = p_l
            probs[b, h, :, LOCAL:] = p_f
            out = dot_nn(p_l.astype(BF), kl[1, b, :, hs]) + dot_nn(p_f.astype(BF), kf[1, :, hs])
            mx[z, rb, hs] = out.astype(BF)
        mx_copy(b).start()

        @pl.when(b == 0)
        def _():
            ag_r[1].wait_recv()
            relay_r[1].start()
            ag_l[2].wait_recv()
            relay_l[0].start()

        @pl.when(b == 1)
        def _():
            for s in range(4):
                wz[s].wait_recv()
                wc[s].start()

    load_c.wait()
    for copy in load_w:
        copy.wait()
    for copy in wc:
        copy.wait_recv()
    for i in range(2):
        relay_r[i].wait_recv()
        relay_l[i].wait_recv()
        ag_r[2 + i].wait_recv()
        ag_l[i].wait_recv()

    def gm_copy(b):
        return rcopy(gms.at[b], gmr.at[b], GM + b, pair)

    @pl.loop(0, NB)
    def _(b):
        give = jnp.zeros((BLOCK, W2), F32)
        for s in range(4):
            give += dot_nt(cg[s, rows_of(b), :], wt[s, pl.ds(ozrow, W2), :])
        gms[b] = give.astype(BF)
        gm_copy(b).start()

    row_y = pl.multiple_of(64 * y, 64)
    row_z = pl.multiple_of(64 * y + 16 * zh, 16)
    own_cols = pl.ds(2 * core, 2)
    gw_core, gw_y, gw_z, gw_zg, gw_yg, gw_cg = [], [], [], [], [], []
    for i in range(2):
        base = GW + 14 * i
        side = z if i == 0 else oz
        gw_core.append(rcopy(gws.at[i], gwr.at[i], base, sib))
        gw_y.append([rcopy(s1b.at[i, :, pl.ds(pl.multiple_of(64 * yk[k], 64), 64)], yr.at[i, k], base + 1 + k, yp[k])
                     for k in range(3)])
        to = zp if i == 0 else zp_pair
        gw_z.append([rcopy(s2b.at[i, :, pl.ds(pl.multiple_of(16 * zk[k], 16), 16)], zr.at[i, k], base + 4 + k, to[k])
                     for k in range(3)])
        piece = gwf.at[side, own_cols, pl.ds(row_z, 16)]
        gw_zg.append([rcopy(piece, piece, base + 7 + k, zp[k]) for k in range(3)])
        piece = gwf.at[side, own_cols, pl.ds(row_y, 64)]
        gw_yg.append([rcopy(piece, piece, base + 10 + k, yp[k]) for k in range(3)])
        piece = gwf.at[side, own_cols]
        gw_cg.append(rcopy(piece, piece, base + 13, sib))
    gw_z[1].append(rcopy(s2b.at[1, :, pl.ds(pl.multiple_of(16 * zh, 16), 16)], zr.at[1, 3], GP, pair))

    def tile(i, side):
        @pl.loop(0, 2)
        def _(j):
            gws[i, j] = dot_tn(mx[side], cg[2 * oc + j]).astype(BF)
        gw_core[i].start()

        @pl.loop(0, 2)
        def _(j):
            gwo[i, j] = dot_tn(mx[side], cg[2 * core + j])

    def after_core(i):
        gw_core[i].wait_recv()
        total = gwo[i] + gwr[i].astype(F32)
        gwo[i] = total
        s1b[i] = total.astype(BF)
        for copy in gw_y[i]:
            copy.start()

    def after_y(i):
        for copy in gw_y[i]:
            copy.wait_recv()
        total = gwo[i, :, pl.ds(row_y, 64), :]
        for k in range(3):
            total += yr[i, k].astype(F32)
        gwo[i, :, pl.ds(row_y, 64), :] = total
        s2b[i] = total.astype(BF)
        for copy in gw_z[i]:
            copy.start()

    def after_z(i):
        for copy in gw_z[i]:
            copy.wait_recv()
        if i == 0:
            total = gwo[0, :, pl.ds(row_z, 16), :]
        else:
            total = zr[1, 3].astype(F32)
        for k in range(3):
            total += zr[i, k].astype(F32)
        gwf[z if i == 0 else oz, own_cols, pl.ds(row_z, 16), :] = total.astype(BF)
        for copy in gw_zg[i]:
            copy.start()

    def after_zg(i):
        for copy in gw_zg[i]:
            copy.wait_recv()
        for copy in gw_yg[i]:
            copy.start()

    def after_yg(i):
        for copy in gw_yg[i]:
            copy.wait_recv()
        gw_cg[i].start()

    def out_w(i, s):
        side = z if i == 0 else oz
        return pltpu.make_async_copy(
            gwf.at[side, s], gw_hbm.at[:, pl.ds(pl.multiple_of(512 * s + W2 * side, W2), W2)], lsem.at[18 + 4 * i + s])

    def after_cg(i):
        gw_cg[i].wait_recv()
        for s in range(4):
            out_w(i, s).start()

    tile(0, z)

    for b in range(NB):
        mx_copy(b).wait_recv()

    def partial(s, b):
        rb = rows_of(b)
        return dot_nn(mx[0, rb, :], wt[s, 0:W2, :]) + dot_nn(mx[1, rb, :], wt[s, W2:2 * W2, :])

    rs1_r = [rcopy(rs_a.at[i], rs_ar.at[i], RS1 + i, right) for i in range(2)]
    rs1_l = [rcopy(rs_a.at[2 + i], rs_ar.at[2 + i], RS1 + 2 + i, left) for i in range(2)]

    @pl.loop(0, NB)
    def _(b):
        rs_a[b] = partial(xf, b).astype(BF)

    for i in range(2):
        rs1_r[i].start()
        rs1_l[i].start()
    rs2_r = [rcopy(rs_b.at[0, b], rs_br.at[0, b], RS2 + b, right) for b in range(NB)]
    rs2_l = [rcopy(rs_b.at[1, b], rs_br.at[1, b], RS2 + 4 + b, left) for b in range(NB)]

    after_core(0)
    tile(1, oz)

    @pl.loop(0, 2)
    def _(i):
        rs_b[0, 2 + i] = partial(xr, 2 + i).astype(BF)
        rs_b[1, i] = partial(xl, i).astype(BF)

    for i in range(2):
        rs2_r[2 + i].start()
        rs2_l[i].start()
    after_core(1)

    @pl.loop(0, 2)
    def _(i):
        part_r[i] = partial(xr, i)
        part_l[i] = partial(xl, 2 + i)

    @pl.loop(0, NB)
    def _(b):
        keep = jnp.zeros((BLOCK, W2), F32)
        for s in range(4):
            keep += dot_nt(cg[s, rows_of(b), :], wt[s, pl.ds(zrow, W2), :])
        gmo[b] = keep

    after_y(0)

    dkf[...] = jnp.zeros_like(dkf)

    @pl.loop(0, NB)
    def _(b):
        rb = rows_of(b)
        gm_copy(b).wait_recv()
        for h in range(2):
            hs = slice(h * HD, h * HD + HD)
            do = (gmo[b, :, hs] + gmr[b, :, hs].astype(F32)).astype(BF)
            qh = q[rb, hs]
            p_l = probs[b, h, :, 0:LOCAL]
            p_f = probs[b, h, :, LOCAL:]
            dp_l = dot_nt(do, kl[1, b, :, hs])
            dp_f = dot_nt(do, kf[1, :, hs])
            inner = jnp.sum(p_l * dp_l, axis=1, keepdims=True) + jnp.sum(p_f * dp_f, axis=1, keepdims=True)
            ds_l = (p_l * (dp_l - inner)).astype(BF)
            ds_f = (p_f * (dp_f - inner)).astype(BF)
            dq = dot_nn(ds_l, kl[0, b, :, hs]) + dot_nn(ds_f, kf[0, :, hs])
            ogq[rb, hs] = (dq * SCALE).astype(BF)
            dkf[0, :, hs] += dot_tn(ds_f, qh) * SCALE
            dkf[1, :, hs] += dot_tn(p_f.astype(BF), do)
            dkl[0, b, :, hs] = dot_tn(ds_l, qh) * SCALE
            dkl[1, b, :, hs] = dot_tn(p_l.astype(BF), do)

        @pl.when(b == 0)
        def _():
            after_y(1)
            for i in range(2):
                rs1_r[i].wait_recv()
                rs1_l[i].wait_recv()
                rs_b[0, i] = (part_r[i] + rs_ar[i].astype(F32)).astype(BF)
                rs_b[1, 2 + i] = (part_l[i] + rs_ar[2 + i].astype(F32)).astype(BF)
                rs2_r[i].start()
                rs2_l[2 + i].start()


        @pl.when(b == 2)
        def _():
            after_z(0)

    gs_s[:, 0:128, :] = dkf[:, 0:128, :].astype(BF)
    gs_s[:, 128:384, :] = dkf[:, 384:640, :].astype(BF)
    gk_s = rcopy(gs_s, gs_r, GS, sib)
    gk_s.start()
    out_q = pltpu.make_async_copy(ogq, gq_hbm, lsem.at[14])
    out_q.start()
    after_z(1)

    @pl.loop(0, NB)
    def _(b):
        part0[b] = partial(x, b)

    after_zg(0)

    gk_s.wait_recv()
    parts7 = []
    for t in range(2):
        total = dkf[t, 128:384, :] + gs_r[t, 128:384, :].astype(F32)
        ga_s[t] = total[0:192, :].astype(BF)
        parts7.append(total[192:256, :].reshape(8, 8, W2))
    gs7[...] = jnp.concatenate(parts7, axis=1).astype(BF)
    gk_d = [rcopy(ga_s.at[:, pl.ds(0, 64)], ga_r.at[:, pl.ds(0, 64)], GD, yp[0]),
            rcopy(ga_s.at[:, pl.ds(64, 32)], ga_r.at[:, pl.ds(64, 32)], GD + 1, yp[1]),
            rcopy(ga_s.at[:, pl.ds(96, 32)], ga_r.at[:, pl.ds(96, 32)], GD + 2, yp[2])]
    gk_d += [rcopy(ga_s.at[:, pl.ds(128 + 16 * i, 16)], ga_r.at[:, pl.ds(128 + 16 * i, 16)], GD + 3 + i, far_chips[i])
             for i in range(4)]
    gk_d += [rcopy(gs7.at[i], gr7.at[i], GD + 7 + i, far_chips[4 + i]) for i in range(8)]
    for copy in gk_d:
        copy.start()

    for t in range(2):
        for p in range(2):
            g2 = dkl[t, 2 - 2 * p, 384:512, :] + dkl[t, 3 - 2 * p, 384:512, :]
            for i in range(2):
                b = 2 * p + i
                g1 = dkl[t, b ^ 1, 256:384, :] + spread(g2[64 * i:64 * i + 64, :], 2)
                tok[t, b] = dkl[t, b, 0:BLOCK, :] + spread(g1, 2)
    after_zg(1)

    for b in range(NB):
        rs2_r[b].wait_recv()
        rs2_l[b].wait_recv()
        oatt[pl.ds(b * BLOCK, BLOCK), :] = (
            part0[b] + rs_br[0, b].astype(F32) + rs_br[1, b].astype(F32)).astype(BF)
    out_att = pltpu.make_async_copy(oatt, att_hbm, lsem.at[15])
    out_att.start()
    after_yg(0)

    for copy in gk_d:
        copy.wait_recv()
    g7 = jnp.sum(gr7[...].astype(F32), axis=0)
    for t in range(2):
        g6 = spread(g7[8 * t:8 * t + 8, :], 2)
        for i in range(4):
            g6 += ga_r[t, 128 + 16 * i:144 + 16 * i, :].astype(F32)
        g5 = ga_r[t, 64:96, :].astype(F32) + ga_r[t, 96:128, :].astype(F32) + spread(g6, 2)
        g4 = ga_r[t, 0:64, :].astype(F32) + spread(g5, 2)
        g3 = gs_r[t, 0:128, :].astype(F32) + spread(g4, 2)
        for b in range(NB):
            ogk[t, pl.ds(b * BLOCK, BLOCK), :] = (tok[t, b] + spread(g3[32 * b:32 * b + 32, :], 8)).astype(BF)
    out_k = pltpu.make_async_copy(ogk.at[0], gk_hbm, lsem.at[16])
    out_v = pltpu.make_async_copy(ogk.at[1], gv_hbm, lsem.at[17])
    out_k.start()
    out_v.start()

    after_cg(0)
    after_yg(1)
    after_cg(1)

    for copy in (ag_r + ag_l + relay_r + relay_l + wz + wc + [ks_own, ks_y, ks_z] + kd_y + kd_6 + kd_7
                 + [mx_copy(b) for b in range(NB)] + [gm_copy(b) for b in range(NB)]
                 + rs1_r + rs1_l + rs2_r + rs2_l
                 + gw_core + gw_y[0] + gw_y[1] + gw_z[0] + gw_z[1]
                 + gw_zg[0] + gw_zg[1] + gw_yg[0] + gw_yg[1] + gw_cg + [gk_s] + gk_d):
        copy.wait_send()
    for copy in [out_q, out_att, out_k, out_v] + [out_w(i, s) for i in range(2) for s in range(4)]:
        copy.wait()


SCRATCH = [
    ((ROWS, W2), BF),
    ((2, NB, LOCAL, W2), BF),
    ((2, FAR, W2), BF),
    ((2, 128, W2), BF),
    ((2, 64, W2), BF),
    ((2, 32, W2), BF),
    ((2, 16, W2), BF),
    ((16, W2), BF),
    ((8, 16, W2), BF),
    ((4, ROWS, W2), BF),
    ((4, 2 * W2, W2), BF),
    ((2, ROWS, W2), BF),
    ((NB, 2, BLOCK, LOCAL + FAR), F32),
    ((NB, BLOCK, W2), F32),
    ((NB, BLOCK, W2), BF),
    ((NB, BLOCK, W2), BF),
    ((NB, BLOCK, W2), BF),
    ((NB, BLOCK, W2), BF),
    ((2, NB, BLOCK, W2), BF),
    ((2, NB, BLOCK, W2), BF),
    ((NB, BLOCK, W2), F32),
    ((2, BLOCK, W2), F32),
    ((2, BLOCK, W2), F32),
    ((2, 2, W2, W2), BF),
    ((2, 2, W2, W2), BF),
    ((2, 2, W2, W2), F32),
    ((2, 2, W2, W2), BF),
    ((2, 3, 2, 64, W2), BF),
    ((2, 2, 64, W2), BF),
    ((2, 4, 2, 16, W2), BF),
    ((2, 4, W2, W2), BF),
    ((2, NB, LOCAL, W2), F32),
    ((2, FAR, W2), F32),
    ((2, NB, BLOCK, W2), F32),
    ((2, 384, W2), BF),
    ((2, 384, W2), BF),
    ((2, 192, W2), BF),
    ((2, 192, W2), BF),
    ((8, 16, W2), BF),
    ((8, 16, W2), BF),
    ((ROWS, W2), BF),
    ((ROWS, W2), BF),
    ((2, ROWS, W2), BF),
]


RESULTS = [(ROWS, W2)] * 4 + [(W2, 2048)]


def move(*refs):
    srcs, dsts, bufs, sem_in, sem_out = refs[:5], refs[5:10], refs[10:15], refs[15], refs[16]
    ins, outs = [], []
    for src, dst, buf in zip(srcs, dsts, bufs):
        step = src.shape[0] // 2
        for i in range(2):
            piece = pl.ds(i * step, step)
            ins.append(pltpu.make_async_copy(src.at[piece], buf.at[piece], sem_in.at[len(ins)]))
            outs.append(pltpu.make_async_copy(buf.at[piece], dst.at[piece], sem_out.at[len(outs)]))
    for copy in ins:
        copy.start()
    for copy, out in zip(ins, outs):
        copy.wait()
        out.start()
    for copy in outs:
        copy.wait()


def body(queries, key_states, value_states, out_weight, cotangent):
    hbm = pl.BlockSpec(memory_space=pl.ANY)
    outs = tuple(jax.ShapeDtypeStruct(shape, BF) for shape in RESULTS)
    results = pl.pallas_call(
        kernel,
        out_shape=outs,
        in_specs=[hbm] * 5,
        out_specs=(hbm,) * 5,
        scratch_shapes=[pltpu.VMEM(shape, kind) for shape, kind in SCRATCH]
        + [pltpu.SemaphoreType.DMA((N_SEM,)), pltpu.SemaphoreType.DMA((N_SEM,)), pltpu.SemaphoreType.DMA((26,))],
        compiler_params=pltpu.CompilerParams(
            collective_id=0, has_side_effects=True, vmem_limit_bytes=60 * 1024 * 1024),
        name="attention",
    )(queries, key_states, value_states, out_weight, cotangent)
    return pl.pallas_call(
        move,
        out_shape=outs,
        in_specs=[hbm] * 5,
        out_specs=(hbm,) * 5,
        scratch_shapes=[pltpu.VMEM(shape, BF) for shape in RESULTS] + [pltpu.SemaphoreType.DMA((10,))] * 2,
        compiler_params=pltpu.CompilerParams(vmem_limit_bytes=60 * 1024 * 1024),
        name="results",
    )(*results)


def solution(mesh):
    return jax.shard_map(
        body,
        mesh=mesh,
        in_specs=(P("seq", "head"), P("seq", "head"), P("seq", "head"), P("head", None), P("seq", "head")),
        out_specs=(P("seq", "head"), P("seq", "head"), P("seq", "head"), P("seq", "head"), P("head", None)),
        check_vma=False,
    )
```
